128 devices in a mesh: ex: 32 (over y, x, core), feat: 4 (over z).
Axes of the slice: x: 4, y: 4, z: 4, core: 2. Of those that a mesh axis runs over, the one named last changes fastest.
Arguments:
- features: bfloat16 [65536, 2048], P('ex', 'feat'), may hold values from -0.125 to 0.125
- weights: float32 [2048], P('feat'), may hold values from -6 to 6
- labels: int32 [65536], P('ex'), may hold values 0 or 1
- signs: int32 [65536], P('ex'), may hold values from -1 to 1, as said below
- samples: int32 [2048], replicated, may hold values from 0 to 65535
- radius: float32 [1], replicated, may hold values from 0.1 to 0.25
Outputs:
- new_weights: float32 [2048], P('feat')
The draws below stay inside these ranges and needn't reach their ends.
Inputs may be any that keep to these rules, and one draw needn't show every extreme that they name: `signs`: each entry is -1 or +1.
All inputs are finite; a program needn't handle non-finite values. No bound on the sum of `labels` on one device may be relied on, other than what follows from the above.
Results may differ from the reference program's by a relative error of at most 0.00067.
Values may be sent and summed in bfloat16 or wider, within the bound.
A program may use at most 192 MiB of HBM per device.

```python
import math
import jax
import jax.numpy as jnp
from jax import lax

D = 2048
M = 2048
ITERS = 4
N = 65536


def draw_signs(key, part):
    return (2 * jax.random.randint(key, (N,), 0, 2) - 1).astype(jnp.int32)


def touch_ends(array, own_key, smallest, top_value):
    extent = array.shape
    index_at = [jax.random.randint(jax.random.fold_in(own_key, axis), (), 0, extent[axis]) for axis in range(len(extent))]
    array = array.at[tuple(index_at)].set(smallest)
    longest = extent.index(max(extent))
    index_at[longest] = (index_at[longest] + 1) % extent[longest]
    return array.at[tuple(index_at)].set(top_value)


def levels(own_key, dims, shards, least, high):
    loudness = 1.0
    for axis_at, shards_of in shards:
        heights = jax.random.uniform(jax.random.fold_in(jax.random.fold_in(own_key, 6), axis_at), (shards_of,), jnp.float32, least / len(shards), high / len(shards))
        loudness = loudness * jnp.repeat(jnp.exp(heights), dims[axis_at] // shards_of).reshape((-1,) + (1,) * (len(dims) - 1 - axis_at))
    return loudness


def gaussian(rng, extent, width, most, pieces=(), held_as=jnp.bfloat16):
    level = levels(rng, extent, pieces, -0.22, 0.18) if pieces else 1.0
    array = jax.random.normal(rng, extent, jnp.float32) * width * level
    return jnp.minimum(jnp.maximum(array, -most), most).astype(held_as)


def setup_inputs(seed: int = 0) -> dict:
    seeds = jax.random.split(jax.random.key(seed), 7)
    return {
        "features": gaussian(seeds[0], (N, D), D ** -0.5, 0.125, ((0, 32), (1, 4))),
        "weights": gaussian(seeds[1], (D,), 1.0, 6.0, ((0, 4),), jnp.float32),
        "labels": touch_ends((jax.random.randint(seeds[2], (N,), 0, 2) < 1).astype(jnp.int32), jax.random.fold_in(seeds[2], 1), 0, 1),
        "signs": draw_signs(jax.random.fold_in(seeds[6], 71), 0),
        "samples": touch_ends(jax.random.randint(seeds[4], (M,), 0, N), jax.random.fold_in(seeds[4], 1), 0, N - 1).astype(jnp.int32),
        "radius": jnp.clip(jax.random.uniform(seeds[5], (1,), jnp.float32, 0.1, 0.25), 0.1, 0.25),
    }


REG = 0.02

def hadamard_rows(matrix):
    length = matrix.shape[0]
    stride = 1
    while stride < length:
        shaped = matrix.reshape(length // (2 * stride), 2, stride, matrix.shape[1])
        matrix = jnp.stack([shaped[:, 0] + shaped[:, 1], shaped[:, 0] - shaped[:, 1]], axis=1).reshape(length, matrix.shape[1])
        stride = stride * 2
    return matrix

def precondition(factor_lower, residual):
    middle = lax.linalg.triangular_solve(factor_lower, residual[:, None], left_side=True, lower=True)
    return lax.linalg.triangular_solve(factor_lower, middle, left_side=True, lower=True, transpose_a=True)[:, 0]

def reference(features, weights, labels, signs, samples, radius):
    highest = lax.Precision.HIGHEST
    dense = features.astype(jnp.float32)
    margins = jnp.dot(dense, weights, precision=highest)
    probability = 1.0 / (1.0 + jnp.exp(-margins))
    curvature = probability * (1.0 - probability)
    ridge = REG / D
    gradient = jnp.dot(probability - labels.astype(jnp.float32), dense, precision=highest) / N + ridge * weights
    weighted = (jnp.sqrt(curvature)[:, None] * dense).astype(jnp.bfloat16)
    weighted_float = weighted.astype(jnp.float32)
    mixed = hadamard_rows(weighted_float * signs.astype(jnp.float32)[:, None])
    sketch = (mixed[samples] * (1.0 / math.sqrt(N * M))).astype(jnp.bfloat16)
    gram = jnp.dot(sketch.T.astype(jnp.float32), sketch.astype(jnp.float32), preferred_element_type=jnp.float32) + ridge * jnp.eye(D, dtype=jnp.float32)
    factor_lower = jnp.linalg.cholesky(gram)
    solution = jnp.zeros((D,), jnp.float32)
    residual = -gradient
    solved = precondition(factor_lower, residual)
    inner_now = jnp.dot(residual, solved)
    direction = solved
    for number in range(ITERS):
        row_sums = jnp.dot(weighted_float, direction, precision=highest)
        curved = jnp.dot(row_sums, weighted_float, precision=highest) / N + ridge * direction
        step_size = inner_now / jnp.dot(direction, curved)
        solution = solution + step_size * direction
        residual = residual - step_size * curved
        solved = precondition(factor_lower, residual)
        inner_next = jnp.dot(residual, solved)
        direction = solved + inner_next / inner_now * direction
        inner_now = inner_next
    length_sq = jnp.dot(solution, solution)
    scale_step = jnp.minimum(1.0, radius[0] * math.sqrt(D) / jnp.sqrt(length_sq + 1e-06))
    return weights + scale_step * solution
```

```python
import math

import jax
import jax.numpy as jnp
from jax import lax
from jax.experimental import pallas as pl
from jax.experimental.pallas import tpu as pltpu
from jax.sharding import PartitionSpec as P

D = 2048
ITERS = 4
REG = 0.02
HI = lax.Precision.HIGHEST
NN = (((1,), (0,)), ((), ()))
NT = (((1,), (1,)), ((), ()))
TN = (((0,), (0,)), ((), ()))
MESH = pl.DeviceIdType.MESH

def split2(value):
    high = value.astype(jnp.bfloat16)
    return high, (value - high.astype(jnp.float32)).astype(jnp.bfloat16)


def block_inverse(block):
    lanes = lax.broadcasted_iota(jnp.int32, (1, 128), 1)
    subs = lax.broadcasted_iota(jnp.int32, (8, 128), 0)
    tiles = [block[8 * t : 8 * t + 8, :] for t in range(16)]
    column = [jnp.broadcast_to(tile[:, 0:1], (8, 128)) for tile in tiles]
    for k in range(128):
        t0, r = k // 8, k % 8
        pivot = jnp.broadcast_to(column[t0][r : r + 1, :], (8, 128))
        inverse = 1.0 / pivot
        scaled = [None] * 16
        for t in range(t0, 16):
            scaled[t] = column[t] * inverse
        scaled[t0] = jnp.where(subs > r, scaled[t0], 0.0)
        row = tiles[t0][r : r + 1, :]
        row = jnp.broadcast_to(jnp.where(lanes == k, row + row, row), (8, 128))
        if k + 1 < 128:
            ahead = [None] * 16
            for t in range(t0, 16):
                ahead[t] = jnp.broadcast_to(tiles[t][:, k + 1 : k + 2], (8, 128))
            cross = jnp.broadcast_to(ahead[t0][r : r + 1, :], (8, 128))
            column = [None] * 16
            for t in range(t0, 16):
                column[t] = ahead[t] - scaled[t] * cross
        for t in range(t0, 16):
            tiles[t] = tiles[t] - scaled[t] * row
    whole = jnp.concatenate(tiles, axis=0)
    rows = lax.broadcasted_iota(jnp.int32, (128, 128), 0)
    cols = lax.broadcasted_iota(jnp.int32, (128, 128), 1)
    diagonal = jnp.where(rows == cols, whole, 0.0)
    along_rows = jnp.sum(diagonal, axis=0, keepdims=True)
    along_cols = jnp.sum(diagonal, axis=1, keepdims=True)
    lower = jnp.where(cols <= rows, whole, 0.0)
    return lower * (1.0 / along_rows) * (1.0 / jnp.sqrt(along_cols))


def factor_kernel(sketch, up_hi, up_lo, inv_hi, inv_lo, gram, invs, trio_l, trio_r):
    ridge = REG / D
    for a in range(4):
        for b in range(a, 4):
            for h in range(2):
                part = lax.dot_general(
                    sketch[:, 512 * a + 256 * h : 512 * a + 256 * h + 256], sketch[:, 512 * b : 512 * b + 512], TN, preferred_element_type=jnp.float32
                )
                if a == b:
                    rows = lax.broadcasted_iota(jnp.int32, (256, 512), 0) + 256 * h
                    cols = lax.broadcasted_iota(jnp.int32, (256, 512), 1)
                    part = part + jnp.where(rows == cols, ridge, 0.0)
                gram[512 * a + 256 * h : 512 * a + 256 * h + 256, 512 * b : 512 * b + 512] = part

    def step(k, carry):
        at = pl.multiple_of(k * 128, 128)
        rows = pl.ds(at, 128)
        inverse = block_inverse(gram[rows, rows])
        invs[k] = inverse
        first = k // 4
        ih, il = split2(inverse)
        ileft = jnp.concatenate([ih, ih, il], axis=1)
        for c in range(4):

            @pl.when(c >= first)
            def _():
                cs = slice(512 * c, 512 * c + 512)
                gh, gl = split2(gram[rows, cs])
                panel = lax.dot_general(ileft, jnp.concatenate([gh, gl, gh], axis=0), NN, preferred_element_type=jnp.float32)
                cols = lax.broadcasted_iota(jnp.int32, (128, 512), 1) + 512 * c
                panel = jnp.where(cols >= at + 128, panel, 0.0)
                gram[rows, cs] = panel
                ph, plo = split2(panel)
                trio_r[0:128, cs] = ph
                trio_r[128:256, cs] = plo
                trio_r[256:384, cs] = ph
                trio_l[0:128, cs] = ph
                trio_l[128:256, cs] = ph
                trio_l[256:384, cs] = plo

        for a in range(4):

            @pl.when(a >= first)
            def _():
                ra = slice(512 * a, 512 * a + 512)
                for b in range(a, 4):
                    cs = slice(512 * b, 512 * b + 512)
                    gram[ra, cs] = gram[ra, cs] - lax.dot_general(trio_l[:, ra], trio_r[:, cs], TN, preferred_element_type=jnp.float32)

        return carry

    lax.fori_loop(0, 16, step, 0)

    def chunk(a, carry):
        at = pl.multiple_of(a * 512, 512)

        def up(i, j, size):
            return gram[pl.ds(pl.multiple_of(at + i, 128), size), pl.ds(pl.multiple_of(at + j, 128), size)]

        def join(top, bottom, cross):
            middle = lax.dot_general(cross, top, TN, precision=HI, preferred_element_type=jnp.float32)
            corner = -lax.dot_general(bottom, middle, NN, precision=HI, preferred_element_type=jnp.float32)
            zero = jnp.zeros_like(top)
            return jnp.concatenate([jnp.concatenate([top, zero], axis=1), jnp.concatenate([corner, bottom], axis=1)], axis=0)

        q = [invs[4 * a + i] for i in range(4)]
        one = join(q[0], q[1], up(0, 128, 128))
        two = join(q[2], q[3], up(256, 384, 128))
        whole = join(one, two, up(0, 256, 256))
        hi, lo = split2(whole)
        inv_hi[a] = hi
        inv_lo[a] = lo
        hi, lo = split2(gram[pl.ds(at, 512), :])
        up_hi[pl.ds(at, 512), :] = hi
        up_lo[pl.ds(at, 512), :] = lo
        return carry

    lax.fori_loop(0, 4, chunk, 0)


def factor(sketch):
    vm = pl.BlockSpec(memory_space=pltpu.VMEM)
    return pl.pallas_call(
        factor_kernel,
        out_shape=(
            jax.ShapeDtypeStruct((D, D), jnp.bfloat16),
            jax.ShapeDtypeStruct((D, D), jnp.bfloat16),
            jax.ShapeDtypeStruct((4, 512, 512), jnp.bfloat16),
            jax.ShapeDtypeStruct((4, 512, 512), jnp.bfloat16),
        ),
        in_specs=[vm],
        out_specs=(vm, vm, vm, vm),
        scratch_shapes=[
            pltpu.VMEM((D, D), jnp.float32),
            pltpu.VMEM((16, 128, 128), jnp.float32),
            pltpu.VMEM((384, D), jnp.bfloat16),
            pltpu.VMEM((384, D), jnp.bfloat16),
        ],
        compiler_params=pltpu.CompilerParams(vmem_limit_bytes=60 * 2**20),
        name="factor",
    )(sketch)


def pieces(row):
    first = row.astype(jnp.bfloat16).astype(jnp.float32)
    rest = row - first
    second = rest.astype(jnp.bfloat16).astype(jnp.float32)
    third = rest - second
    which = lax.broadcasted_iota(jnp.int32, (16, row.shape[1]), 0)
    stacked = jnp.where(which == 0, first, jnp.where(which == 1, second, jnp.where(which == 2, third, 0.0)))
    return stacked.astype(jnp.bfloat16)


def row_times(row, matrix, dims):
    return jnp.sum(lax.dot_general(pieces(row), matrix, dims, preferred_element_type=jnp.float32), axis=0, keepdims=True)


def pcg_kernel(total_rows, weighted, grad, up_hi, up_lo, inv_hi, inv_lo, weights, radius, out, full, zbuf, abuf, bbuf, zs, zr, a_s, a_r, b_s, b_r):
    ex = lax.axis_index("ex")
    feat = lax.axis_index("feat")
    plane, within = ex // 8, ex % 8
    ridge = REG / D
    own = pl.ds(pl.multiple_of(feat * 512, 512), 512)

    def near(o):
        return (plane * 8 + (within + o) % 8, feat)

    def far(o):
        other = (plane * 4 + feat + o) % 16
        return ((other // 4) * 8 + within, other % 4)

    def along(o):
        return (ex, (feat + o) % 4)

    barrier = pltpu.get_barrier_semaphore()
    for o in range(1, 8):
        pl.semaphore_signal(barrier, inc=1, device_id=near(o), device_id_type=MESH)
    for o in range(1, 16):
        pl.semaphore_signal(barrier, inc=1, device_id=far(o), device_id_type=MESH)
    pl.semaphore_wait(barrier, 22)

    def exchange(value, buf, turn, me, count, peer, send, recv):
        buf[turn, me] = value
        copies = [
            pltpu.make_async_remote_copy(
                src_ref=buf.at[turn, me],
                dst_ref=buf.at[turn, me],
                send_sem=send.at[turn, o],
                recv_sem=recv.at[turn, o],
                device_id=peer(o),
                device_id_type=MESH,
            )
            for o in range(1, count)
        ]
        for copy in copies:
            copy.start()
        for copy in copies:
            copy.wait()

    def over_examples(part, turn):
        exchange(part, abuf, turn, within, 8, near, a_s, a_r)
        total = abuf[turn, 0]
        for q in range(1, 8):
            total = total + abuf[turn, q]
        exchange(total, bbuf, turn, plane * 4 + feat, 16, far, b_s, b_r)
        parts = []
        for z in range(4):
            parts.append((bbuf[turn, z] + bbuf[turn, 4 + z]) + (bbuf[turn, 8 + z] + bbuf[turn, 12 + z]))
        return jnp.concatenate(parts, axis=1)

    def over_features(part, turn):
        exchange(part, zbuf, turn, feat, 4, along, zs, zr)
        return (zbuf[turn, 0] + zbuf[turn, 1]) + (zbuf[turn, 2] + zbuf[turn, 3])

    def times(row, high, low, dims):
        high_row = row.astype(jnp.bfloat16).astype(jnp.float32)
        which = lax.broadcasted_iota(jnp.int32, (16, row.shape[1]), 0)
        stacked = jnp.where(which == 0, high_row, jnp.where(which == 1, row - high_row, 0.0)).astype(jnp.bfloat16)
        product = lax.dot_general(stacked, high, dims, preferred_element_type=jnp.float32)
        product = product + lax.dot_general(stacked, low, dims, preferred_element_type=jnp.float32)
        return jnp.sum(product, axis=0, keepdims=True)

    def solve(row):
        rest = row
        middle = []
        for a in range(4):
            part = times(rest[:, :512], inv_hi[a], inv_lo[a], NT)
            middle.append(part)
            if a < 3:
                here, right = slice(512 * a, 512 * a + 512), slice(512 * a + 512, D)
                rest = rest[:, 512:] - times(part, up_hi[here, right], up_lo[here, right], NN)
        rest = jnp.concatenate(middle, axis=1)
        result = []
        for a in range(3, -1, -1):
            part = times(rest[:, 512 * a :], inv_hi[a], inv_lo[a], NN)
            result.insert(0, part)
            if a > 0:
                above, here = slice(0, 512 * a), slice(512 * a, 512 * a + 512)
                rest = rest[:, : 512 * a] - times(part, up_hi[above, here], up_lo[above, here], NT)
        return jnp.concatenate(result, axis=1)

    def dot(left, right):
        return jnp.sum(left * right, axis=1, keepdims=True)

    residual = -over_examples(grad[...] * (1.0 / total_rows) + weights[...] * (ridge / 32), 0)

    def step(number, carry):
        answer, residual, direction, inner = carry
        solved = solve(residual)
        inner_now = dot(residual, solved)
        direction = solved + jnp.where(number == 0, 0.0, inner_now / inner) * direction
        full[...] = direction
        row_sums = over_features(row_times(full[:, own], weighted[...], NT), number)
        product = over_examples(row_times(row_sums, weighted[...], NN), number + 1)
        curved = product * (1.0 / total_rows) + ridge * direction
        step_size = inner_now / dot(direction, curved)
        return answer + step_size * direction, residual - step_size * curved, direction, inner_now

    zero = jnp.zeros((1, D), jnp.float32)
    answer = lax.fori_loop(0, ITERS, step, (zero, residual, zero, jnp.ones((1, 1), jnp.float32)))[0]
    scale = jnp.minimum(1.0, radius[...] * math.sqrt(D) / jnp.sqrt(dot(answer, answer) + 1e-06))
    full[...] = answer
    out[...] = weights[...] + scale * full[:, own]


def pcg(total_rows, weighted, grad, factors, weights, radius):
    vm = pl.BlockSpec(memory_space=pltpu.VMEM)
    dma = pltpu.SemaphoreType.DMA
    return pl.pallas_call(
        lambda *refs: pcg_kernel(total_rows, *refs),
        out_shape=jax.ShapeDtypeStruct((1, 512), jnp.float32),
        in_specs=[vm] * 8,
        out_specs=vm,
        scratch_shapes=[
            pltpu.VMEM((1, D), jnp.float32),
            pltpu.VMEM((4, 4, 1, D), jnp.float32),
            pltpu.VMEM((5, 8, 1, 512), jnp.float32),
            pltpu.VMEM((5, 16, 1, 512), jnp.float32),
            dma((4, 4)),
            dma((4, 4)),
            dma((5, 8)),
            dma((5, 8)),
            dma((5, 16)),
            dma((5, 16)),
        ],
        compiler_params=pltpu.CompilerParams(vmem_limit_bytes=48 * 2**20, collective_id=0, has_side_effects=True),
        name="pcg",
    )(weighted, grad, *factors, weights, radius)


def parity(common):
    for shift in (8, 4, 2, 1):
        common = common ^ (common >> shift)
    return 1 - 2 * (common & 1)


def local(features, weights, labels, signs, samples, radius):
    row_count, feat_width = features.shape
    ex_count = lax.axis_size("ex")
    ex_index = lax.axis_index("ex")
    total_rows = row_count * ex_count
    sample_count = samples.shape[0]
    dense = features.astype(jnp.float32)
    margins = lax.psum(jnp.dot(dense, weights, precision=HI), "feat")
    probability = 1.0 / (1.0 + jnp.exp(-margins))
    curvature = probability * (1.0 - probability)
    grad_part = jnp.dot(probability - labels.astype(jnp.float32), dense, precision=HI)
    weighted = (jnp.sqrt(curvature)[:, None] * dense).astype(jnp.bfloat16)
    signed = weighted * signs.astype(jnp.bfloat16)[:, None]
    low, high = samples % row_count, samples // row_count
    coarse = parity((low[:, None] // 128) & lax.iota(jnp.int32, row_count // 128)[None, :])
    coarse = coarse * parity(high & ex_index)[:, None]
    fine = parity((low[:, None] % 128) & lax.iota(jnp.int32, 128)[None, :])
    pattern = (coarse.astype(jnp.bfloat16)[:, :, None] * fine.astype(jnp.bfloat16)[:, None, :]).reshape(sample_count, row_count)
    picked = lax.dot_general(pattern, signed, NN, preferred_element_type=jnp.float32)
    summed = lax.psum_scatter(picked, "ex", scatter_dimension=0, tiled=True)
    sketch = (summed * (1.0 / math.sqrt(total_rows * sample_count))).astype(jnp.bfloat16)
    wide = lax.all_gather(sketch, "feat", axis=1, tiled=True)
    whole = lax.all_gather(wide, "ex", axis=0, tiled=True)
    factors = factor(whole)
    out = pcg(total_rows, weighted, grad_part[None, :], factors, weights[None, :], radius[None, :])
    return out[0]


def solution(mesh):
    in_specs = (P("ex", "feat"), P("feat"), P("ex"), P("ex"), P(), P())
    return jax.shard_map(local, mesh=mesh, in_specs=in_specs, out_specs=P("feat"), check_vma=False)
```

```python
import math

import jax
import jax.numpy as jnp
from jax import lax
from jax.experimental import pallas as pl
from jax.experimental.pallas import tpu as pltpu
from jax.sharding import PartitionSpec as P

D = 2048
ITERS = 4
REG = 0.02
HI = lax.Precision.HIGHEST
NN = (((1,), (0,)), ((), ()))
NT = (((1,), (1,)), ((), ()))
TN = (((0,), (0,)), ((), ()))
MESH = pl.DeviceIdType.MESH

def split2(value):
    high = value.astype(jnp.bfloat16)
    return high, (value - high.astype(jnp.float32)).astype(jnp.bfloat16)


def block_inverse(block):
    lanes = lax.broadcasted_iota(jnp.int32, (1, 128), 1)
    subs = lax.broadcasted_iota(jnp.int32, (8, 128), 0)
    tiles = [block[8 * t : 8 * t + 8, :] for t in range(16)]

    def lane(t, at):
        return jnp.broadcast_to(tiles[t][:, at : at + 1], (8, 128))

    def sub(tile, at):
        return jnp.broadcast_to(tile[at : at + 1, :], (8, 128))

    own = [lane(0, j) for j in range(8)]
    nxt = [lane(1, j) for j in range(8)]
    for g in range(16):
        base = 8 * g
        more, most = g + 1 < 16, g + 2 < 16
        if more:
            own_later = [lane(g + 1, base + 8 + j) for j in range(8)]
        if most:
            nxt_later = [lane(g + 2, base + 8 + j) for j in range(8)]
            second = [lane(g + 2, base + j) for j in range(8)]
        inverses, crosses, rows = [], {}, []
        head = tiles[g]
        nxt_scaled, second_scaled = [], []
        for j in range(8):
            inverse = 1.0 / sub(own[j], j)
            inverses.append(inverse)
            scaled = jnp.where(subs > j, own[j] * inverse, 0.0)
            if more:
                nxt_scaled.append(nxt[j] * inverse)
            if most:
                second_scaled.append(second[j] * inverse)
            for i in range(j + 1, 8):
                cross = sub(own[i], j)
                crosses[j, i] = cross
                own[i] = own[i] - scaled * cross
                if more:
                    nxt[i] = nxt[i] - nxt_scaled[j] * cross
                if most:
                    second[i] = second[i] - second_scaled[j] * cross
            if more:
                for i in range(8):
                    cross = sub(nxt[j], i)
                    own_later[i] = own_later[i] - nxt_scaled[j] * cross
                    if most:
                        nxt_later[i] = nxt_later[i] - second_scaled[j] * cross
            row = head[j : j + 1, :]
            row = jnp.broadcast_to(jnp.where(lanes == base + j, row + row, row), (8, 128))
            rows.append(row)
            head = head - scaled * row
        tiles[g] = head
        for t in range(g + 1, 16):
            if t == g + 1:
                scaled = nxt_scaled
            elif t == g + 2:
                scaled = second_scaled
            else:
                column = [lane(t, base + j) for j in range(8)]
                scaled = []
                for j in range(8):
                    scaled.append(column[j] * inverses[j])
                    for i in range(j + 1, 8):
                        column[i] = column[i] - scaled[j] * crosses[j, i]
            tile = tiles[t]
            for j in range(8):
                tile = tile - scaled[j] * rows[j]
            tiles[t] = tile
        if more:
            own = own_later
        if most:
            nxt = nxt_later
    whole = jnp.concatenate(tiles, axis=0)
    rows = lax.broadcasted_iota(jnp.int32, (128, 128), 0)
    cols = lax.broadcasted_iota(jnp.int32, (128, 128), 1)
    diagonal = jnp.where(rows == cols, whole, 0.0)
    along_rows = jnp.sum(diagonal, axis=0, keepdims=True)
    along_cols = jnp.sum(diagonal, axis=1, keepdims=True)
    lower = jnp.where(cols <= rows, whole, 0.0)
    return lower * (1.0 / along_rows) * (1.0 / jnp.sqrt(along_cols))


def factor_kernel(left, right, up_hi, up_lo, inv_hi, inv_lo, gram, invs, trio_l, trio_r):
    ridge = REG / D
    halves = (left, right)
    for a in range(4):
        for b in range(a, 4):
            for h in range(2):
                for side in range(h if a == b else 0, 2):
                    part = lax.dot_general(
                        halves[h][:, 256 * a : 256 * a + 256],
                        halves[side][:, 256 * b : 256 * b + 256],
                        TN,
                        preferred_element_type=jnp.float32,
                    )
                    if a == b and h == side:
                        rows = lax.broadcasted_iota(jnp.int32, (256, 256), 0)
                        cols = lax.broadcasted_iota(jnp.int32, (256, 256), 1)
                        part = part + jnp.where(rows == cols, ridge, 0.0)
                    gram[512 * a + 256 * h : 512 * a + 256 * h + 256, 512 * b + 256 * side : 512 * b + 256 * side + 256] = part
                    if a == b and h < side:
                        gram[512 * a + 256 : 512 * a + 512, 512 * a : 512 * a + 256] = jnp.zeros((256, 256), jnp.float32)

    def step(k, carry):
        at = pl.multiple_of(k * 128, 128)
        rows = pl.ds(at, 128)
        inverse = block_inverse(gram[rows, rows])
        invs[k] = inverse
        first = k // 4
        ih, il = split2(inverse)
        ileft = jnp.concatenate([ih, ih, il], axis=1)
        for c in range(4):

            @pl.when(c >= first)
            def _():
                cs = slice(512 * c, 512 * c + 512)
                gh, gl = split2(gram[rows, cs])
                panel = lax.dot_general(ileft, jnp.concatenate([gh, gl, gh], axis=0), NN, preferred_element_type=jnp.float32)
                cols = lax.broadcasted_iota(jnp.int32, (128, 512), 1) + 512 * c
                panel = jnp.where(cols >= at + 128, panel, 0.0)
                gram[rows, cs] = panel
                ph, plo = split2(panel)
                trio_r[0:128, cs] = ph
                trio_r[128:256, cs] = plo
                trio_r[256:384, cs] = ph
                trio_l[0:128, cs] = ph
                trio_l[128:256, cs] = ph
                trio_l[256:384, cs] = plo

        for a in range(4):

            @pl.when(a >= first)
            def _():
                ra = slice(512 * a, 512 * a + 512)
                for b in range(a, 4):
                    cs = slice(512 * b, 512 * b + 512)
                    gram[ra, cs] = gram[ra, cs] - lax.dot_general(trio_l[:, ra], trio_r[:, cs], TN, preferred_element_type=jnp.float32)

        return carry

    lax.fori_loop(0, 16, step, 0)

    def chunk(a, carry):
        at = pl.multiple_of(a * 512, 512)

        def up(i, j, size):
            return gram[pl.ds(pl.multiple_of(at + i, 128), size), pl.ds(pl.multiple_of(at + j, 128), size)]

        def join(top, bottom, cross):
            middle = lax.dot_general(cross, top, TN, precision=HI, preferred_element_type=jnp.float32)
            corner = -lax.dot_general(bottom, middle, NN, precision=HI, preferred_element_type=jnp.float32)
            zero = jnp.zeros_like(top)
            return jnp.concatenate([jnp.concatenate([top, zero], axis=1), jnp.concatenate([corner, bottom], axis=1)], axis=0)

        q = [invs[4 * a + i] for i in range(4)]
        one = join(q[0], q[1], up(0, 128, 128))
        two = join(q[2], q[3], up(256, 384, 128))
        whole = join(one, two, up(0, 256, 256))
        hi, lo = split2(whole)
        inv_hi[a] = hi
        inv_lo[a] = lo
        hi, lo = split2(gram[pl.ds(at, 512), :])
        up_hi[pl.ds(at, 512), :] = hi
        up_lo[pl.ds(at, 512), :] = lo
        return carry

    lax.fori_loop(0, 4, chunk, 0)


def factor(left, right):
    vm = pl.BlockSpec(memory_space=pltpu.VMEM)
    return pl.pallas_call(
        factor_kernel,
        out_shape=(
            jax.ShapeDtypeStruct((D, D), jnp.bfloat16),
            jax.ShapeDtypeStruct((D, D), jnp.bfloat16),
            jax.ShapeDtypeStruct((4, 512, 512), jnp.bfloat16),
            jax.ShapeDtypeStruct((4, 512, 512), jnp.bfloat16),
        ),
        in_specs=[vm, vm],
        out_specs=(vm, vm, vm, vm),
        scratch_shapes=[
            pltpu.VMEM((D, D), jnp.float32),
            pltpu.VMEM((16, 128, 128), jnp.float32),
            pltpu.VMEM((384, D), jnp.bfloat16),
            pltpu.VMEM((384, D), jnp.bfloat16),
        ],
        compiler_params=pltpu.CompilerParams(vmem_limit_bytes=60 * 2**20),
        name="factor",
    )(left, right)


def pieces(row):
    first = row.astype(jnp.bfloat16).astype(jnp.float32)
    rest = row - first
    second = rest.astype(jnp.bfloat16).astype(jnp.float32)
    third = rest - second
    which = lax.broadcasted_iota(jnp.int32, (16, row.shape[1]), 0)
    stacked = jnp.where(which == 0, first, jnp.where(which == 1, second, jnp.where(which == 2, third, 0.0)))
    return stacked.astype(jnp.bfloat16)


def row_times(row, matrix, dims):
    return jnp.sum(lax.dot_general(pieces(row), matrix, dims, preferred_element_type=jnp.float32), axis=0, keepdims=True)


def pcg_kernel(total_rows, weighted, grad, up_hi, up_lo, inv_hi, inv_lo, weights, radius, out, full, zbuf, abuf, bbuf, zs, zr, a_s, a_r, b_s, b_r):
    ex = lax.axis_index("ex")
    feat = lax.axis_index("feat")
    plane, within = ex // 8, ex % 8
    ridge = REG / D
    own = pl.ds(pl.multiple_of(feat * 512, 512), 512)

    def near(o):
        return (plane * 8 + (within + o) % 8, feat)

    def far(o):
        other = (plane * 4 + feat + o) % 16
        return ((other // 4) * 8 + within, other % 4)

    def along(o):
        return (ex, (feat + o) % 4)

    barrier = pltpu.get_barrier_semaphore()
    for o in range(1, 8):
        pl.semaphore_signal(barrier, inc=1, device_id=near(o), device_id_type=MESH)
    for o in range(1, 16):
        pl.semaphore_signal(barrier, inc=1, device_id=far(o), device_id_type=MESH)
    pl.semaphore_wait(barrier, 22)

    def exchange(value, buf, turn, me, count, peer, send, recv):
        buf[turn, me] = value
        copies = [
            pltpu.make_async_remote_copy(
                src_ref=buf.at[turn, me],
                dst_ref=buf.at[turn, me],
                send_sem=send.at[turn, o],
                recv_sem=recv.at[turn, o],
                device_id=peer(o),
                device_id_type=MESH,
            )
            for o in range(1, count)
        ]
        for copy in copies:
            copy.start()
        for copy in copies:
            copy.wait()

    def over_examples(part, turn):
        exchange(part, abuf, turn, within, 8, near, a_s, a_r)
        total = abuf[turn, 0]
        for q in range(1, 8):
            total = total + abuf[turn, q]
        exchange(total, bbuf, turn, plane * 4 + feat, 16, far, b_s, b_r)
        parts = []
        for z in range(4):
            parts.append((bbuf[turn, z] + bbuf[turn, 4 + z]) + (bbuf[turn, 8 + z] + bbuf[turn, 12 + z]))
        return jnp.concatenate(parts, axis=1)

    def over_features(part, turn):
        exchange(part, zbuf, turn, feat, 4, along, zs, zr)
        return (zbuf[turn, 0] + zbuf[turn, 1]) + (zbuf[turn, 2] + zbuf[turn, 3])

    def times(row, high, low, dims):
        high_row = row.astype(jnp.bfloat16).astype(jnp.float32)
        which = lax.broadcasted_iota(jnp.int32, (16, row.shape[1]), 0)
        stacked = jnp.where(which == 0, high_row, jnp.where(which == 1, row - high_row, 0.0)).astype(jnp.bfloat16)
        product = lax.dot_general(stacked, high, dims, preferred_element_type=jnp.float32)
        product = product + lax.dot_general(stacked, low, dims, preferred_element_type=jnp.float32)
        return jnp.sum(product, axis=0, keepdims=True)

    def solve(row):
        rest = row
        middle = []
        for a in range(4):
            part = times(rest[:, :512], inv_hi[a], inv_lo[a], NT)
            middle.append(part)
            if a < 3:
                here, right = slice(512 * a, 512 * a + 512), slice(512 * a + 512, D)
                rest = rest[:, 512:] - times(part, up_hi[here, right], up_lo[here, right], NN)
        rest = jnp.concatenate(middle, axis=1)
        result = []
        for a in range(3, -1, -1):
            part = times(rest[:, 512 * a :], inv_hi[a], inv_lo[a], NN)
            result.insert(0, part)
            if a > 0:
                above, here = slice(0, 512 * a), slice(512 * a, 512 * a + 512)
                rest = rest[:, : 512 * a] - times(part, up_hi[above, here], up_lo[above, here], NT)
        return jnp.concatenate(result, axis=1)

    def dot(left, right):
        return jnp.sum(left * right, axis=1, keepdims=True)

    residual = -over_examples(grad[...] * (1.0 / total_rows) + weights[...] * (ridge / 32), 0)

    def step(number, carry):
        answer, residual, direction, inner = carry
        solved = solve(residual)
        inner_now = dot(residual, solved)
        direction = solved + jnp.where(number == 0, 0.0, inner_now / inner) * direction
        full[...] = direction
        row_sums = over_features(row_times(full[:, own], weighted[...], NT), number)
        product = over_examples(row_times(row_sums, weighted[...], NN), number + 1)
        curved = product * (1.0 / total_rows) + ridge * direction
        step_size = inner_now / dot(direction, curved)
        return answer + step_size * direction, residual - step_size * curved, direction, inner_now

    zero = jnp.zeros((1, D), jnp.float32)
    answer = lax.fori_loop(0, ITERS, step, (zero, residual, zero, jnp.ones((1, 1), jnp.float32)))[0]
    scale = jnp.minimum(1.0, radius[...] * math.sqrt(D) / jnp.sqrt(dot(answer, answer) + 1e-06))
    full[...] = answer
    out[...] = weights[...] + scale * full[:, own]


def pcg(total_rows, weighted, grad, factors, weights, radius):
    vm = pl.BlockSpec(memory_space=pltpu.VMEM)
    dma = pltpu.SemaphoreType.DMA
    return pl.pallas_call(
        lambda *refs: pcg_kernel(total_rows, *refs),
        out_shape=jax.ShapeDtypeStruct((1, 512), jnp.float32),
        in_specs=[vm] * 8,
        out_specs=vm,
        scratch_shapes=[
            pltpu.VMEM((1, D), jnp.float32),
            pltpu.VMEM((4, 4, 1, D), jnp.float32),
            pltpu.VMEM((5, 8, 1, 512), jnp.float32),
            pltpu.VMEM((5, 16, 1, 512), jnp.float32),
            dma((4, 4)),
            dma((4, 4)),
            dma((5, 8)),
            dma((5, 8)),
            dma((5, 16)),
            dma((5, 16)),
        ],
        compiler_params=pltpu.CompilerParams(vmem_limit_bytes=48 * 2**20, collective_id=0, has_side_effects=True),
        name="pcg",
    )(weighted, grad, *factors, weights, radius)


def sketch_kernel(scale, signed, coarse, fine, left, right, send, keep, arrive, narrow, xin, yin, stage, xlast, ylast, mine, ssem, rsem, lsem):
    ex = lax.axis_index("ex")
    z = lax.axis_index("feat")
    y, x, c = ex // 8, (ex // 2) % 4, ex % 2

    def to_x(o):
        return ((y * 4 + (x + o) % 4) * 2 + c, z)

    def to_y(o):
        return ((((y + o) % 4) * 4 + x) * 2 + c, z)

    def to_z(o):
        return (ex, (z + o) % 4)

    other = (ex + 1 - 2 * c, z)
    barrier = pltpu.get_barrier_semaphore()
    for o in range(1, 4):
        for peer in (to_x, to_y, to_z):
            pl.semaphore_signal(barrier, inc=1, device_id=peer(o), device_id_type=MESH)
    pl.semaphore_signal(barrier, inc=1, device_id=other, device_id_type=MESH)

    started = []

    def ship(src, dst, device):
        at = len(started)
        copy = pltpu.make_async_remote_copy(
            src_ref=src, dst_ref=dst, send_sem=ssem.at[at], recv_sem=rsem.at[at], device_id=device, device_id_type=MESH
        )
        copy.start()
        started.append(copy)
        return copy

    def mixed(row):
        rows = pl.ds(pl.multiple_of(row, 256), 256)
        fine_rows = fine[rows, :]
        pattern = jnp.concatenate([fine_rows * jnp.broadcast_to(coarse[rows, h : h + 1], (256, 128)) for h in range(16)], axis=1)
        return jnp.dot(pattern, signed[...], preferred_element_type=jnp.float32)

    halves = []
    for q in range(4):
        send[q] = mixed((1 - c) * 1024 + 256 * q)
        if q == 0:
            pl.semaphore_wait(barrier, 10)
        halves.append(ship(send.at[q], arrive.at[q], other))
    for q in range(4):
        keep[q] = mixed(c * 1024 + 256 * q)
    for q in range(4):
        halves[q].wait_recv()
        total = keep[q] + arrive[q]
        keep[q] = total
        narrow[0, q] = total[:, :256].astype(jnp.bfloat16)
        narrow[1, q] = total[:, 256:].astype(jnp.bfloat16)
    first = []
    for o in range(1, 4):
        first.append(ship(narrow.at[0, (x + o) % 4], xin.at[o - 1], to_x(o)))
        first.append(ship(narrow.at[1, (y + o) % 4], yin.at[o - 1], to_y(o)))
    for copy in first:
        copy.wait_recv()
    left_total = keep[x, :, :256]
    right_total = keep[y, :, 256:]
    for o in range(3):
        left_total = left_total + xin[o].astype(jnp.float32)
        right_total = right_total + yin[o].astype(jnp.float32)
    for q in range(4):
        stage[0, q] = left_total[64 * q : 64 * q + 64, :]
        stage[1, q] = right_total[64 * q : 64 * q + 64, :]
    second = []
    for o in range(1, 4):
        second.append(ship(stage.at[0, (y + o) % 4], ylast.at[o - 1], to_y(o)))
        second.append(ship(stage.at[1, (x + o) % 4], xlast.at[o - 1], to_x(o)))
    for copy in second:
        copy.wait_recv()
    mine[0] = ((stage[0, y] + ylast[0] + ylast[1] + ylast[2]) * scale).astype(jnp.bfloat16)
    mine[1] = ((stage[1, x] + xlast[0] + xlast[1] + xlast[2]) * scale).astype(jnp.bfloat16)

    cols = pl.ds(pl.multiple_of(z * 256, 256), 256)
    big, small = pl.ds(0, 48), pl.ds(48, 16)
    every = pl.ds(0, 4)
    own_left = pltpu.make_async_copy(mine.at[0], left.at[c, x, y, :, cols], lsem.at[0])
    own_right = pltpu.make_async_copy(mine.at[1], right.at[c, y, x, :, cols], lsem.at[1])
    own_left.start()
    own_right.start()

    def pass_on(work):
        copies = []
        for o in range(1, 4):
            for src, dst, peer in work:
                copies.append(ship(src, dst, peer(o)))
        return copies

    def same(ref, peer):
        return (ref, ref, peer)

    here_left, here_right = left.at[c, x, y], right.at[c, y, x]
    copies = pass_on(
        [
            (mine.at[0, big], left.at[c, x, y, big, cols], to_z),
            (mine.at[1, big], right.at[c, y, x, big, cols], to_z),
            (mine.at[0, small], left.at[c, x, y, small, cols], to_y),
            (mine.at[1, small], right.at[c, y, x, small, cols], to_x),
        ]
    )
    own_left.wait()
    own_right.wait()
    for copy in copies:
        copy.wait_recv()
    copies = pass_on(
        [
            same(left.at[c, x, y, big, :], to_y),
            same(right.at[c, y, x, big, :], to_x),
            same(left.at[c, x, every, small, cols], to_x),
            same(right.at[c, y, every, small, cols], to_y),
        ]
    )
    for copy in copies:
        copy.wait_recv()
    copies = pass_on(
        [
            same(left.at[c, x, every, big, :], to_x),
            same(right.at[c, y, every, big, :], to_y),
            same(left.at[c, every, every, small, cols], to_z),
            same(right.at[c, every, every, small, cols], to_z),
        ]
    )
    across = []
    for o in range(4):
        if o > 0:
            for copy in copies[4 * o - 4 : 4 * o]:
                copy.wait_recv()
        from_x, from_y = (x + 4 - o) % 4, (y + 4 - o) % 4
        from_z = pl.ds(pl.multiple_of(((z + 4 - o) % 4) * 256, 256), 256)
        for ref in (
            left.at[c, from_x, every, big, :],
            right.at[c, from_y, every, big, :],
            left.at[c, every, every, small, from_z],
            right.at[c, every, every, small, from_z],
        ):
            across.append(ship(ref, ref, other))
    for copy in across:
        copy.wait_recv()
    for copy in started:
        copy.wait_send()


def sketch_rows(scale, signed, coarse, fine):
    vm = pl.BlockSpec(memory_space=pltpu.VMEM)
    anywhere = pl.BlockSpec(memory_space=pl.ANY)
    f32, bf16 = jnp.float32, jnp.bfloat16
    half = jax.ShapeDtypeStruct((2, 4, 4, 64, D // 2), bf16)
    left, right = pl.pallas_call(
        lambda *refs: sketch_kernel(scale, *refs),
        out_shape=(half, half),
        in_specs=[vm] * 3,
        out_specs=(anywhere, anywhere),
        scratch_shapes=[
            pltpu.VMEM((4, 256, 512), f32),
            pltpu.VMEM((4, 256, 512), f32),
            pltpu.VMEM((4, 256, 512), f32),
            pltpu.VMEM((2, 4, 256, 256), bf16),
            pltpu.VMEM((3, 256, 256), bf16),
            pltpu.VMEM((3, 256, 256), bf16),
            pltpu.VMEM((2, 4, 64, 256), f32),
            pltpu.VMEM((3, 64, 256), f32),
            pltpu.VMEM((3, 64, 256), f32),
            pltpu.VMEM((2, 64, 256), bf16),
            pltpu.SemaphoreType.DMA((72,)),
            pltpu.SemaphoreType.DMA((72,)),
            pltpu.SemaphoreType.DMA((2,)),
        ],
        compiler_params=pltpu.CompilerParams(vmem_limit_bytes=32 * 2**20, collective_id=1, has_side_effects=True),
        name="sketch",
    )(signed, coarse, fine)
    return left.reshape(D, D // 2), right.reshape(D, D // 2)


def parity(common):
    for shift in (8, 4, 2, 1):
        common = common ^ (common >> shift)
    return 1 - 2 * (common & 1)


def local(features, weights, labels, signs, samples, radius):
    row_count, feat_width = features.shape
    ex_count = lax.axis_size("ex")
    ex_index = lax.axis_index("ex")
    total_rows = row_count * ex_count
    sample_count = samples.shape[0]
    dense = features.astype(jnp.float32)
    margins = lax.psum(jnp.dot(dense, weights, precision=HI), "feat")
    probability = 1.0 / (1.0 + jnp.exp(-margins))
    curvature = probability * (1.0 - probability)
    grad_part = jnp.dot(probability - labels.astype(jnp.float32), dense, precision=HI)
    weighted = (jnp.sqrt(curvature)[:, None] * dense).astype(jnp.bfloat16)
    signed = weighted * signs.astype(jnp.bfloat16)[:, None]
    low, high = samples % row_count, samples // row_count
    coarse = parity((low[:, None] // 128) & lax.iota(jnp.int32, row_count // 128)[None, :])
    coarse = coarse * parity(high & ex_index)[:, None]
    fine = parity((low[:, None] % 128) & lax.iota(jnp.int32, 128)[None, :])
    scale = 1.0 / math.sqrt(total_rows * sample_count)
    left, right = sketch_rows(scale, signed, coarse.astype(jnp.bfloat16), fine.astype(jnp.bfloat16))
    factors = factor(left, right)
    out = pcg(total_rows, weighted, grad_part[None, :], factors, weights[None, :], radius[None, :])
    return out[0]


def solution(mesh):
    in_specs = (P("ex", "feat"), P("feat"), P("ex"), P("ex"), P(), P())
    return jax.shard_map(local, mesh=mesh, in_specs=in_specs, out_specs=P("feat"), check_vma=False)
```

```python
import math

import jax
import jax.numpy as jnp
from jax import lax
from jax.experimental import pallas as pl
from jax.experimental.pallas import tpu as pltpu
from jax.sharding import PartitionSpec as P

D = 2048
ITERS = 4
REG = 0.02
HI = lax.Precision.HIGHEST
NN = (((1,), (0,)), ((), ()))
NT = (((1,), (1,)), ((), ()))
TN = (((0,), (0,)), ((), ()))
MESH = pl.DeviceIdType.MESH

def split2(value):
    high = value.astype(jnp.bfloat16)
    return high, (value - high.astype(jnp.float32)).astype(jnp.bfloat16)


def block_inverse(block):
    lanes = lax.broadcasted_iota(jnp.int32, (1, 128), 1)
    subs = lax.broadcasted_iota(jnp.int32, (8, 128), 0)
    tiles = [block[8 * t : 8 * t + 8, :] for t in range(16)]

    def lane(t, at):
        return jnp.broadcast_to(tiles[t][:, at : at + 1], (8, 128))

    def sub(tile, at):
        return jnp.broadcast_to(tile[at : at + 1, :], (8, 128))

    own = [lane(0, j) for j in range(8)]
    nxt = [lane(1, j) for j in range(8)]
    for g in range(16):
        base = 8 * g
        more, most = g + 1 < 16, g + 2 < 16
        if more:
            own_later = [lane(g + 1, base + 8 + j) for j in range(8)]
        if most:
            nxt_later = [lane(g + 2, base + 8 + j) for j in range(8)]
            second = [lane(g + 2, base + j) for j in range(8)]
        inverses, crosses, rows = [], {}, []
        head = tiles[g]
        nxt_scaled, second_scaled = [], []
        for j in range(8):
            inverse = 1.0 / sub(own[j], j)
            inverses.append(inverse)
            scaled = jnp.where(subs > j, own[j] * inverse, 0.0)
            if more:
                nxt_scaled.append(nxt[j] * inverse)
            if most:
                second_scaled.append(second[j] * inverse)
            for i in range(j + 1, 8):
                cross = sub(own[i], j)
                crosses[j, i] = cross
                own[i] = own[i] - scaled * cross
                if more:
                    nxt[i] = nxt[i] - nxt_scaled[j] * cross
                if most:
                    second[i] = second[i] - second_scaled[j] * cross
            if more:
                for i in range(8):
                    cross = sub(nxt[j], i)
                    own_later[i] = own_later[i] - nxt_scaled[j] * cross
                    if most:
                        nxt_later[i] = nxt_later[i] - second_scaled[j] * cross
            row = head[j : j + 1, :]
            row = jnp.broadcast_to(jnp.where(lanes == base + j, row + row, row), (8, 128))
            rows.append(row)
            head = head - scaled * row
        tiles[g] = head
        for t in range(g + 1, 16):
            if t == g + 1:
                scaled = nxt_scaled
            elif t == g + 2:
                scaled = second_scaled
            else:
                column = [lane(t, base + j) for j in range(8)]
                scaled = []
                for j in range(8):
                    scaled.append(column[j] * inverses[j])
                    for i in range(j + 1, 8):
                        column[i] = column[i] - scaled[j] * crosses[j, i]
            tile = tiles[t]
            for j in range(8):
                tile = tile - scaled[j] * rows[j]
            tiles[t] = tile
        if more:
            own = own_later
        if most:
            nxt = nxt_later
    whole = jnp.concatenate(tiles, axis=0)
    rows = lax.broadcasted_iota(jnp.int32, (128, 128), 0)
    cols = lax.broadcasted_iota(jnp.int32, (128, 128), 1)
    diagonal = jnp.where(rows == cols, whole, 0.0)
    along_rows = jnp.sum(diagonal, axis=0, keepdims=True)
    along_cols = jnp.sum(diagonal, axis=1, keepdims=True)
    lower = jnp.where(cols <= rows, whole, 0.0)
    return lower * (1.0 / along_rows) * (1.0 / jnp.sqrt(along_cols))


def factor_kernel(left, right, up_hi, up_lo, inv_hi, inv_lo, gram, invs, crosses, corner, trio_l, trio_r):
    ridge = REG / D
    halves = (left, right)
    for a in range(4):
        for b in range(a, 4):
            for h in range(2):
                for side in range(h if a == b else 0, 2):
                    part = lax.dot_general(
                        halves[h][:, 256 * a : 256 * a + 256],
                        halves[side][:, 256 * b : 256 * b + 256],
                        TN,
                        preferred_element_type=jnp.float32,
                    )
                    if a == b and h == side:
                        rows = lax.broadcasted_iota(jnp.int32, (256, 256), 0)
                        cols = lax.broadcasted_iota(jnp.int32, (256, 256), 1)
                        part = part + jnp.where(rows == cols, ridge, 0.0)
                    gram[512 * a + 256 * h : 512 * a + 256 * h + 256, 512 * b + 256 * side : 512 * b + 256 * side + 256] = part
                    if a == b and h < side:
                        gram[512 * a + 256 : 512 * a + 512, 512 * a : 512 * a + 256] = jnp.zeros((256, 256), jnp.float32)

    def join(top, bottom, cross):
        middle = lax.dot_general(cross, top, TN, precision=HI, preferred_element_type=jnp.float32)
        edge = -lax.dot_general(bottom, middle, NN, precision=HI, preferred_element_type=jnp.float32)
        zero = jnp.zeros_like(top)
        return jnp.concatenate([jnp.concatenate([top, zero], axis=1), jnp.concatenate([edge, bottom], axis=1)], axis=0)

    def step(s, carry):
        at = pl.multiple_of(s * 256, 256)
        next_at = pl.multiple_of(at + 128, 128)
        rows = pl.ds(at, 256)
        first = s // 2
        upper, lower = pl.ds(at, 128), pl.ds(next_at, 128)
        corner[0] = gram[upper, upper]

        def one(h, carry):
            corner[2 + h] = block_inverse(corner[h])

            if h == 0:
                cross = lax.dot_general(corner[2], gram[upper, lower], NN, precision=HI, preferred_element_type=jnp.float32)
                corner[4] = cross
                corner[1] = gram[lower, lower] - lax.dot_general(cross, cross, TN, precision=HI, preferred_element_type=jnp.float32)

            return carry

        one(0, 0)
        one(1, 0)
        inverse = join(corner[2], corner[3], corner[4])
        invs[s] = inverse
        ih, il = split2(inverse)
        ileft = jnp.concatenate([ih, ih, il], axis=1)
        half = pl.ds(pl.multiple_of((s % 2) * 256, 256), 256)
        for c in range(4):

            @pl.when(c >= (s + 1) // 2)
            def _():
                cs = slice(512 * c, 512 * c + 512)
                gh, gl = split2(gram[rows, cs])
                panel = lax.dot_general(ileft, jnp.concatenate([gh, gl, gh], axis=0), NN, preferred_element_type=jnp.float32)
                cols = lax.broadcasted_iota(jnp.int32, (256, 512), 1) + 512 * c
                panel = jnp.where(cols >= at + 256, panel, 0.0)
                ph, plo = split2(panel)
                trio_r[0:256, cs] = ph
                trio_r[256:512, cs] = plo
                trio_r[512:768, cs] = ph
                trio_l[0:256, cs] = ph
                trio_l[256:512, cs] = ph
                trio_l[512:768, cs] = plo

                @pl.when(c == first)
                def _():
                    crosses[first] = panel[:, 256:]

                @pl.when(c > first)
                def _():
                    block = first * (7 - first) // 2 + c - first - 1
                    up_hi[block, half, :] = ph
                    up_lo[block, half, :] = plo

        def across(a, carry):
            ra = pl.ds(pl.multiple_of(a * 512, 512), 512)

            def along(b, carry):
                cs = pl.ds(pl.multiple_of(b * 512, 512), 512)
                gram[ra, cs] = gram[ra, cs] - lax.dot_general(trio_l[:, ra], trio_r[:, cs], TN, preferred_element_type=jnp.float32)
                return carry

            return lax.fori_loop(a, 4, along, carry)

        lax.fori_loop((s + 1) // 2, 4, across, 0)
        return carry

    lax.fori_loop(0, 8, step, 0)

    def chunk(a, carry):
        hi, lo = split2(join(invs[2 * a], invs[2 * a + 1], crosses[a]))
        inv_hi[a] = hi
        inv_lo[a] = lo
        return carry

    lax.fori_loop(0, 4, chunk, 0)


def factor(left, right):
    vm = pl.BlockSpec(memory_space=pltpu.VMEM)
    ups = jax.ShapeDtypeStruct((6, 512, 512), jnp.bfloat16)
    inverses = jax.ShapeDtypeStruct((4, 512, 512), jnp.bfloat16)
    return pl.pallas_call(
        factor_kernel,
        out_shape=(ups, ups, inverses, inverses),
        in_specs=[vm, vm],
        out_specs=(vm, vm, vm, vm),
        scratch_shapes=[
            pltpu.VMEM((D, D), jnp.float32),
            pltpu.VMEM((8, 256, 256), jnp.float32),
            pltpu.VMEM((4, 256, 256), jnp.float32),
            pltpu.VMEM((5, 128, 128), jnp.float32),
            pltpu.VMEM((768, D), jnp.bfloat16),
            pltpu.VMEM((768, D), jnp.bfloat16),
        ],
        compiler_params=pltpu.CompilerParams(vmem_limit_bytes=50 * 2**20),
        cost_estimate=pl.CostEstimate(flops=60 * 10**9, bytes_accessed=18 * 2**20, transcendentals=0),
        name="factor",
    )(left, right)


def pieces(row):
    first = row.astype(jnp.bfloat16).astype(jnp.float32)
    rest = row - first
    second = rest.astype(jnp.bfloat16).astype(jnp.float32)
    third = rest - second
    which = lax.broadcasted_iota(jnp.int32, (16, row.shape[1]), 0)
    stacked = jnp.where(which == 0, first, jnp.where(which == 1, second, jnp.where(which == 2, third, 0.0)))
    return stacked.astype(jnp.bfloat16)


def pair(row):
    first = row.astype(jnp.bfloat16).astype(jnp.float32)
    which = lax.broadcasted_iota(jnp.int32, (16, row.shape[1]), 0)
    return jnp.where(which == 0, first, jnp.where(which == 1, row - first, 0.0)).astype(jnp.bfloat16)


def place(a, b):
    return a * (7 - a) // 2 + b - a - 1


def pcg_kernel(total_rows, w0, w1, w2, w3, grad, up_hi, up_lo, inv_hi, inv_lo, weights, radius, out, full, wide, abuf, bbuf, a_s, a_r, b_s, b_r):
    ex = lax.axis_index("ex")
    feat = lax.axis_index("feat")
    plane, within = ex // 8, ex % 8
    ridge = REG / D
    blocks = (w0, w1, w2, w3)

    def columns(o):
        return pl.ds(pl.multiple_of(((feat + 4 - o) % 4) * 512, 512), 512)

    def near(o):
        return (plane * 8 + (within + o) % 8, feat)

    def far(o):
        other = (plane * 4 + feat + o) % 16
        return ((other // 4) * 8 + within, other % 4)

    barrier = pltpu.get_barrier_semaphore()
    for o in range(1, 8):
        pl.semaphore_signal(barrier, inc=1, device_id=near(o), device_id_type=MESH)
    for o in range(1, 16):
        pl.semaphore_signal(barrier, inc=1, device_id=far(o), device_id_type=MESH)
    pl.semaphore_wait(barrier, 22)

    def exchange(value, buf, turn, me, count, peer, send, recv):
        buf[turn, me] = value
        copies = [
            pltpu.make_async_remote_copy(
                src_ref=buf.at[turn, me],
                dst_ref=buf.at[turn, me],
                send_sem=send.at[turn, o],
                recv_sem=recv.at[turn, o],
                device_id=peer(o),
                device_id_type=MESH,
            )
            for o in range(1, count)
        ]
        for copy in copies:
            copy.start()
        for copy in copies:
            copy.wait()
        totals = [buf[turn, q] for q in range(count)]
        while len(totals) > 1:
            totals = [totals[i] + totals[i + 1] for i in range(0, len(totals), 2)]
        return totals[0]

    def everywhere(part, turn):
        return exchange(exchange(part, abuf, turn, within, 8, near, a_s, a_r), bbuf, turn, plane * 4 + feat, 16, far, b_s, b_r)

    def product(stacked, high, low, dims):
        total = lax.dot_general(stacked, high, dims, preferred_element_type=jnp.float32)
        total = total + lax.dot_general(stacked, low, dims, preferred_element_type=jnp.float32)
        return jnp.sum(total, axis=0, keepdims=True)

    def solve(row):
        rest = [row[:, 512 * a : 512 * a + 512] for a in range(4)]
        for a in range(4):
            rest[a] = product(pair(rest[a]), inv_hi[a], inv_lo[a], NT)
            stacked = pair(rest[a])
            for b in range(a + 1, 4):
                at = place(a, b)
                rest[b] = rest[b] - product(stacked, up_hi[at], up_lo[at], NN)
        for a in range(3, -1, -1):
            rest[a] = product(pair(rest[a]), inv_hi[a], inv_lo[a], NN)
            stacked = pair(rest[a])
            for b in range(a):
                at = place(b, a)
                rest[b] = rest[b] - product(stacked, up_hi[at], up_lo[at], NT)
        return jnp.concatenate(rest, axis=1)

    def dot(left, right):
        return jnp.sum(left * right, axis=1, keepdims=True)

    wide[...] = jnp.zeros((1, D), jnp.float32)
    wide[:, columns(0)] = grad[...] * (1.0 / total_rows) + weights[...] * (ridge / 32)
    residual = -everywhere(wide[...], 0)

    def step(number, carry):
        answer, residual, direction, inner = carry
        solved = solve(residual)
        inner_now = dot(residual, solved)
        direction = solved + jnp.where(number == 0, 0.0, inner_now / inner) * direction
        full[...] = direction
        row_sums = jnp.zeros((16, 512), jnp.float32)
        for o in range(4):
            row_sums = row_sums + lax.dot_general(pieces(full[:, columns(o)]), blocks[o][...], NT, preferred_element_type=jnp.float32)
        stacked = pieces(jnp.sum(row_sums, axis=0, keepdims=True))
        for o in range(4):
            part = lax.dot_general(stacked, blocks[o][...], NN, preferred_element_type=jnp.float32)
            wide[:, columns(o)] = jnp.sum(part, axis=0, keepdims=True)
        curved = everywhere(wide[...], number + 1) * (1.0 / total_rows) + ridge * direction
        step_size = inner_now / dot(direction, curved)
        return answer + step_size * direction, residual - step_size * curved, direction, inner_now

    zero = jnp.zeros((1, D), jnp.float32)
    answer = lax.fori_loop(0, ITERS, step, (zero, residual, zero, jnp.ones((1, 1), jnp.float32)))[0]
    scale = jnp.minimum(1.0, radius[...] * math.sqrt(D) / jnp.sqrt(dot(answer, answer) + 1e-06))
    full[...] = answer
    out[...] = weights[...] + scale * full[:, columns(0)]


def pcg(total_rows, blocks, grad, factors, weights, radius):
    vm = pl.BlockSpec(memory_space=pltpu.VMEM)
    dma = pltpu.SemaphoreType.DMA
    return pl.pallas_call(
        lambda *refs: pcg_kernel(total_rows, *refs),
        out_shape=jax.ShapeDtypeStruct((1, 512), jnp.float32),
        in_specs=[vm] * 11,
        out_specs=vm,
        scratch_shapes=[
            pltpu.VMEM((1, D), jnp.float32),
            pltpu.VMEM((1, D), jnp.float32),
            pltpu.VMEM((5, 8, 1, D), jnp.float32),
            pltpu.VMEM((5, 16, 1, D), jnp.float32),
            dma((5, 8)),
            dma((5, 8)),
            dma((5, 16)),
            dma((5, 16)),
        ],
        compiler_params=pltpu.CompilerParams(vmem_limit_bytes=32 * 2**20, collective_id=0, has_side_effects=True),
        name="pcg",
    )(*blocks, grad, *factors, weights, radius)


def sketch_kernel(scale, signed, coarse, fine, left, right, send, keep, arrive, narrow, xin, yin, stage, xlast, ylast, mine, ssem, rsem, lsem):
    ex = lax.axis_index("ex")
    z = lax.axis_index("feat")
    y, x, c = ex // 8, (ex // 2) % 4, ex % 2

    def to_x(o):
        return ((y * 4 + (x + o) % 4) * 2 + c, z)

    def to_y(o):
        return ((((y + o) % 4) * 4 + x) * 2 + c, z)

    def to_z(o):
        return (ex, (z + o) % 4)

    other = (ex + 1 - 2 * c, z)
    barrier = pltpu.get_barrier_semaphore()
    for o in range(1, 4):
        for peer in (to_x, to_y, to_z):
            pl.semaphore_signal(barrier, inc=1, device_id=peer(o), device_id_type=MESH)
    pl.semaphore_signal(barrier, inc=1, device_id=other, device_id_type=MESH)

    started = []

    def ship(src, dst, device):
        at = len(started)
        copy = pltpu.make_async_remote_copy(
            src_ref=src, dst_ref=dst, send_sem=ssem.at[at], recv_sem=rsem.at[at], device_id=device, device_id_type=MESH
        )
        copy.start()
        started.append(copy)
        return copy

    def mixed(row):
        rows = pl.ds(pl.multiple_of(row, 256), 256)
        fine_rows = fine[rows, :]
        pattern = jnp.concatenate([fine_rows * jnp.broadcast_to(coarse[rows, h : h + 1], (256, 128)) for h in range(16)], axis=1)
        return jnp.dot(pattern, signed[...], preferred_element_type=jnp.float32)

    halves = []
    for q in range(4):
        send[q] = mixed((1 - c) * 1024 + 256 * q)
        if q == 0:
            pl.semaphore_wait(barrier, 10)
        halves.append(ship(send.at[q], arrive.at[q], other))
    for q in range(4):
        keep[q] = mixed(c * 1024 + 256 * q)
    for q in range(4):
        halves[q].wait_recv()
        total = keep[q] + arrive[q]
        keep[q] = total
        narrow[0, q] = total[:, :256].astype(jnp.bfloat16)
        narrow[1, q] = total[:, 256:].astype(jnp.bfloat16)
    first = []
    for o in range(1, 4):
        first.append(ship(narrow.at[0, (x + o) % 4], xin.at[o - 1], to_x(o)))
        first.append(ship(narrow.at[1, (y + o) % 4], yin.at[o - 1], to_y(o)))
    for copy in first:
        copy.wait_recv()
    left_total = keep[x, :, :256]
    right_total = keep[y, :, 256:]
    for o in range(3):
        left_total = left_total + xin[o].astype(jnp.float32)
        right_total = right_total + yin[o].astype(jnp.float32)
    for q in range(4):
        stage[0, q] = left_total[64 * q : 64 * q + 64, :]
        stage[1, q] = right_total[64 * q : 64 * q + 64, :]
    second = []
    for o in range(1, 4):
        second.append(ship(stage.at[0, (y + o) % 4], ylast.at[o - 1], to_y(o)))
        second.append(ship(stage.at[1, (x + o) % 4], xlast.at[o - 1], to_x(o)))
    for copy in second:
        copy.wait_recv()
    mine[0] = ((stage[0, y] + ylast[0] + ylast[1] + ylast[2]) * scale).astype(jnp.bfloat16)
    mine[1] = ((stage[1, x] + xlast[0] + xlast[1] + xlast[2]) * scale).astype(jnp.bfloat16)

    cols = pl.ds(pl.multiple_of(z * 256, 256), 256)
    big, small = pl.ds(0, 48), pl.ds(48, 16)
    every = pl.ds(0, 4)
    own_left = pltpu.make_async_copy(mine.at[0], left.at[c, x, y, :, cols], lsem.at[0])
    own_right = pltpu.make_async_copy(mine.at[1], right.at[c, y, x, :, cols], lsem.at[1])
    own_left.start()
    own_right.start()

    def pass_on(work):
        copies = []
        for o in range(1, 4):
            for src, dst, peer in work:
                copies.append(ship(src, dst, peer(o)))
        return copies

    def same(ref, peer):
        return (ref, ref, peer)

    here_left, here_right = left.at[c, x, y], right.at[c, y, x]
    copies = pass_on(
        [
            (mine.at[0, big], left.at[c, x, y, big, cols], to_z),
            (mine.at[1, big], right.at[c, y, x, big, cols], to_z),
            (mine.at[0, small], left.at[c, x, y, small, cols], to_y),
            (mine.at[1, small], right.at[c, y, x, small, cols], to_x),
        ]
    )
    own_left.wait()
    own_right.wait()
    for copy in copies:
        copy.wait_recv()
    copies = pass_on(
        [
            same(left.at[c, x, y, big, :], to_y),
            same(right.at[c, y, x, big, :], to_x),
            same(left.at[c, x, every, small, cols], to_x),
            same(right.at[c, y, every, small, cols], to_y),
        ]
    )
    for copy in copies:
        copy.wait_recv()
    copies = pass_on(
        [
            same(left.at[c, x, every, big, :], to_x),
            same(right.at[c, y, every, big, :], to_y),
            same(left.at[c, every, every, small, cols], to_z),
            same(right.at[c, every, every, small, cols], to_z),
        ]
    )
    across = []
    for o in range(4):
        if o > 0:
            for copy in copies[4 * o - 4 : 4 * o]:
                copy.wait_recv()
        from_x, from_y = (x + 4 - o) % 4, (y + 4 - o) % 4
        from_z = pl.ds(pl.multiple_of(((z + 4 - o) % 4) * 256, 256), 256)
        for ref in (
            left.at[c, from_x, every, big, :],
            right.at[c, from_y, every, big, :],
            left.at[c, every, every, small, from_z],
            right.at[c, every, every, small, from_z],
        ):
            across.append(ship(ref, ref, other))
    for copy in across:
        copy.wait_recv()
    for copy in started:
        copy.wait_send()


def sketch_rows(scale, signed, coarse, fine):
    vm = pl.BlockSpec(memory_space=pltpu.VMEM)
    anywhere = pl.BlockSpec(memory_space=pl.ANY)
    f32, bf16 = jnp.float32, jnp.bfloat16
    half = jax.ShapeDtypeStruct((2, 4, 4, 64, D // 2), bf16)
    left, right = pl.pallas_call(
        lambda *refs: sketch_kernel(scale, *refs),
        out_shape=(half, half),
        in_specs=[vm] * 3,
        out_specs=(anywhere, anywhere),
        scratch_shapes=[
            pltpu.VMEM((4, 256, 512), f32),
            pltpu.VMEM((4, 256, 512), f32),
            pltpu.VMEM((4, 256, 512), f32),
            pltpu.VMEM((2, 4, 256, 256), bf16),
            pltpu.VMEM((3, 256, 256), bf16),
            pltpu.VMEM((3, 256, 256), bf16),
            pltpu.VMEM((2, 4, 64, 256), f32),
            pltpu.VMEM((3, 64, 256), f32),
            pltpu.VMEM((3, 64, 256), f32),
            pltpu.VMEM((2, 64, 256), bf16),
            pltpu.SemaphoreType.DMA((72,)),
            pltpu.SemaphoreType.DMA((72,)),
            pltpu.SemaphoreType.DMA((2,)),
        ],
        compiler_params=pltpu.CompilerParams(vmem_limit_bytes=32 * 2**20, collective_id=1, has_side_effects=True),
        name="sketch",
    )(signed, coarse, fine)
    return left.reshape(D, D // 2), right.reshape(D, D // 2)


def parity(common):
    for shift in (8, 4, 2, 1):
        common = common ^ (common >> shift)
    return 1 - 2 * (common & 1)


def local(features, weights, labels, signs, samples, radius):
    row_count, feat_width = features.shape
    ex_count = lax.axis_size("ex")
    ex_index = lax.axis_index("ex")
    total_rows = row_count * ex_count
    sample_count = samples.shape[0]
    dense = features.astype(jnp.float32)
    margins = lax.psum(jnp.dot(dense, weights, precision=HI), "feat")
    probability = 1.0 / (1.0 + jnp.exp(-margins))
    curvature = probability * (1.0 - probability)
    grad_part = jnp.dot(probability - labels.astype(jnp.float32), dense, precision=HI)
    weighted = (jnp.sqrt(curvature)[:, None] * dense).astype(jnp.bfloat16)
    signed = weighted * signs.astype(jnp.bfloat16)[:, None]
    low, high = samples % row_count, samples // row_count
    coarse = parity((low[:, None] // 128) & lax.iota(jnp.int32, row_count // 128)[None, :])
    coarse = coarse * parity(high & ex_index)[:, None]
    fine = parity((low[:, None] % 128) & lax.iota(jnp.int32, 128)[None, :])
    scale = 1.0 / math.sqrt(total_rows * sample_count)
    left, right = sketch_rows(scale, signed, coarse.astype(jnp.bfloat16), fine.astype(jnp.bfloat16))
    factors = factor(left, right)
    feat_index = lax.axis_index("feat")
    part = row_count // 4
    blocks = []
    for o in range(4):
        rows = lax.dynamic_slice_in_dim(weighted, ((feat_index + o) % 4) * part, part, 0)
        blocks.append(lax.ppermute(rows, "feat", [(i, (i + o) % 4) for i in range(4)]) if o else rows)
    out = pcg(total_rows, blocks, grad_part[None, :], factors, weights[None, :], radius[None, :])
    return out[0]


def solution(mesh):
    in_specs = (P("ex", "feat"), P("feat"), P("ex"), P("ex"), P(), P())
    return jax.shard_map(local, mesh=mesh, in_specs=in_specs, out_specs=P("feat"), check_vma=False)
```

```python
import math

import jax
import jax.numpy as jnp
from jax import lax
from jax.experimental import pallas as pl
from jax.experimental.pallas import tpu as pltpu
from jax.sharding import PartitionSpec as P

D = 2048
ITERS = 4
REG = 0.02
HI = lax.Precision.HIGHEST
NN = (((1,), (0,)), ((), ()))
NT = (((1,), (1,)), ((), ()))
TN = (((0,), (0,)), ((), ()))
MESH = pl.DeviceIdType.MESH

def split2(value):
    high = value.astype(jnp.bfloat16)
    return high, (value - high.astype(jnp.float32)).astype(jnp.bfloat16)


def block_inverse(block):
    lanes = lax.broadcasted_iota(jnp.int32, (1, 128), 1)
    subs = lax.broadcasted_iota(jnp.int32, (8, 128), 0)
    tiles = [block[8 * t : 8 * t + 8, :] for t in range(16)]

    def lane(t, at):
        return jnp.broadcast_to(tiles[t][:, at : at + 1], (8, 128))

    def sub(tile, at):
        return jnp.broadcast_to(tile[at : at + 1, :], (8, 128))

    own = [lane(0, j) for j in range(8)]
    nxt = [lane(1, j) for j in range(8)]
    for g in range(16):
        base = 8 * g
        more, most = g + 1 < 16, g + 2 < 16
        if more:
            own_later = [lane(g + 1, base + 8 + j) for j in range(8)]
        if most:
            nxt_later = [lane(g + 2, base + 8 + j) for j in range(8)]
            second = [lane(g + 2, base + j) for j in range(8)]
        inverses, crosses, rows = [], {}, []
        head = tiles[g]
        nxt_scaled, second_scaled = [], []
        for j in range(8):
            inverse = 1.0 / sub(own[j], j)
            inverses.append(inverse)
            scaled = jnp.where(subs > j, own[j] * inverse, 0.0)
            if more:
                nxt_scaled.append(nxt[j] * inverse)
            if most:
                second_scaled.append(second[j] * inverse)
            for i in range(j + 1, 8):
                cross = sub(own[i], j)
                crosses[j, i] = cross
                own[i] = own[i] - scaled * cross
                if more:
                    nxt[i] = nxt[i] - nxt_scaled[j] * cross
                if most:
                    second[i] = second[i] - second_scaled[j] * cross
            if more:
                for i in range(8):
                    cross = sub(nxt[j], i)
                    own_later[i] = own_later[i] - nxt_scaled[j] * cross
                    if most:
                        nxt_later[i] = nxt_later[i] - second_scaled[j] * cross
            row = head[j : j + 1, :]
            row = jnp.broadcast_to(jnp.where(lanes == base + j, row + row, row), (8, 128))
            rows.append(row)
            head = head - scaled * row
        tiles[g] = head
        for t in range(g + 1, 16):
            if t == g + 1:
                scaled = nxt_scaled
            elif t == g + 2:
                scaled = second_scaled
            else:
                column = [lane(t, base + j) for j in range(8)]
                scaled = []
                for j in range(8):
                    scaled.append(column[j] * inverses[j])
                    for i in range(j + 1, 8):
                        column[i] = column[i] - scaled[j] * crosses[j, i]
            tile = tiles[t]
            for j in range(8):
                tile = tile - scaled[j] * rows[j]
            tiles[t] = tile
        if more:
            own = own_later
        if most:
            nxt = nxt_later
    whole = jnp.concatenate(tiles, axis=0)
    rows = lax.broadcasted_iota(jnp.int32, (128, 128), 0)
    cols = lax.broadcasted_iota(jnp.int32, (128, 128), 1)
    diagonal = jnp.where(rows == cols, whole, 0.0)
    along_rows = jnp.sum(diagonal, axis=0, keepdims=True)
    along_cols = jnp.sum(diagonal, axis=1, keepdims=True)
    lower = jnp.where(cols <= rows, whole, 0.0)
    return lower * (1.0 / along_rows) * (1.0 / jnp.sqrt(along_cols))


def factor_kernel(left, right, up_hi, up_lo, inv_hi, inv_lo, gram, invs, crosses, corner, trio_l, trio_r):
    ridge = REG / D
    halves = (left, right)
    for a in range(4):
        for b in range(a, 4):
            for h in range(2):
                for side in range(h if a == b else 0, 2):
                    part = lax.dot_general(
                        halves[h][:, 256 * a : 256 * a + 256],
                        halves[side][:, 256 * b : 256 * b + 256],
                        TN,
                        preferred_element_type=jnp.float32,
                    )
                    if a == b and h == side:
                        rows = lax.broadcasted_iota(jnp.int32, (256, 256), 0)
                        cols = lax.broadcasted_iota(jnp.int32, (256, 256), 1)
                        part = part + jnp.where(rows == cols, ridge, 0.0)
                    gram[512 * a + 256 * h : 512 * a + 256 * h + 256, 512 * b + 256 * side : 512 * b + 256 * side + 256] = part
                    if a == b and h < side:
                        gram[512 * a + 256 : 512 * a + 512, 512 * a : 512 * a + 256] = jnp.zeros((256, 256), jnp.float32)

    def join(top, bottom, cross):
        middle = lax.dot_general(cross, top, TN, precision=HI, preferred_element_type=jnp.float32)
        edge = -lax.dot_general(bottom, middle, NN, precision=HI, preferred_element_type=jnp.float32)
        zero = jnp.zeros_like(top)
        return jnp.concatenate([jnp.concatenate([top, zero], axis=1), jnp.concatenate([edge, bottom], axis=1)], axis=0)

    def step(s, carry):
        at = pl.multiple_of(s * 256, 256)
        next_at = pl.multiple_of(at + 128, 128)
        rows = pl.ds(at, 256)
        first = s // 2
        upper, lower = pl.ds(at, 128), pl.ds(next_at, 128)
        corner[0] = gram[upper, upper]

        def one(h, carry):
            corner[2 + h] = block_inverse(corner[h])

            if h == 0:
                cross = lax.dot_general(corner[2], gram[upper, lower], NN, precision=HI, preferred_element_type=jnp.float32)
                corner[4] = cross
                corner[1] = gram[lower, lower] - lax.dot_general(cross, cross, TN, precision=HI, preferred_element_type=jnp.float32)

            return carry

        one(0, 0)
        one(1, 0)
        inverse = join(corner[2], corner[3], corner[4])
        invs[s] = inverse
        ih, il = split2(inverse)
        ileft = jnp.concatenate([ih, ih, il], axis=1)
        half = pl.ds(pl.multiple_of((s % 2) * 256, 256), 256)
        for c in range(4):

            @pl.when(c >= (s + 1) // 2)
            def _():
                cs = slice(512 * c, 512 * c + 512)
                gh, gl = split2(gram[rows, cs])
                panel = lax.dot_general(ileft, jnp.concatenate([gh, gl, gh], axis=0), NN, preferred_element_type=jnp.float32)
                cols = lax.broadcasted_iota(jnp.int32, (256, 512), 1) + 512 * c
                panel = jnp.where(cols >= at + 256, panel, 0.0)
                ph, plo = split2(panel)
                trio_r[0:256, cs] = ph
                trio_r[256:512, cs] = plo
                trio_r[512:768, cs] = ph
                trio_l[0:256, cs] = ph
                trio_l[256:512, cs] = ph
                trio_l[512:768, cs] = plo

                @pl.when(c == first)
                def _():
                    crosses[first] = panel[:, 256:]

                @pl.when(c > first)
                def _():
                    block = first * (7 - first) // 2 + c - first - 1
                    up_hi[block, half, :] = ph
                    up_lo[block, half, :] = plo

        def across(a, carry):
            ra = pl.ds(pl.multiple_of(a * 512, 512), 512)

            def along(b, carry):
                cs = pl.ds(pl.multiple_of(b * 512, 512), 512)
                gram[ra, cs] = gram[ra, cs] - lax.dot_general(trio_l[:, ra], trio_r[:, cs], TN, preferred_element_type=jnp.float32)
                return carry

            return lax.fori_loop(a, 4, along, carry)

        lax.fori_loop((s + 1) // 2, 4, across, 0)
        return carry

    lax.fori_loop(0, 8, step, 0)

    def chunk(a, carry):
        hi, lo = split2(join(invs[2 * a], invs[2 * a + 1], crosses[a]))
        inv_hi[a] = hi
        inv_lo[a] = lo
        return carry

    lax.fori_loop(0, 4, chunk, 0)


def factor(left, right):
    vm = pl.BlockSpec(memory_space=pltpu.VMEM)
    ups = jax.ShapeDtypeStruct((6, 512, 512), jnp.bfloat16)
    inverses = jax.ShapeDtypeStruct((4, 512, 512), jnp.bfloat16)
    return pl.pallas_call(
        factor_kernel,
        out_shape=(ups, ups, inverses, inverses),
        in_specs=[vm, vm],
        out_specs=(vm, vm, vm, vm),
        scratch_shapes=[
            pltpu.VMEM((D, D), jnp.float32),
            pltpu.VMEM((8, 256, 256), jnp.float32),
            pltpu.VMEM((4, 256, 256), jnp.float32),
            pltpu.VMEM((5, 128, 128), jnp.float32),
            pltpu.VMEM((768, D), jnp.bfloat16),
            pltpu.VMEM((768, D), jnp.bfloat16),
        ],
        compiler_params=pltpu.CompilerParams(vmem_limit_bytes=30 * 2**20),
        cost_estimate=pl.CostEstimate(flops=60 * 10**9, bytes_accessed=18 * 2**20, transcendentals=0),
        name="factor",
    )(left, right)


def pieces(row):
    first = row.astype(jnp.bfloat16).astype(jnp.float32)
    rest = row - first
    second = rest.astype(jnp.bfloat16).astype(jnp.float32)
    third = rest - second
    which = lax.broadcasted_iota(jnp.int32, (16, row.shape[1]), 0)
    stacked = jnp.where(which == 0, first, jnp.where(which == 1, second, jnp.where(which == 2, third, 0.0)))
    return stacked.astype(jnp.bfloat16)


def pair(row):
    first = row.astype(jnp.bfloat16).astype(jnp.float32)
    which = lax.broadcasted_iota(jnp.int32, (16, row.shape[1]), 0)
    return jnp.where(which == 0, first, jnp.where(which == 1, row - first, 0.0)).astype(jnp.bfloat16)


def place(a, b):
    return a * (7 - a) // 2 + b - a - 1


def pcg_kernel(total_rows, blocks, start, up_hi, up_lo, inv_hi, inv_lo, weights, radius, out, full, wide, abuf, bbuf, a_s, a_r, b_s, b_r):
    ex = lax.axis_index("ex")
    feat = lax.axis_index("feat")
    plane, within = ex // 8, ex % 8
    ridge = REG / D

    def columns(o):
        return pl.ds(pl.multiple_of(((feat + 4 - o) % 4) * 512, 512), 512)

    def near(o):
        return (plane * 8 + (within + o) % 8, feat)

    def far(o):
        other = (plane * 4 + feat + o) % 16
        return ((other // 4) * 8 + within, other % 4)

    barrier = pltpu.get_barrier_semaphore()
    for o in range(1, 8):
        pl.semaphore_signal(barrier, inc=1, device_id=near(o), device_id_type=MESH)
    for o in range(1, 16):
        pl.semaphore_signal(barrier, inc=1, device_id=far(o), device_id_type=MESH)
    pl.semaphore_wait(barrier, 22)

    def exchange(value, buf, turn, me, count, peer, send, recv):
        buf[turn, me] = value
        copies = [
            pltpu.make_async_remote_copy(
                src_ref=buf.at[turn, me],
                dst_ref=buf.at[turn, me],
                send_sem=send.at[turn, o],
                recv_sem=recv.at[turn, o],
                device_id=peer(o),
                device_id_type=MESH,
            )
            for o in range(1, count)
        ]
        for copy in copies:
            copy.start()
        for copy in copies:
            copy.wait()
        totals = [buf[turn, q] for q in range(count)]
        while len(totals) > 1:
            totals = [totals[i] + totals[i + 1] for i in range(0, len(totals), 2)]
        return totals[0]

    def everywhere(part, turn):
        return exchange(exchange(part, abuf, turn, within, 8, near, a_s, a_r), bbuf, turn, plane * 4 + feat, 16, far, b_s, b_r)

    def product(stacked, high, low, dims):
        total = lax.dot_general(stacked, high, dims, preferred_element_type=jnp.float32)
        total = total + lax.dot_general(stacked, low, dims, preferred_element_type=jnp.float32)
        return jnp.sum(total, axis=0, keepdims=True)

    def solve(row):
        rest = [row[:, 512 * a : 512 * a + 512] for a in range(4)]
        for a in range(4):
            rest[a] = product(pair(rest[a]), inv_hi[a], inv_lo[a], NT)
            stacked = pair(rest[a])
            for b in range(a + 1, 4):
                at = place(a, b)
                rest[b] = rest[b] - product(stacked, up_hi[at], up_lo[at], NN)
        for a in range(3, -1, -1):
            rest[a] = product(pair(rest[a]), inv_hi[a], inv_lo[a], NN)
            stacked = pair(rest[a])
            for b in range(a):
                at = place(b, a)
                rest[b] = rest[b] - product(stacked, up_hi[at], up_lo[at], NT)
        return jnp.concatenate(rest, axis=1)

    def dot(left, right):
        return jnp.sum(left * right, axis=1, keepdims=True)

    residual = start[...]

    def step(number, carry):
        answer, residual, direction, inner = carry
        solved = solve(residual)
        inner_now = dot(residual, solved)
        direction = solved + jnp.where(number == 0, 0.0, inner_now / inner) * direction
        full[...] = direction
        row_sums = jnp.zeros((16, 512), jnp.float32)
        for o in range(4):
            row_sums = row_sums + lax.dot_general(pieces(full[:, columns(o)]), blocks[o], NT, preferred_element_type=jnp.float32)
        stacked = pieces(jnp.sum(row_sums, axis=0, keepdims=True))
        for o in range(4):
            part = lax.dot_general(stacked, blocks[o], NN, preferred_element_type=jnp.float32)
            wide[:, columns(o)] = jnp.sum(part, axis=0, keepdims=True)
        curved = everywhere(wide[...], number) * (1.0 / total_rows) + ridge * direction
        step_size = inner_now / dot(direction, curved)
        return answer + step_size * direction, residual - step_size * curved, direction, inner_now

    zero = jnp.zeros((1, D), jnp.float32)
    answer = lax.fori_loop(0, ITERS, step, (zero, residual, zero, jnp.ones((1, 1), jnp.float32)))[0]
    scale = jnp.minimum(1.0, radius[...] * math.sqrt(D) / jnp.sqrt(dot(answer, answer) + 1e-06))
    full[...] = answer
    out[...] = weights[...] + scale * full[:, columns(0)]


def pcg(total_rows, blocks, start, factors, weights, radius):
    vm = pl.BlockSpec(memory_space=pltpu.VMEM)
    dma = pltpu.SemaphoreType.DMA
    return pl.pallas_call(
        lambda *refs: pcg_kernel(total_rows, *refs),
        out_shape=jax.ShapeDtypeStruct((1, 512), jnp.float32),
        in_specs=[vm] * 8,
        out_specs=vm,
        scratch_shapes=[
            pltpu.VMEM((1, D), jnp.float32),
            pltpu.VMEM((1, D), jnp.float32),
            pltpu.VMEM((4, 8, 1, D), jnp.float32),
            pltpu.VMEM((4, 16, 1, D), jnp.float32),
            dma((4, 8)),
            dma((4, 8)),
            dma((4, 16)),
            dma((4, 16)),
        ],
        compiler_params=pltpu.CompilerParams(vmem_limit_bytes=32 * 2**20, collective_id=0, has_side_effects=True),
        name="pcg",
    )(blocks, start, *factors, weights, radius)


def row_times(row, matrix, dims):
    return jnp.sum(lax.dot_general(pieces(row), matrix, dims, preferred_element_type=jnp.float32), axis=0, keepdims=True)

def sketch_kernel(
    scale, total_rows, features, weights, labels, signs, coarse, fine,
    left, right, residual, blocks,
    send, keep, arrive, narrow, xin, yin, stage, xlast, ylast, mine, pattern, weighted, wide, zbuf, abuf, bbuf, ssem, rsem, lsem,
):
    ex = lax.axis_index("ex")
    z = lax.axis_index("feat")
    y, x, c = ex // 8, (ex // 2) % 4, ex % 2

    def to_x(o):
        return ((y * 4 + (x + o) % 4) * 2 + c, z)

    def to_y(o):
        return ((((y + o) % 4) * 4 + x) * 2 + c, z)

    def to_z(o):
        return (ex, (z + o) % 4)

    other = (ex + 1 - 2 * c, z)
    within = ex % 8

    def near(o):
        return (y * 8 + (within + o) % 8, z)

    def far(o):
        to = (y * 4 + z + o) % 16
        return ((to // 4) * 8 + within, to % 4)

    barrier = pltpu.get_barrier_semaphore()
    for o in range(1, 8):
        pl.semaphore_signal(barrier, inc=1, device_id=near(o), device_id_type=MESH)
    for o in range(1, 16):
        pl.semaphore_signal(barrier, inc=1, device_id=far(o), device_id_type=MESH)

    started = []

    def ship(src, dst, device):
        at = len(started)
        copy = pltpu.make_async_remote_copy(
            src_ref=src, dst_ref=dst, send_sem=ssem.at[at], recv_sem=rsem.at[at], device_id=device, device_id_type=MESH
        )
        copy.start()
        started.append(copy)
        return copy

    def spread(buf, me, count, peer):
        return [ship(buf.at[me], buf.at[me], peer(o)) for o in range(1, count)]

    def gathered(copies, buf, count):
        for copy in copies:
            copy.wait_recv()
        totals = [buf[q] for q in range(count)]
        while len(totals) > 1:
            totals = [totals[i] + totals[i + 1] for i in range(0, len(totals), 2)]
        return totals[0]

    zbuf[z] = row_times(weights[...], features[...], NT)
    pl.semaphore_wait(barrier, 22)
    margin_copies = spread(zbuf, z, 4, to_z)
    sign_row = signs[...].astype(jnp.bfloat16)

    def patterns(q, carry):
        rows = pl.ds(pl.multiple_of(q * 256, 256), 256)
        fine_rows = fine[rows, :]
        for h in range(16):
            signed_rows = fine_rows * jnp.broadcast_to(sign_row[:, 128 * h : 128 * h + 128], (256, 128))
            pattern[rows, 128 * h : 128 * h + 128] = signed_rows * jnp.broadcast_to(coarse[rows, h : h + 1], (256, 128))
        return carry

    lax.fori_loop(0, 8, patterns, 0)
    margins = gathered(margin_copies, zbuf, 4)
    probability = 1.0 / (1.0 + jnp.exp(-margins))
    root = jnp.sqrt(probability * (1.0 - probability))
    for i in range(16):
        rows = slice(128 * i, 128 * i + 128)
        column = jnp.transpose(jnp.broadcast_to(root[:, rows], (128, 128)))
        for h in range(4):
            cols = slice(128 * h, 128 * h + 128)
            weighted[rows, cols] = (features[rows, cols].astype(jnp.float32) * column).astype(jnp.bfloat16)
    for o in range(1, 4):
        ship(weighted.at[pl.ds(pl.multiple_of(((z + o) % 4) * 512, 512), 512), :], blocks.at[o], to_z(o))
    kept = pltpu.make_async_copy(weighted.at[pl.ds(pl.multiple_of(z * 512, 512), 512), :], blocks.at[0], lsem.at[2])
    kept.start()
    redistributed = started[-3:]

    def mixed(row):
        rows = pl.ds(pl.multiple_of(row, 256), 256)
        return jnp.dot(pattern[rows, :], weighted[...], preferred_element_type=jnp.float32)

    halves = []
    for q in range(4):
        send[q] = mixed((1 - c) * 1024 + 256 * q)
        halves.append(ship(send.at[q], arrive.at[q], other))
    slope = row_times(probability - labels[...].astype(jnp.float32), features[...], NN)
    wide[...] = jnp.zeros((1, D), jnp.float32)
    wide[:, pl.ds(pl.multiple_of(z * 512, 512), 512)] = slope * (1.0 / total_rows) + weights[...] * (REG / D / 32)
    abuf[within] = wide[...]
    near_copies = spread(abuf, within, 8, near)
    for q in range(4):
        keep[q] = mixed(c * 1024 + 256 * q)
    for q in range(4):
        halves[q].wait_recv()
        total = keep[q] + arrive[q]
        keep[q] = total
        narrow[0, q] = total[:, :256].astype(jnp.bfloat16)
        narrow[1, q] = total[:, 256:].astype(jnp.bfloat16)
    first = []
    for o in range(1, 4):
        first.append(ship(narrow.at[0, (x + o) % 4], xin.at[o - 1], to_x(o)))
        first.append(ship(narrow.at[1, (y + o) % 4], yin.at[o - 1], to_y(o)))
    bbuf[y * 4 + z] = gathered(near_copies, abuf, 8)
    far_copies = spread(bbuf, y * 4 + z, 16, far)
    for copy in first:
        copy.wait_recv()
    left_total = keep[x, :, :256]
    right_total = keep[y, :, 256:]
    for o in range(3):
        left_total = left_total + xin[o].astype(jnp.float32)
        right_total = right_total + yin[o].astype(jnp.float32)
    for q in range(4):
        stage[0, q] = left_total[64 * q : 64 * q + 64, :]
        stage[1, q] = right_total[64 * q : 64 * q + 64, :]
    second = []
    for o in range(1, 4):
        second.append(ship(stage.at[0, (y + o) % 4], ylast.at[o - 1], to_y(o)))
        second.append(ship(stage.at[1, (x + o) % 4], xlast.at[o - 1], to_x(o)))
    for copy in second:
        copy.wait_recv()
    mine[0] = ((stage[0, y] + ylast[0] + ylast[1] + ylast[2]) * scale).astype(jnp.bfloat16)
    mine[1] = ((stage[1, x] + xlast[0] + xlast[1] + xlast[2]) * scale).astype(jnp.bfloat16)

    cols = pl.ds(pl.multiple_of(z * 256, 256), 256)
    big, small = pl.ds(0, 48), pl.ds(48, 16)
    every = pl.ds(0, 4)
    own_left = pltpu.make_async_copy(mine.at[0], left.at[c, x, y, :, cols], lsem.at[0])
    own_right = pltpu.make_async_copy(mine.at[1], right.at[c, y, x, :, cols], lsem.at[1])
    own_left.start()
    own_right.start()

    def pass_on(work):
        copies = []
        for o in range(1, 4):
            for src, dst, peer in work:
                copies.append(ship(src, dst, peer(o)))
        return copies

    def same(ref, peer):
        return (ref, ref, peer)

    here_left, here_right = left.at[c, x, y], right.at[c, y, x]
    copies = pass_on(
        [
            (mine.at[0, big], left.at[c, x, y, big, cols], to_z),
            (mine.at[1, big], right.at[c, y, x, big, cols], to_z),
            (mine.at[0, small], left.at[c, x, y, small, cols], to_y),
            (mine.at[1, small], right.at[c, y, x, small, cols], to_x),
        ]
    )
    own_left.wait()
    own_right.wait()
    for copy in copies:
        copy.wait_recv()
    copies = pass_on(
        [
            same(left.at[c, x, y, big, :], to_y),
            same(right.at[c, y, x, big, :], to_x),
            same(left.at[c, x, every, small, cols], to_x),
            same(right.at[c, y, every, small, cols], to_y),
        ]
    )
    for copy in copies:
        copy.wait_recv()
    copies = pass_on(
        [
            same(left.at[c, x, every, big, :], to_x),
            same(right.at[c, y, every, big, :], to_y),
            same(left.at[c, every, every, small, cols], to_z),
            same(right.at[c, every, every, small, cols], to_z),
        ]
    )
    across = []
    for o in range(4):
        if o > 0:
            for copy in copies[4 * o - 4 : 4 * o]:
                copy.wait_recv()
        from_x, from_y = (x + 4 - o) % 4, (y + 4 - o) % 4
        from_z = pl.ds(pl.multiple_of(((z + 4 - o) % 4) * 256, 256), 256)
        for ref in (
            left.at[c, from_x, every, big, :],
            right.at[c, from_y, every, big, :],
            left.at[c, every, every, small, from_z],
            right.at[c, every, every, small, from_z],
        ):
            across.append(ship(ref, ref, other))
    for copy in across:
        copy.wait_recv()
    residual[...] = -gathered(far_copies, bbuf, 16)
    for copy in redistributed:
        copy.wait_recv()
    kept.wait()
    for copy in started:
        copy.wait_send()


def sketch_rows(scale, total_rows, features, weights, labels, signs, coarse, fine):
    vm = pl.BlockSpec(memory_space=pltpu.VMEM)
    anywhere = pl.BlockSpec(memory_space=pl.ANY)
    f32, bf16 = jnp.float32, jnp.bfloat16
    half = jax.ShapeDtypeStruct((2, 4, 4, 64, D // 2), bf16)
    left, right, residual, blocks = pl.pallas_call(
        lambda *refs: sketch_kernel(scale, total_rows, *refs),
        out_shape=(half, half, jax.ShapeDtypeStruct((1, D), f32), jax.ShapeDtypeStruct((4, 512, 512), bf16)),
        in_specs=[vm] * 6,
        out_specs=(anywhere, anywhere, vm, anywhere),
        scratch_shapes=[
            pltpu.VMEM((4, 256, 512), f32),
            pltpu.VMEM((4, 256, 512), f32),
            pltpu.VMEM((4, 256, 512), f32),
            pltpu.VMEM((2, 4, 256, 256), bf16),
            pltpu.VMEM((3, 256, 256), bf16),
            pltpu.VMEM((3, 256, 256), bf16),
            pltpu.VMEM((2, 4, 64, 256), f32),
            pltpu.VMEM((3, 64, 256), f32),
            pltpu.VMEM((3, 64, 256), f32),
            pltpu.VMEM((2, 64, 256), bf16),
            pltpu.VMEM((D, 2048), bf16),
            pltpu.VMEM((2048, 512), bf16),
            pltpu.VMEM((1, D), f32),
            pltpu.VMEM((4, 1, 2048), f32),
            pltpu.VMEM((8, 1, D), f32),
            pltpu.VMEM((16, 1, D), f32),
            pltpu.SemaphoreType.DMA((112,)),
            pltpu.SemaphoreType.DMA((112,)),
            pltpu.SemaphoreType.DMA((3,)),
        ],
        compiler_params=pltpu.CompilerParams(vmem_limit_bytes=36 * 2**20, collective_id=1, has_side_effects=True),
        name="sketch",
    )(features, weights, labels, signs, coarse, fine)
    return left.reshape(D, D // 2), right.reshape(D, D // 2), residual, blocks


def parity(common):
    for shift in (8, 4, 2, 1):
        common = common ^ (common >> shift)
    return 1 - 2 * (common & 1)


def local(features, weights, labels, signs, samples, radius):
    row_count, feat_width = features.shape
    ex_count = lax.axis_size("ex")
    ex_index = lax.axis_index("ex")
    total_rows = row_count * ex_count
    sample_count = samples.shape[0]
    low, high = samples % row_count, samples // row_count
    coarse = parity((low[:, None] // 128) & lax.iota(jnp.int32, row_count // 128)[None, :])
    coarse = coarse * parity(high & ex_index)[:, None]
    fine = parity((low[:, None] % 128) & lax.iota(jnp.int32, 128)[None, :])
    scale = 1.0 / math.sqrt(total_rows * sample_count)
    left, right, residual, blocks = sketch_rows(
        scale,
        total_rows,
        features,
        weights[None, :],
        labels[None, :],
        signs[None, :],
        coarse.astype(jnp.bfloat16),
        fine.astype(jnp.bfloat16),
    )
    out = pcg(total_rows, blocks, residual, factor(left, right), weights[None, :], radius[None, :])
    return out[0]


def solution(mesh):
    in_specs = (P("ex", "feat"), P("feat"), P("ex"), P("ex"), P(), P())
    return jax.shard_map(local, mesh=mesh, in_specs=in_specs, out_specs=P("feat"), check_vma=False)
```

```python
import math

import jax
import jax.numpy as jnp
from jax import lax
from jax.experimental import pallas as pl
from jax.experimental.pallas import tpu as pltpu
from jax.sharding import PartitionSpec as P

D = 2048
ITERS = 4
REG = 0.02
HI = lax.Precision.HIGHEST
NN = (((1,), (0,)), ((), ()))
NT = (((1,), (1,)), ((), ()))
TN = (((0,), (0,)), ((), ()))
MESH = pl.DeviceIdType.MESH

def split2(value):
    high = value.astype(jnp.bfloat16)
    return high, (value - high.astype(jnp.float32)).astype(jnp.bfloat16)


def dot3(left, right, dims):
    (lc,), (rc,) = dims[0]
    lh, ll = split2(left)
    rh, rl = split2(right)
    left = jnp.concatenate([lh, lh, ll], axis=lc)
    right = jnp.concatenate([rh, rl, rh], axis=rc)
    return lax.dot_general(left, right, dims, preferred_element_type=jnp.float32)


def block_inverse(block):
    lanes = lax.broadcasted_iota(jnp.int32, (1, 128), 1)
    subs = lax.broadcasted_iota(jnp.int32, (8, 128), 0)
    tiles = [block[8 * t : 8 * t + 8, :] for t in range(16)]

    def lane(t, at):
        return jnp.broadcast_to(tiles[t][:, at : at + 1], (8, 128))

    def sub(tile, at):
        return jnp.broadcast_to(tile[at : at + 1, :], (8, 128))

    own = [lane(0, j) for j in range(8)]
    nxt = [lane(1, j) for j in range(8)]
    for g in range(16):
        base = 8 * g
        more, most = g + 1 < 16, g + 2 < 16
        if more:
            own_later = [lane(g + 1, base + 8 + j) for j in range(8)]
        if most:
            nxt_later = [lane(g + 2, base + 8 + j) for j in range(8)]
            second = [lane(g + 2, base + j) for j in range(8)]
        inverses, crosses, rows = [], {}, []
        head = tiles[g]
        nxt_scaled, second_scaled = [], []
        for j in range(8):
            inverse = 1.0 / sub(own[j], j)
            inverses.append(inverse)
            scaled = jnp.where(subs > j, own[j] * inverse, 0.0)
            if more:
                nxt_scaled.append(nxt[j] * inverse)
            if most:
                second_scaled.append(second[j] * inverse)
            for i in range(j + 1, 8):
                cross = sub(own[i], j)
                crosses[j, i] = cross
                own[i] = own[i] - scaled * cross
                if more:
                    nxt[i] = nxt[i] - nxt_scaled[j] * cross
                if most:
                    second[i] = second[i] - second_scaled[j] * cross
            if more:
                for i in range(8):
                    cross = sub(nxt[j], i)
                    own_later[i] = own_later[i] - nxt_scaled[j] * cross
                    if most:
                        nxt_later[i] = nxt_later[i] - second_scaled[j] * cross
            row = head[j : j + 1, :]
            row = jnp.broadcast_to(jnp.where(lanes == base + j, row + row, row), (8, 128))
            rows.append(row)
            head = head - scaled * row
        tiles[g] = head
        for t in range(g + 1, 16):
            if t == g + 1:
                scaled = nxt_scaled
            elif t == g + 2:
                scaled = second_scaled
            else:
                column = [lane(t, base + j) for j in range(8)]
                scaled = []
                for j in range(8):
                    scaled.append(column[j] * inverses[j])
                    for i in range(j + 1, 8):
                        column[i] = column[i] - scaled[j] * crosses[j, i]
            tile = tiles[t]
            for j in range(8):
                tile = tile - scaled[j] * rows[j]
            tiles[t] = tile
        if more:
            own = own_later
        if most:
            nxt = nxt_later
    whole = jnp.concatenate(tiles, axis=0)
    rows = lax.broadcasted_iota(jnp.int32, (128, 128), 0)
    cols = lax.broadcasted_iota(jnp.int32, (128, 128), 1)
    diagonal = jnp.where(rows == cols, whole, 0.0)
    along_rows = jnp.sum(diagonal, axis=0, keepdims=True)
    along_cols = jnp.sum(diagonal, axis=1, keepdims=True)
    lower = jnp.where(cols <= rows, whole, 0.0)
    return lower * (1.0 / along_rows) * (1.0 / jnp.sqrt(along_cols))


def factor_kernel(left, right, up_hi, up_lo, inv_hi, inv_lo, gram, invs, crosses, corner, trio_l, trio_r):
    ridge = REG / D
    halves = (left, right)
    for a in range(4):
        for b in range(a, 4):
            for h in range(2):
                for side in range(h if a == b else 0, 2):
                    part = lax.dot_general(
                        halves[h][:, 256 * a : 256 * a + 256],
                        halves[side][:, 256 * b : 256 * b + 256],
                        TN,
                        preferred_element_type=jnp.float32,
                    )
                    if a == b and h == side:
                        rows = lax.broadcasted_iota(jnp.int32, (256, 256), 0)
                        cols = lax.broadcasted_iota(jnp.int32, (256, 256), 1)
                        part = part + jnp.where(rows == cols, ridge, 0.0)
                    gram[512 * a + 256 * h : 512 * a + 256 * h + 256, 512 * b + 256 * side : 512 * b + 256 * side + 256] = part
                    if a == b and h < side:
                        gram[512 * a + 256 : 512 * a + 512, 512 * a : 512 * a + 256] = jnp.zeros((256, 256), jnp.float32)

    def join(top, bottom, cross):
        middle = dot3(cross, top, TN)
        edge = -dot3(bottom, middle, NN)
        zero = jnp.zeros_like(top)
        return jnp.concatenate([jnp.concatenate([top, zero], axis=1), jnp.concatenate([edge, bottom], axis=1)], axis=0)

    def step(s, carry):
        at = pl.multiple_of(s * 256, 256)
        next_at = pl.multiple_of(at + 128, 128)
        rows = pl.ds(at, 256)
        first = s // 2
        upper, lower = pl.ds(at, 128), pl.ds(next_at, 128)
        corner[0] = gram[upper, upper]

        def one(h, carry):
            corner[2 + h] = block_inverse(corner[h])

            if h == 0:
                cross = dot3(corner[2], gram[upper, lower], NN)
                corner[4] = cross
                corner[1] = gram[lower, lower] - dot3(cross, cross, TN)

            return carry

        one(0, 0)
        one(1, 0)
        inverse = join(corner[2], corner[3], corner[4])
        invs[s] = inverse
        ih, il = split2(inverse)
        ileft = jnp.concatenate([ih, ih, il], axis=1)
        half = pl.ds(pl.multiple_of((s % 2) * 256, 256), 256)
        for c in range(4):

            @pl.when(c >= (s + 1) // 2)
            def _():
                cs = slice(512 * c, 512 * c + 512)
                gh, gl = split2(gram[rows, cs])
                panel = lax.dot_general(ileft, jnp.concatenate([gh, gl, gh], axis=0), NN, preferred_element_type=jnp.float32)
                cols = lax.broadcasted_iota(jnp.int32, (256, 512), 1) + 512 * c
                panel = jnp.where(cols >= at + 256, panel, 0.0)
                ph, plo = split2(panel)
                trio_r[0:256, cs] = ph
                trio_r[256:512, cs] = plo
                trio_r[512:768, cs] = ph
                trio_l[0:256, cs] = ph
                trio_l[256:512, cs] = ph
                trio_l[512:768, cs] = plo

                @pl.when(c == first)
                def _():
                    crosses[first] = panel[:, 256:]

                @pl.when(c > first)
                def _():
                    block = first * (7 - first) // 2 + c - first - 1
                    up_hi[block, half, :] = ph
                    up_lo[block, half, :] = plo

        def across(a, carry):
            ra = pl.ds(pl.multiple_of(a * 512, 512), 512)

            def along(b, carry):
                cs = pl.ds(pl.multiple_of(b * 512, 512), 512)
                gram[ra, cs] = gram[ra, cs] - lax.dot_general(trio_l[:, ra], trio_r[:, cs], TN, preferred_element_type=jnp.float32)
                return carry

            return lax.fori_loop(a, 4, along, carry)

        lax.fori_loop((s + 1) // 2, 4, across, 0)
        return carry

    lax.fori_loop(0, 8, step, 0)

    def chunk(a, carry):
        hi, lo = split2(join(invs[2 * a], invs[2 * a + 1], crosses[a]))
        inv_hi[a] = hi
        inv_lo[a] = lo
        return carry

    lax.fori_loop(0, 4, chunk, 0)


def factor(left, right):
    vm = pl.BlockSpec(memory_space=pltpu.VMEM)
    ups = jax.ShapeDtypeStruct((6, 512, 512), jnp.bfloat16)
    inverses = jax.ShapeDtypeStruct((4, 512, 512), jnp.bfloat16)
    return pl.pallas_call(
        factor_kernel,
        out_shape=(ups, ups, inverses, inverses),
        in_specs=[vm, vm],
        out_specs=(vm, vm, vm, vm),
        scratch_shapes=[
            pltpu.VMEM((D, D), jnp.float32),
            pltpu.VMEM((8, 256, 256), jnp.float32),
            pltpu.VMEM((4, 256, 256), jnp.float32),
            pltpu.VMEM((5, 128, 128), jnp.float32),
            pltpu.VMEM((768, D), jnp.bfloat16),
            pltpu.VMEM((768, D), jnp.bfloat16),
        ],
        compiler_params=pltpu.CompilerParams(vmem_limit_bytes=30 * 2**20),
        cost_estimate=pl.CostEstimate(flops=60 * 10**9, bytes_accessed=18 * 2**20, transcendentals=0),
        name="factor",
    )(left, right)


def pieces(row):
    first = row.astype(jnp.bfloat16).astype(jnp.float32)
    rest = row - first
    second = rest.astype(jnp.bfloat16).astype(jnp.float32)
    third = rest - second
    which = lax.broadcasted_iota(jnp.int32, (16, row.shape[1]), 0)
    stacked = jnp.where(which == 0, first, jnp.where(which == 1, second, jnp.where(which == 2, third, 0.0)))
    return stacked.astype(jnp.bfloat16)


def pair(row):
    first = row.astype(jnp.bfloat16).astype(jnp.float32)
    which = lax.broadcasted_iota(jnp.int32, (16, row.shape[1]), 0)
    return jnp.where(which == 0, first, jnp.where(which == 1, row - first, 0.0)).astype(jnp.bfloat16)


def place(a, b):
    return a * (7 - a) // 2 + b - a - 1


def pcg_kernel(total_rows, blocks, start, up_hi, up_lo, inv_hi, inv_lo, weights, radius, out, full, wide, abuf, bbuf, a_s, a_r, b_s, b_r):
    ex = lax.axis_index("ex")
    feat = lax.axis_index("feat")
    plane, within = ex // 8, ex % 8
    ridge = REG / D

    def columns(o):
        return pl.ds(pl.multiple_of(((feat + 4 - o) % 4) * 512, 512), 512)

    def near(o):
        return (plane * 8 + (within + o) % 8, feat)

    def far(o):
        other = (plane * 4 + feat + o) % 16
        return ((other // 4) * 8 + within, other % 4)

    barrier = pltpu.get_barrier_semaphore()
    for o in range(1, 8):
        pl.semaphore_signal(barrier, inc=1, device_id=near(o), device_id_type=MESH)
    for o in range(1, 16):
        pl.semaphore_signal(barrier, inc=1, device_id=far(o), device_id_type=MESH)
    pl.semaphore_wait(barrier, 22)

    def exchange(value, buf, turn, me, count, peer, send, recv):
        buf[turn, me] = value
        copies = [
            pltpu.make_async_remote_copy(
                src_ref=buf.at[turn, me],
                dst_ref=buf.at[turn, me],
                send_sem=send.at[turn, o],
                recv_sem=recv.at[turn, o],
                device_id=peer(o),
                device_id_type=MESH,
            )
            for o in range(1, count)
        ]
        for copy in copies:
            copy.start()
        for copy in copies:
            copy.wait()
        totals = [buf[turn, q] for q in range(count)]
        while len(totals) > 1:
            totals = [totals[i] + totals[i + 1] for i in range(0, len(totals), 2)]
        return totals[0]

    def everywhere(part, turn):
        return exchange(exchange(part, abuf, turn, within, 8, near, a_s, a_r), bbuf, turn, plane * 4 + feat, 16, far, b_s, b_r)

    def product(stacked, high, low, dims):
        total = lax.dot_general(stacked, high, dims, preferred_element_type=jnp.float32)
        total = total + lax.dot_general(stacked, low, dims, preferred_element_type=jnp.float32)
        return jnp.sum(total, axis=0, keepdims=True)

    def solve(row):
        rest = [row[:, 512 * a : 512 * a + 512] for a in range(4)]
        for a in range(4):
            rest[a] = product(pair(rest[a]), inv_hi[a], inv_lo[a], NT)
            stacked = pair(rest[a])
            for b in range(a + 1, 4):
                at = place(a, b)
                rest[b] = rest[b] - product(stacked, up_hi[at], up_lo[at], NN)
        for a in range(3, -1, -1):
            rest[a] = product(pair(rest[a]), inv_hi[a], inv_lo[a], NN)
            stacked = pair(rest[a])
            for b in range(a):
                at = place(b, a)
                rest[b] = rest[b] - product(stacked, up_hi[at], up_lo[at], NT)
        return jnp.concatenate(rest, axis=1)

    def dot(left, right):
        return jnp.sum(left * right, axis=1, keepdims=True)

    residual = start[...]

    def step(number, carry):
        answer, residual, direction, inner = carry
        solved = solve(residual)
        inner_now = dot(residual, solved)
        direction = solved + jnp.where(number == 0, 0.0, inner_now / inner) * direction
        full[...] = direction
        row_sums = jnp.zeros((16, 512), jnp.float32)
        for o in range(4):
            row_sums = row_sums + lax.dot_general(pieces(full[:, columns(o)]), blocks[o], NT, preferred_element_type=jnp.float32)
        stacked = pieces(jnp.sum(row_sums, axis=0, keepdims=True))
        for o in range(4):
            part = lax.dot_general(stacked, blocks[o], NN, preferred_element_type=jnp.float32)
            wide[:, columns(o)] = jnp.sum(part, axis=0, keepdims=True)
        curved = everywhere(wide[...], number) * (1.0 / total_rows) + ridge * direction
        step_size = inner_now / dot(direction, curved)
        return answer + step_size * direction, residual - step_size * curved, direction, inner_now

    zero = jnp.zeros((1, D), jnp.float32)
    answer = lax.fori_loop(0, ITERS, step, (zero, residual, zero, jnp.ones((1, 1), jnp.float32)))[0]
    scale = jnp.minimum(1.0, radius[...] * math.sqrt(D) / jnp.sqrt(dot(answer, answer) + 1e-06))
    full[...] = answer
    out[...] = weights[...] + scale * full[:, columns(0)]


def pcg(total_rows, blocks, start, factors, weights, radius):
    vm = pl.BlockSpec(memory_space=pltpu.VMEM)
    dma = pltpu.SemaphoreType.DMA
    return pl.pallas_call(
        lambda *refs: pcg_kernel(total_rows, *refs),
        out_shape=jax.ShapeDtypeStruct((1, 512), jnp.float32),
        in_specs=[vm] * 8,
        out_specs=vm,
        scratch_shapes=[
            pltpu.VMEM((1, D), jnp.float32),
            pltpu.VMEM((1, D), jnp.float32),
            pltpu.VMEM((4, 8, 1, D), jnp.float32),
            pltpu.VMEM((4, 16, 1, D), jnp.float32),
            dma((4, 8)),
            dma((4, 8)),
            dma((4, 16)),
            dma((4, 16)),
        ],
        compiler_params=pltpu.CompilerParams(vmem_limit_bytes=32 * 2**20, collective_id=0, has_side_effects=True),
        name="pcg",
    )(blocks, start, *factors, weights, radius)


def row_times(row, matrix, dims):
    return jnp.sum(lax.dot_general(pieces(row), matrix, dims, preferred_element_type=jnp.float32), axis=0, keepdims=True)

def sketch_kernel(
    scale, total_rows, features, weights, labels, signs, coarse, fine,
    left, right, residual, blocks,
    send, arrive, narrow, xin, yin, stage, xlast, ylast, mine, pattern, weighted, wide, zbuf, abuf, bbuf, ssem, rsem, lsem,
):
    ex = lax.axis_index("ex")
    z = lax.axis_index("feat")
    y, x, c = ex // 8, (ex // 2) % 4, ex % 2

    def to_x(o):
        return ((y * 4 + (x + o) % 4) * 2 + c, z)

    def to_y(o):
        return ((((y + o) % 4) * 4 + x) * 2 + c, z)

    def to_z(o):
        return (ex, (z + o) % 4)

    other = (ex + 1 - 2 * c, z)
    within = ex % 8

    def near(o):
        return (y * 8 + (within + o) % 8, z)

    def far(o):
        to = (y * 4 + z + o) % 16
        return ((to // 4) * 8 + within, to % 4)

    barrier = pltpu.get_barrier_semaphore()
    for o in range(1, 8):
        pl.semaphore_signal(barrier, inc=1, device_id=near(o), device_id_type=MESH)
    for o in range(1, 16):
        pl.semaphore_signal(barrier, inc=1, device_id=far(o), device_id_type=MESH)

    started = []

    def ship(src, dst, device):
        at = len(started)
        copy = pltpu.make_async_remote_copy(
            src_ref=src, dst_ref=dst, send_sem=ssem.at[at], recv_sem=rsem.at[at], device_id=device, device_id_type=MESH
        )
        copy.start()
        started.append(copy)
        return copy

    def spread(buf, me, count, peer):
        return [ship(buf.at[me], buf.at[me], peer(o)) for o in range(1, count)]

    def gathered(copies, buf, count):
        for copy in copies:
            copy.wait_recv()
        totals = [buf[q] for q in range(count)]
        while len(totals) > 1:
            totals = [totals[i] + totals[i + 1] for i in range(0, len(totals), 2)]
        return totals[0]

    zbuf[z] = row_times(weights[...], features[...], NT)
    pl.semaphore_wait(barrier, 22)
    margin_copies = spread(zbuf, z, 4, to_z)
    sign_row = signs[...].astype(jnp.bfloat16)

    def patterns(q, carry):
        rows = pl.ds(pl.multiple_of(q * 256, 256), 256)
        fine_rows = fine[rows, :]
        for h in range(16):
            signed_rows = fine_rows * jnp.broadcast_to(sign_row[:, 128 * h : 128 * h + 128], (256, 128))
            pattern[rows, 128 * h : 128 * h + 128] = signed_rows * jnp.broadcast_to(coarse[rows, h : h + 1], (256, 128))
        return carry

    lax.fori_loop(0, 8, patterns, 0)
    margins = gathered(margin_copies, zbuf, 4)
    probability = 1.0 / (1.0 + jnp.exp(-margins))
    root = jnp.sqrt(probability * (1.0 - probability))
    for i in range(16):
        rows = slice(128 * i, 128 * i + 128)
        column = jnp.transpose(jnp.broadcast_to(root[:, rows], (128, 128)))
        for h in range(4):
            cols = slice(128 * h, 128 * h + 128)
            weighted[rows, cols] = (features[rows, cols].astype(jnp.float32) * column).astype(jnp.bfloat16)
    for o in range(1, 4):
        ship(weighted.at[pl.ds(pl.multiple_of(((z + o) % 4) * 512, 512), 512), :], blocks.at[o], to_z(o))
    kept = pltpu.make_async_copy(weighted.at[pl.ds(pl.multiple_of(z * 512, 512), 512), :], blocks.at[0], lsem.at[2])
    kept.start()
    redistributed = started[-3:]

    def mixed(half, o):
        parts = []
        for block, cols in (((x + o) % 4, slice(0, 256)), ((y + o) % 4, slice(256, 512))):
            rows = pl.ds(pl.multiple_of(half * 1024 + block * 256, 256), 256)
            parts.append(jnp.dot(pattern[rows, :], weighted[:, cols], preferred_element_type=jnp.float32))
        return parts

    halves = []
    for at, o in enumerate((1, 2, 3, 0)):
        send[at, 0], send[at, 1] = mixed(1 - c, o)
        halves.append(ship(send.at[at], arrive.at[at], other))
    slope = row_times(probability - labels[...].astype(jnp.float32), features[...], NN)
    wide[...] = jnp.zeros((1, D), jnp.float32)
    wide[:, pl.ds(pl.multiple_of(z * 512, 512), 512)] = slope * (1.0 / total_rows) + weights[...] * (REG / D / 32)
    abuf[within] = wide[...]
    near_copies = spread(abuf, within, 8, near)
    first = []
    for at, o in enumerate((1, 2, 3, 0)):
        left_total, right_total = mixed(c, o)
        halves[at].wait_recv()
        left_total = left_total + arrive[at, 0]
        right_total = right_total + arrive[at, 1]
        if o > 0:
            narrow[0, at] = left_total.astype(jnp.bfloat16)
            narrow[1, at] = right_total.astype(jnp.bfloat16)
            first.append(ship(narrow.at[0, at], xin.at[at], to_x(o)))
            first.append(ship(narrow.at[1, at], yin.at[at], to_y(o)))
    bbuf[y * 4 + z] = gathered(near_copies, abuf, 8)
    far_copies = spread(bbuf, y * 4 + z, 16, far)
    for copy in first:
        copy.wait_recv()
    for o in range(3):
        left_total = left_total + xin[o].astype(jnp.float32)
        right_total = right_total + yin[o].astype(jnp.float32)
    for q in range(4):
        stage[0, q] = left_total[64 * q : 64 * q + 64, :]
        stage[1, q] = right_total[64 * q : 64 * q + 64, :]
    second = []
    for o in range(1, 4):
        second.append(ship(stage.at[0, (y + o) % 4], ylast.at[o - 1], to_y(o)))
        second.append(ship(stage.at[1, (x + o) % 4], xlast.at[o - 1], to_x(o)))
    for copy in second:
        copy.wait_recv()
    mine[0] = ((stage[0, y] + ylast[0] + ylast[1] + ylast[2]) * scale).astype(jnp.bfloat16)
    mine[1] = ((stage[1, x] + xlast[0] + xlast[1] + xlast[2]) * scale).astype(jnp.bfloat16)

    cols = pl.ds(pl.multiple_of(z * 256, 256), 256)
    big, small = pl.ds(0, 48), pl.ds(48, 16)
    every = pl.ds(0, 4)
    own_left = pltpu.make_async_copy(mine.at[0], left.at[c, x, y, :, cols], lsem.at[0])
    own_right = pltpu.make_async_copy(mine.at[1], right.at[c, y, x, :, cols], lsem.at[1])
    own_left.start()
    own_right.start()

    def pass_on(work):
        copies = []
        for o in range(1, 4):
            for src, dst, peer in work:
                copies.append(ship(src, dst, peer(o)))
        return copies

    def same(ref, peer):
        return (ref, ref, peer)

    copies = pass_on(
        [
            (mine.at[0, big], left.at[c, x, y, big, cols], to_z),
            (mine.at[1, big], right.at[c, y, x, big, cols], to_z),
            (mine.at[0, small], left.at[c, x, y, small, cols], to_y),
            (mine.at[1, small], right.at[c, y, x, small, cols], to_x),
        ]
    )
    own_left.wait()
    own_right.wait()
    for copy in copies:
        copy.wait_recv()
    copies = pass_on(
        [
            same(left.at[c, x, y, big, :], to_y),
            same(right.at[c, y, x, big, :], to_x),
            same(left.at[c, x, every, small, cols], to_x),
            same(right.at[c, y, every, small, cols], to_y),
        ]
    )
    for copy in copies:
        copy.wait_recv()
    across = []

    def cross(ref):
        across.append(ship(ref, ref, other))

    def zcols(o):
        return pl.ds(pl.multiple_of(((z + o) % 4) * 256, 256), 256)

    def x_piece(o, part):
        return left.at[c, (x + o) % 4, pl.ds(2 * part, 2), big, :]

    def y_piece(o, part):
        return right.at[c, (y + o) % 4, pl.ds(2 * part, 2), big, :]

    def z_piece(o, part):
        return (left, right)[part].at[c, every, every, small, zcols(o)]

    streams = ((x_piece, to_x), (y_piece, to_y), (z_piece, to_z))
    up, down, late = [], [], []
    for piece, peer in streams:
        up.append(ship(piece(0, 0), piece(0, 0), peer(1)))
        down.append(ship(piece(0, 1), piece(0, 1), peer(3)))
    for piece, peer in streams:
        late.append((ship(piece(0, 1), piece(0, 1), peer(1)), piece(3, 1)))
        late.append((ship(piece(0, 0), piece(0, 0), peer(3)), piece(1, 0)))
    for piece, peer in streams:
        cross(piece(0, 0))
        cross(piece(0, 1))
    for at, (piece, peer) in enumerate(streams):
        up[at].wait_recv()
        late.append((ship(piece(3, 0), piece(3, 0), peer(1)), piece(2, 0)))
        cross(piece(3, 0))
        down[at].wait_recv()
        late.append((ship(piece(1, 1), piece(1, 1), peer(3)), piece(2, 1)))
        cross(piece(1, 1))
    for copy, ref in late:
        copy.wait_recv()
        cross(ref)
    for copy in across:
        copy.wait_recv()
    residual[...] = -gathered(far_copies, bbuf, 16)
    for copy in redistributed:
        copy.wait_recv()
    kept.wait()
    for copy in started:
        copy.wait_send()


def sketch_rows(scale, total_rows, features, weights, labels, signs, coarse, fine):
    vm = pl.BlockSpec(memory_space=pltpu.VMEM)
    anywhere = pl.BlockSpec(memory_space=pl.ANY)
    f32, bf16 = jnp.float32, jnp.bfloat16
    half = jax.ShapeDtypeStruct((2, 4, 4, 64, D // 2), bf16)
    left, right, residual, blocks = pl.pallas_call(
        lambda *refs: sketch_kernel(scale, total_rows, *refs),
        out_shape=(half, half, jax.ShapeDtypeStruct((1, D), f32), jax.ShapeDtypeStruct((4, 512, 512), bf16)),
        in_specs=[vm] * 6,
        out_specs=(anywhere, anywhere, vm, anywhere),
        scratch_shapes=[
            pltpu.VMEM((4, 2, 256, 256), f32),
            pltpu.VMEM((4, 2, 256, 256), f32),
            pltpu.VMEM((2, 3, 256, 256), bf16),
            pltpu.VMEM((3, 256, 256), bf16),
            pltpu.VMEM((3, 256, 256), bf16),
            pltpu.VMEM((2, 4, 64, 256), f32),
            pltpu.VMEM((3, 64, 256), f32),
            pltpu.VMEM((3, 64, 256), f32),
            pltpu.VMEM((2, 64, 256), bf16),
            pltpu.VMEM((D, 2048), bf16),
            pltpu.VMEM((2048, 512), bf16),
            pltpu.VMEM((1, D), f32),
            pltpu.VMEM((4, 1, 2048), f32),
            pltpu.VMEM((8, 1, D), f32),
            pltpu.VMEM((16, 1, D), f32),
            pltpu.SemaphoreType.DMA((120,)),
            pltpu.SemaphoreType.DMA((120,)),
            pltpu.SemaphoreType.DMA((3,)),
        ],
        compiler_params=pltpu.CompilerParams(vmem_limit_bytes=36 * 2**20, collective_id=1, has_side_effects=True),
        name="sketch",
    )(features, weights, labels, signs, coarse, fine)
    return left.reshape(D, D // 2), right.reshape(D, D // 2), residual, blocks


def parity(common):
    for shift in (8, 4, 2, 1):
        common = common ^ (common >> shift)
    return 1 - 2 * (common & 1)


def local(features, weights, labels, signs, samples, radius):
    row_count, feat_width = features.shape
    ex_count = lax.axis_size("ex")
    ex_index = lax.axis_index("ex")
    total_rows = row_count * ex_count
    sample_count = samples.shape[0]
    low, high = samples % row_count, samples // row_count
    coarse = parity((low[:, None] // 128) & lax.iota(jnp.int32, row_count // 128)[None, :])
    coarse = coarse * parity(high & ex_index)[:, None]
    fine = parity((low[:, None] % 128) & lax.iota(jnp.int32, 128)[None, :])
    scale = 1.0 / math.sqrt(total_rows * sample_count)
    left, right, residual, blocks = sketch_rows(
        scale,
        total_rows,
        features,
        weights[None, :],
        labels[None, :],
        signs[None, :],
        coarse.astype(jnp.bfloat16),
        fine.astype(jnp.bfloat16),
    )
    out = pcg(total_rows, blocks, residual, factor(left, right), weights[None, :], radius[None, :])
    return out[0]


def solution(mesh):
    in_specs = (P("ex", "feat"), P("feat"), P("ex"), P("ex"), P(), P())
    return jax.shard_map(local, mesh=mesh, in_specs=in_specs, out_specs=P("feat"), check_vma=False)
```

```python
import math

import jax
import jax.numpy as jnp
from jax import lax
from jax.experimental import pallas as pl
from jax.experimental.pallas import tpu as pltpu
from jax.sharding import PartitionSpec as P

D = 2048
ITERS = 4
REG = 0.02
HI = lax.Precision.HIGHEST
NN = (((1,), (0,)), ((), ()))
NT = (((1,), (1,)), ((), ()))
TN = (((0,), (0,)), ((), ()))
MESH = pl.DeviceIdType.MESH

def split2(value):
    high = value.astype(jnp.bfloat16)
    return high, (value - high.astype(jnp.float32)).astype(jnp.bfloat16)


def dot3(left, right, dims):
    (lc,), (rc,) = dims[0]
    lh, ll = split2(left)
    rh, rl = split2(right)
    left = jnp.concatenate([lh, lh, ll], axis=lc)
    right = jnp.concatenate([rh, rl, rh], axis=rc)
    return lax.dot_general(left, right, dims, preferred_element_type=jnp.float32)


def block_inverse(block):
    lanes = lax.broadcasted_iota(jnp.int32, (1, 128), 1)
    subs = lax.broadcasted_iota(jnp.int32, (8, 128), 0)
    tiles = [block[8 * t : 8 * t + 8, :] for t in range(16)]

    def lane(t, at):
        return jnp.broadcast_to(tiles[t][:, at : at + 1], (8, 128))

    def sub(tile, at):
        return jnp.broadcast_to(tile[at : at + 1, :], (8, 128))

    own = [lane(0, j) for j in range(8)]
    nxt = [lane(1, j) for j in range(8)]
    for g in range(16):
        base = 8 * g
        more, most = g + 1 < 16, g + 2 < 16
        if more:
            own_later = [lane(g + 1, base + 8 + j) for j in range(8)]
        if most:
            nxt_later = [lane(g + 2, base + 8 + j) for j in range(8)]
            second = [lane(g + 2, base + j) for j in range(8)]
        inverses, crosses, rows = [], {}, []
        head = tiles[g]
        nxt_scaled, second_scaled = [], []
        for j in range(8):
            inverse = 1.0 / sub(own[j], j)
            inverses.append(inverse)
            scaled = jnp.where(subs > j, own[j] * inverse, 0.0)
            if more:
                nxt_scaled.append(nxt[j] * inverse)
            if most:
                second_scaled.append(second[j] * inverse)
            for i in range(j + 1, 8):
                cross = sub(own[i], j)
                crosses[j, i] = cross
                own[i] = own[i] - scaled * cross
                if more:
                    nxt[i] = nxt[i] - nxt_scaled[j] * cross
                if most:
                    second[i] = second[i] - second_scaled[j] * cross
            if more:
                for i in range(8):
                    cross = sub(nxt[j], i)
                    own_later[i] = own_later[i] - nxt_scaled[j] * cross
                    if most:
                        nxt_later[i] = nxt_later[i] - second_scaled[j] * cross
            row = head[j : j + 1, :]
            row = jnp.broadcast_to(jnp.where(lanes == base + j, row + row, row), (8, 128))
            rows.append(row)
            head = head - scaled * row
        tiles[g] = head
        for t in range(g + 1, 16):
            if t == g + 1:
                scaled = nxt_scaled
            elif t == g + 2:
                scaled = second_scaled
            else:
                column = [lane(t, base + j) for j in range(8)]
                scaled = []
                for j in range(8):
                    scaled.append(column[j] * inverses[j])
                    for i in range(j + 1, 8):
                        column[i] = column[i] - scaled[j] * crosses[j, i]
            tile = tiles[t]
            for j in range(8):
                tile = tile - scaled[j] * rows[j]
            tiles[t] = tile
        if more:
            own = own_later
        if most:
            nxt = nxt_later
    whole = jnp.concatenate(tiles, axis=0)
    rows = lax.broadcasted_iota(jnp.int32, (128, 128), 0)
    cols = lax.broadcasted_iota(jnp.int32, (128, 128), 1)
    diagonal = jnp.where(rows == cols, whole, 0.0)
    along_rows = jnp.sum(diagonal, axis=0, keepdims=True)
    along_cols = jnp.sum(diagonal, axis=1, keepdims=True)
    lower = jnp.where(cols <= rows, whole, 0.0)
    return lower * (1.0 / along_rows) * (1.0 / jnp.sqrt(along_cols))


def factor_kernel(left, right, up_hi, up_lo, inv_hi, inv_lo, gram, invs, crosses, corner, trio_l, trio_r):
    ridge = REG / D
    halves = (left, right)
    for a in range(4):
        for b in range(a, 4):
            for h in range(2):
                for side in range(h if a == b else 0, 2):
                    part = lax.dot_general(
                        halves[h][:, 256 * a : 256 * a + 256],
                        halves[side][:, 256 * b : 256 * b + 256],
                        TN,
                        preferred_element_type=jnp.float32,
                    )
                    if a == b and h == side:
                        rows = lax.broadcasted_iota(jnp.int32, (256, 256), 0)
                        cols = lax.broadcasted_iota(jnp.int32, (256, 256), 1)
                        part = part + jnp.where(rows == cols, ridge, 0.0)
                    gram[512 * a + 256 * h : 512 * a + 256 * h + 256, 512 * b + 256 * side : 512 * b + 256 * side + 256] = part
                    if a == b and h < side:
                        gram[512 * a + 256 : 512 * a + 512, 512 * a : 512 * a + 256] = jnp.zeros((256, 256), jnp.float32)

    def join(top, bottom, cross):
        middle = dot3(cross, top, TN)
        edge = -dot3(bottom, middle, NN)
        zero = jnp.zeros_like(top)
        return jnp.concatenate([jnp.concatenate([top, zero], axis=1), jnp.concatenate([edge, bottom], axis=1)], axis=0)

    def step(s, carry):
        at = pl.multiple_of(s * 256, 256)
        next_at = pl.multiple_of(at + 128, 128)
        rows = pl.ds(at, 256)
        first = s // 2
        upper, lower = pl.ds(at, 128), pl.ds(next_at, 128)
        corner[0] = gram[upper, upper]

        def one(h, carry):
            corner[2 + h] = block_inverse(corner[h])

            if h == 0:
                cross = dot3(corner[2], gram[upper, lower], NN)
                corner[4] = cross
                corner[1] = gram[lower, lower] - dot3(cross, cross, TN)

            return carry

        one(0, 0)
        one(1, 0)
        inverse = join(corner[2], corner[3], corner[4])
        invs[s] = inverse
        ih, il = split2(inverse)
        ileft = jnp.concatenate([ih, ih, il], axis=1)
        half = pl.ds(pl.multiple_of((s % 2) * 256, 256), 256)
        for c in range(4):

            @pl.when(c >= (s + 1) // 2)
            def _():
                cs = slice(512 * c, 512 * c + 512)
                gh, gl = split2(gram[rows, cs])
                panel = lax.dot_general(ileft, jnp.concatenate([gh, gl, gh], axis=0), NN, preferred_element_type=jnp.float32)
                cols = lax.broadcasted_iota(jnp.int32, (256, 512), 1) + 512 * c
                panel = jnp.where(cols >= at + 256, panel, 0.0)
                ph, plo = split2(panel)
                trio_r[0:256, cs] = ph
                trio_r[256:512, cs] = plo
                trio_r[512:768, cs] = ph
                trio_l[0:256, cs] = ph
                trio_l[256:512, cs] = ph
                trio_l[512:768, cs] = plo

                @pl.when(c == first)
                def _():
                    crosses[first] = panel[:, 256:]

                @pl.when(c > first)
                def _():
                    block = first * (7 - first) // 2 + c - first - 1
                    up_hi[block, half, :] = ph
                    up_lo[block, half, :] = plo

        def across(a, carry):
            ra = pl.ds(pl.multiple_of(a * 512, 512), 512)

            def along(b, carry):
                cs = pl.ds(pl.multiple_of(b * 512, 512), 512)
                gram[ra, cs] = gram[ra, cs] - lax.dot_general(trio_l[:, ra], trio_r[:, cs], TN, preferred_element_type=jnp.float32)
                return carry

            return lax.fori_loop(a, 4, along, carry)

        lax.fori_loop((s + 1) // 2, 4, across, 0)
        return carry

    lax.fori_loop(0, 8, step, 0)

    def chunk(a, carry):
        hi, lo = split2(join(invs[2 * a], invs[2 * a + 1], crosses[a]))
        inv_hi[a] = hi
        inv_lo[a] = lo
        return carry

    lax.fori_loop(0, 4, chunk, 0)


def factor(left, right):
    vm = pl.BlockSpec(memory_space=pltpu.VMEM)
    ups = jax.ShapeDtypeStruct((6, 512, 512), jnp.bfloat16)
    inverses = jax.ShapeDtypeStruct((4, 512, 512), jnp.bfloat16)
    return pl.pallas_call(
        factor_kernel,
        out_shape=(ups, ups, inverses, inverses),
        in_specs=[vm, vm],
        out_specs=(vm, vm, vm, vm),
        scratch_shapes=[
            pltpu.VMEM((D, D), jnp.float32),
            pltpu.VMEM((8, 256, 256), jnp.float32),
            pltpu.VMEM((4, 256, 256), jnp.float32),
            pltpu.VMEM((5, 128, 128), jnp.float32),
            pltpu.VMEM((768, D), jnp.bfloat16),
            pltpu.VMEM((768, D), jnp.bfloat16),
        ],
        compiler_params=pltpu.CompilerParams(vmem_limit_bytes=30 * 2**20),
        cost_estimate=pl.CostEstimate(flops=60 * 10**9, bytes_accessed=18 * 2**20, transcendentals=0),
        name="factor",
    )(left, right)


def pieces(row):
    first = row.astype(jnp.bfloat16).astype(jnp.float32)
    rest = row - first
    second = rest.astype(jnp.bfloat16).astype(jnp.float32)
    third = rest - second
    which = lax.broadcasted_iota(jnp.int32, (16, row.shape[1]), 0)
    stacked = jnp.where(which == 0, first, jnp.where(which == 1, second, jnp.where(which == 2, third, 0.0)))
    return stacked.astype(jnp.bfloat16)


def pair(row):
    first = row.astype(jnp.bfloat16).astype(jnp.float32)
    which = lax.broadcasted_iota(jnp.int32, (16, row.shape[1]), 0)
    return jnp.where(which == 0, first, jnp.where(which == 1, row - first, 0.0)).astype(jnp.bfloat16)


def place(a, b):
    return a * (7 - a) // 2 + b - a - 1


def pcg_kernel(total_rows, blocks, start, up_hi, up_lo, inv_hi, inv_lo, weights, radius, out, full, wide, abuf, bbuf, a_s, a_r, b_s, b_r):
    ex = lax.axis_index("ex")
    feat = lax.axis_index("feat")
    plane, within = ex // 8, ex % 8
    ridge = REG / D

    def columns(o):
        return pl.ds(pl.multiple_of(((feat + 4 - o) % 4) * 512, 512), 512)

    def near(o):
        return (plane * 8 + (within + o) % 8, feat)

    def far(o):
        other = (plane * 4 + feat + o) % 16
        return ((other // 4) * 8 + within, other % 4)

    barrier = pltpu.get_barrier_semaphore()
    for o in range(1, 8):
        pl.semaphore_signal(barrier, inc=1, device_id=near(o), device_id_type=MESH)
    for o in range(1, 16):
        pl.semaphore_signal(barrier, inc=1, device_id=far(o), device_id_type=MESH)

    def exchange(value, buf, turn, me, count, peer, send, recv):
        buf[turn, me] = value
        copies = [
            pltpu.make_async_remote_copy(
                src_ref=buf.at[turn, me],
                dst_ref=buf.at[turn, me],
                send_sem=send.at[turn, o],
                recv_sem=recv.at[turn, o],
                device_id=peer(o),
                device_id_type=MESH,
            )
            for o in range(1, count)
        ]
        for copy in copies:
            copy.start()
        for copy in copies:
            copy.wait()
        totals = [buf[turn, q] for q in range(count)]
        while len(totals) > 1:
            totals = [totals[i] + totals[i + 1] for i in range(0, len(totals), 2)]
        return totals[0]

    def everywhere(part, turn):
        return exchange(exchange(part, abuf, turn, within, 8, near, a_s, a_r), bbuf, turn, plane * 4 + feat, 16, far, b_s, b_r)

    def product(stacked, high, low, dims):
        total = lax.dot_general(stacked, high, dims, preferred_element_type=jnp.float32)
        total = total + lax.dot_general(stacked, low, dims, preferred_element_type=jnp.float32)
        return jnp.sum(total, axis=0, keepdims=True)

    def solve(row):
        rest = [row[:, 512 * a : 512 * a + 512] for a in range(4)]
        for a in range(4):
            rest[a] = product(pair(rest[a]), inv_hi[a], inv_lo[a], NT)
            stacked = pair(rest[a])
            for b in range(a + 1, 4):
                at = place(a, b)
                rest[b] = rest[b] - product(stacked, up_hi[at], up_lo[at], NN)
        for a in range(3, -1, -1):
            rest[a] = product(pair(rest[a]), inv_hi[a], inv_lo[a], NN)
            stacked = pair(rest[a])
            for b in range(a):
                at = place(b, a)
                rest[b] = rest[b] - product(stacked, up_hi[at], up_lo[at], NT)
        return jnp.concatenate(rest, axis=1)

    def dot(left, right):
        return jnp.sum(left * right, axis=1, keepdims=True)

    residual = start[...]

    def step(number, carry):
        answer, residual, direction, inner = carry
        solved = solve(residual)
        inner_now = dot(residual, solved)
        direction = solved + jnp.where(number == 0, 0.0, inner_now / inner) * direction
        full[...] = direction
        row_sums = jnp.zeros((16, 512), jnp.float32)
        for o in range(4):
            row_sums = row_sums + lax.dot_general(pieces(full[:, columns(o)]), blocks[o], NT, preferred_element_type=jnp.float32)
        stacked = pieces(jnp.sum(row_sums, axis=0, keepdims=True))
        for o in range(4):
            part = lax.dot_general(stacked, blocks[o], NN, preferred_element_type=jnp.float32)
            wide[:, columns(o)] = jnp.sum(part, axis=0, keepdims=True)

        @pl.when(number == 0)
        def _():
            pl.semaphore_wait(barrier, 22)

        curved = everywhere(wide[...], number) * (1.0 / total_rows) + ridge * direction
        step_size = inner_now / dot(direction, curved)
        return answer + step_size * direction, residual - step_size * curved, direction, inner_now

    zero = jnp.zeros((1, D), jnp.float32)
    answer = lax.fori_loop(0, ITERS, step, (zero, residual, zero, jnp.ones((1, 1), jnp.float32)))[0]
    scale = jnp.minimum(1.0, radius[...] * math.sqrt(D) / jnp.sqrt(dot(answer, answer) + 1e-06))
    full[...] = answer
    out[...] = weights[...] + scale * full[:, columns(0)]


def pcg(total_rows, blocks, start, factors, weights, radius):
    vm = pl.BlockSpec(memory_space=pltpu.VMEM)
    dma = pltpu.SemaphoreType.DMA
    return pl.pallas_call(
        lambda *refs: pcg_kernel(total_rows, *refs),
        out_shape=jax.ShapeDtypeStruct((1, 512), jnp.float32),
        in_specs=[vm] * 8,
        out_specs=vm,
        scratch_shapes=[
            pltpu.VMEM((1, D), jnp.float32),
            pltpu.VMEM((1, D), jnp.float32),
            pltpu.VMEM((4, 8, 1, D), jnp.float32),
            pltpu.VMEM((4, 16, 1, D), jnp.float32),
            dma((4, 8)),
            dma((4, 8)),
            dma((4, 16)),
            dma((4, 16)),
        ],
        compiler_params=pltpu.CompilerParams(vmem_limit_bytes=32 * 2**20, collective_id=0, has_side_effects=True),
        name="pcg",
    )(blocks, start, *factors, weights, radius)


def row_times(row, matrix, dims):
    return jnp.sum(lax.dot_general(pieces(row), matrix, dims, preferred_element_type=jnp.float32), axis=0, keepdims=True)

def sketch_kernel(
    scale, total_rows, features, weights, labels, signs, coarse, fine,
    left, right, residual, blocks,
    send, arrive, narrow, xin, yin, stage, xlast, ylast, mine, pattern, weighted, relay, wide, zbuf, abuf, bbuf, ssem, rsem, lsem,
):
    ex = lax.axis_index("ex")
    z = lax.axis_index("feat")
    y, x, c = ex // 8, (ex // 2) % 4, ex % 2

    def to_x(o):
        return ((y * 4 + (x + o) % 4) * 2 + c, z)

    def to_y(o):
        return ((((y + o) % 4) * 4 + x) * 2 + c, z)

    def to_z(o):
        return (ex, (z + o) % 4)

    other = (ex + 1 - 2 * c, z)
    within = ex % 8

    def near(o):
        return (y * 8 + (within + o) % 8, z)

    def far(o):
        to = (y * 4 + z + o) % 16
        return ((to // 4) * 8 + within, to % 4)

    barrier = pltpu.get_barrier_semaphore()
    for o in range(1, 8):
        pl.semaphore_signal(barrier, inc=1, device_id=near(o), device_id_type=MESH)
    for o in range(1, 16):
        pl.semaphore_signal(barrier, inc=1, device_id=far(o), device_id_type=MESH)

    started = []

    def ship(src, dst, device):
        at = len(started)
        copy = pltpu.make_async_remote_copy(
            src_ref=src, dst_ref=dst, send_sem=ssem.at[at], recv_sem=rsem.at[at], device_id=device, device_id_type=MESH
        )
        copy.start()
        started.append(copy)
        return copy

    def spread(buf, me, count, peer):
        return [ship(buf.at[me], buf.at[me], peer(o)) for o in range(1, count)]

    def gathered(copies, buf, count):
        for copy in copies:
            copy.wait_recv()
        totals = [buf[q] for q in range(count)]
        while len(totals) > 1:
            totals = [totals[i] + totals[i + 1] for i in range(0, len(totals), 2)]
        return totals[0]

    zbuf[z] = row_times(weights[...], features[...], NT)
    pl.semaphore_wait(barrier, 22)
    margin_copies = spread(zbuf, z, 4, to_z)
    sign_row = signs[...].astype(jnp.bfloat16)

    def patterns(q, carry):
        rows = pl.ds(pl.multiple_of(q * 256, 256), 256)
        fine_rows = fine[rows, :]
        for h in range(16):
            signed_rows = fine_rows * jnp.broadcast_to(sign_row[:, 128 * h : 128 * h + 128], (256, 128))
            pattern[rows, 128 * h : 128 * h + 128] = signed_rows * jnp.broadcast_to(coarse[rows, h : h + 1], (256, 128))
        return carry

    lax.fori_loop(0, 8, patterns, 0)
    margins = gathered(margin_copies, zbuf, 4)
    probability = 1.0 / (1.0 + jnp.exp(-margins))
    root = jnp.sqrt(probability * (1.0 - probability))
    for i in range(16):
        rows = slice(128 * i, 128 * i + 128)
        column = jnp.transpose(jnp.broadcast_to(root[:, rows], (128, 128)))
        for h in range(4):
            cols = slice(128 * h, 128 * h + 128)
            weighted[rows, cols] = (features[rows, cols].astype(jnp.float32) * column).astype(jnp.bfloat16)

    def rows_for(o, part, size):
        return weighted.at[pl.ds(pl.multiple_of(((z + o) % 4) * 512 + part * 256, 256), size), :]

    passing = [ship(rows_for(2, 0, 256), relay.at[0], to_z(1)), ship(rows_for(2, 1, 256), relay.at[1], to_z(3))]
    redistributed = [ship(rows_for(1, 0, 512), blocks.at[1], to_z(1)), ship(rows_for(3, 0, 512), blocks.at[3], to_z(3))]
    kept = pltpu.make_async_copy(weighted.at[pl.ds(pl.multiple_of(z * 512, 512), 512), :], blocks.at[0], lsem.at[2])
    kept.start()

    def mixed(half, o):
        parts = []
        for block, cols in (((x + o) % 4, slice(0, 256)), ((y + o) % 4, slice(256, 512))):
            rows = pl.ds(pl.multiple_of(half * 1024 + block * 256, 256), 256)
            parts.append(jnp.dot(pattern[rows, :], weighted[:, cols], preferred_element_type=jnp.float32))
        return parts

    halves = []
    for at, o in enumerate((1, 2, 3, 0)):
        send[at, 0], send[at, 1] = mixed(1 - c, o)
        halves.append(ship(send.at[at], arrive.at[at], other))
    slope = row_times(probability - labels[...].astype(jnp.float32), features[...], NN)
    wide[...] = jnp.zeros((1, D), jnp.float32)
    wide[:, pl.ds(pl.multiple_of(z * 512, 512), 512)] = slope * (1.0 / total_rows) + weights[...] * (REG / D / 32)
    abuf[within] = wide[...]
    near_copies = spread(abuf, within, 8, near)
    first = []
    for at, o in enumerate((1, 2, 3, 0)):
        left_total, right_total = mixed(c, o)
        halves[at].wait_recv()
        left_total = left_total + arrive[at, 0]
        right_total = right_total + arrive[at, 1]
        if o > 0:
            narrow[0, at] = left_total.astype(jnp.bfloat16)
            narrow[1, at] = right_total.astype(jnp.bfloat16)
            first.append(ship(narrow.at[0, at], xin.at[at], to_x(o)))
            first.append(ship(narrow.at[1, at], yin.at[at], to_y(o)))
    for part, o in ((0, 1), (1, 3)):
        passing[part].wait_recv()
        redistributed.append(ship(relay.at[part], blocks.at[2, pl.ds(256 * part, 256)], to_z(o)))
    bbuf[y * 4 + z] = gathered(near_copies, abuf, 8)
    far_copies = spread(bbuf, y * 4 + z, 16, far)
    for copy in first:
        copy.wait_recv()
    for o in range(3):
        left_total = left_total + xin[o].astype(jnp.float32)
        right_total = right_total + yin[o].astype(jnp.float32)
    for q in range(4):
        stage[0, q] = left_total[64 * q : 64 * q + 64, :]
        stage[1, q] = right_total[64 * q : 64 * q + 64, :]
    second = []
    for o in range(1, 4):
        second.append(ship(stage.at[0, (y + o) % 4], ylast.at[o - 1], to_y(o)))
        second.append(ship(stage.at[1, (x + o) % 4], xlast.at[o - 1], to_x(o)))
    for copy in second:
        copy.wait_recv()
    mine[0] = ((stage[0, y] + ylast[0] + ylast[1] + ylast[2]) * scale).astype(jnp.bfloat16)
    mine[1] = ((stage[1, x] + xlast[0] + xlast[1] + xlast[2]) * scale).astype(jnp.bfloat16)

    cols = pl.ds(pl.multiple_of(z * 256, 256), 256)
    big, small = pl.ds(0, 48), pl.ds(48, 16)
    every = pl.ds(0, 4)
    own_left = pltpu.make_async_copy(mine.at[0], left.at[c, x, y, :, cols], lsem.at[0])
    own_right = pltpu.make_async_copy(mine.at[1], right.at[c, y, x, :, cols], lsem.at[1])
    own_left.start()
    own_right.start()

    def pass_on(work):
        copies = []
        for o in range(1, 4):
            for src, dst, peer in work:
                copies.append(ship(src, dst, peer(o)))
        return copies

    def same(ref, peer):
        return (ref, ref, peer)

    copies = pass_on(
        [
            (mine.at[0, big], left.at[c, x, y, big, cols], to_z),
            (mine.at[1, big], right.at[c, y, x, big, cols], to_z),
            (mine.at[0, small], left.at[c, x, y, small, cols], to_y),
            (mine.at[1, small], right.at[c, y, x, small, cols], to_x),
        ]
    )
    own_left.wait()
    own_right.wait()
    for copy in copies:
        copy.wait_recv()
    copies = pass_on(
        [
            same(left.at[c, x, y, big, :], to_y),
            same(right.at[c, y, x, big, :], to_x),
            same(left.at[c, x, every, small, cols], to_x),
            same(right.at[c, y, every, small, cols], to_y),
        ]
    )
    for copy in copies:
        copy.wait_recv()
    across = []

    def cross(ref):
        across.append(ship(ref, ref, other))

    def zcols(o):
        return pl.ds(pl.multiple_of(((z + o) % 4) * 256, 256), 256)

    def x_piece(o, part):
        return left.at[c, (x + o) % 4, pl.ds(2 * part, 2), big, :]

    def y_piece(o, part):
        return right.at[c, (y + o) % 4, pl.ds(2 * part, 2), big, :]

    def z_piece(o, part):
        return (left, right)[part].at[c, every, every, small, zcols(o)]

    streams = ((x_piece, to_x), (y_piece, to_y), (z_piece, to_z))
    up, down, late = [], [], []
    for piece, peer in streams:
        up.append(ship(piece(0, 0), piece(0, 0), peer(1)))
        down.append(ship(piece(0, 1), piece(0, 1), peer(3)))
    for piece, peer in streams:
        late.append((ship(piece(0, 1), piece(0, 1), peer(1)), piece(3, 1)))
        late.append((ship(piece(0, 0), piece(0, 0), peer(3)), piece(1, 0)))
    for piece, peer in streams:
        cross(piece(0, 0))
        cross(piece(0, 1))
    for at, (piece, peer) in enumerate(streams):
        up[at].wait_recv()
        late.append((ship(piece(3, 0), piece(3, 0), peer(1)), piece(2, 0)))
        cross(piece(3, 0))
        down[at].wait_recv()
        late.append((ship(piece(1, 1), piece(1, 1), peer(3)), piece(2, 1)))
        cross(piece(1, 1))
    for copy, ref in late:
        copy.wait_recv()
        cross(ref)
    for copy in across:
        copy.wait_recv()
    residual[...] = -gathered(far_copies, bbuf, 16)
    for copy in redistributed:
        copy.wait_recv()
    kept.wait()
    for copy in started:
        copy.wait_send()


def sketch_rows(scale, total_rows, features, weights, labels, signs, coarse, fine):
    vm = pl.BlockSpec(memory_space=pltpu.VMEM)
    anywhere = pl.BlockSpec(memory_space=pl.ANY)
    f32, bf16 = jnp.float32, jnp.bfloat16
    half = jax.ShapeDtypeStruct((2, 4, 4, 64, D // 2), bf16)
    left, right, residual, blocks = pl.pallas_call(
        lambda *refs: sketch_kernel(scale, total_rows, *refs),
        out_shape=(half, half, jax.ShapeDtypeStruct((1, D), f32), jax.ShapeDtypeStruct((4, 512, 512), bf16)),
        in_specs=[vm] * 6,
        out_specs=(anywhere, anywhere, vm, anywhere),
        scratch_shapes=[
            pltpu.VMEM((4, 2, 256, 256), f32),
            pltpu.VMEM((4, 2, 256, 256), f32),
            pltpu.VMEM((2, 3, 256, 256), bf16),
            pltpu.VMEM((3, 256, 256), bf16),
            pltpu.VMEM((3, 256, 256), bf16),
            pltpu.VMEM((2, 4, 64, 256), f32),
            pltpu.VMEM((3, 64, 256), f32),
            pltpu.VMEM((3, 64, 256), f32),
            pltpu.VMEM((2, 64, 256), bf16),
            pltpu.VMEM((D, 2048), bf16),
            pltpu.VMEM((2048, 512), bf16),
            pltpu.VMEM((2, 256, 512), bf16),
            pltpu.VMEM((1, D), f32),
            pltpu.VMEM((4, 1, 2048), f32),
            pltpu.VMEM((8, 1, D), f32),
            pltpu.VMEM((16, 1, D), f32),
            pltpu.SemaphoreType.DMA((120,)),
            pltpu.SemaphoreType.DMA((120,)),
            pltpu.SemaphoreType.DMA((3,)),
        ],
        compiler_params=pltpu.CompilerParams(vmem_limit_bytes=36 * 2**20, collective_id=1, has_side_effects=True),
        name="sketch",
    )(features, weights, labels, signs, coarse, fine)
    return left.reshape(D, D // 2), right.reshape(D, D // 2), residual, blocks


def parity(common):
    for shift in (8, 4, 2, 1):
        common = common ^ (common >> shift)
    return 1 - 2 * (common & 1)


def local(features, weights, labels, signs, samples, radius):
    row_count, feat_width = features.shape
    ex_count = lax.axis_size("ex")
    ex_index = lax.axis_index("ex")
    total_rows = row_count * ex_count
    sample_count = samples.shape[0]
    low, high = samples % row_count, samples // row_count
    coarse = parity((low[:, None] // 128) & lax.iota(jnp.int32, row_count // 128)[None, :])
    coarse = coarse * parity(high & ex_index)[:, None]
    fine = parity((low[:, None] % 128) & lax.iota(jnp.int32, 128)[None, :])
    scale = 1.0 / math.sqrt(total_rows * sample_count)
    left, right, residual, blocks = sketch_rows(
        scale,
        total_rows,
        features,
        weights[None, :],
        labels[None, :],
        signs[None, :],
        coarse.astype(jnp.bfloat16),
        fine.astype(jnp.bfloat16),
    )
    out = pcg(total_rows, blocks, residual, factor(left, right), weights[None, :], radius[None, :])
    return out[0]


def solution(mesh):
    in_specs = (P("ex", "feat"), P("feat"), P("ex"), P("ex"), P(), P())
    return jax.shard_map(local, mesh=mesh, in_specs=in_specs, out_specs=P("feat"), check_vma=False)
```

```python
import math

import jax
import jax.numpy as jnp
from jax import lax
from jax.experimental import pallas as pl
from jax.experimental.pallas import tpu as pltpu
from jax.sharding import PartitionSpec as P

D = 2048
ITERS = 4
REG = 0.02
HI = lax.Precision.HIGHEST
NN = (((1,), (0,)), ((), ()))
NT = (((1,), (1,)), ((), ()))
TN = (((0,), (0,)), ((), ()))
MESH = pl.DeviceIdType.MESH

def split2(value):
    high = value.astype(jnp.bfloat16)
    return high, (value - high.astype(jnp.float32)).astype(jnp.bfloat16)


def dot3(left, right, dims):
    (lc,), (rc,) = dims[0]
    lh, ll = split2(left)
    rh, rl = split2(right)
    left = jnp.concatenate([lh, lh, ll], axis=lc)
    right = jnp.concatenate([rh, rl, rh], axis=rc)
    return lax.dot_general(left, right, dims, preferred_element_type=jnp.float32)


def block_inverse(block):
    lanes = lax.broadcasted_iota(jnp.int32, (1, 128), 1)
    subs = lax.broadcasted_iota(jnp.int32, (8, 128), 0)
    tiles = [block[8 * t : 8 * t + 8, :] for t in range(16)]

    def lane(t, at):
        return jnp.broadcast_to(tiles[t][:, at : at + 1], (8, 128))

    def sub(tile, at):
        return jnp.broadcast_to(tile[at : at + 1, :], (8, 128))

    own = [lane(0, j) for j in range(8)]
    nxt = [lane(1, j) for j in range(8)]
    for g in range(16):
        base = 8 * g
        more, most = g + 1 < 16, g + 2 < 16
        if more:
            own_later = [lane(g + 1, base + 8 + j) for j in range(8)]
        if most:
            nxt_later = [lane(g + 2, base + 8 + j) for j in range(8)]
            second = [lane(g + 2, base + j) for j in range(8)]
        inverses, crosses, rows = [], {}, []
        head = tiles[g]
        nxt_scaled, second_scaled = [], []
        for j in range(8):
            inverse = 1.0 / sub(own[j], j)
            inverses.append(inverse)
            scaled = jnp.where(subs > j, own[j] * inverse, 0.0)
            if more:
                nxt_scaled.append(nxt[j] * inverse)
            if most:
                second_scaled.append(second[j] * inverse)
            for i in range(j + 1, 8):
                cross = sub(own[i], j)
                crosses[j, i] = cross
                own[i] = own[i] - scaled * cross
                if more:
                    nxt[i] = nxt[i] - nxt_scaled[j] * cross
                if most:
                    second[i] = second[i] - second_scaled[j] * cross
            if more:
                for i in range(8):
                    cross = sub(nxt[j], i)
                    own_later[i] = own_later[i] - nxt_scaled[j] * cross
                    if most:
                        nxt_later[i] = nxt_later[i] - second_scaled[j] * cross
            row = head[j : j + 1, :]
            row = jnp.broadcast_to(jnp.where(lanes == base + j, row + row, row), (8, 128))
            rows.append(row)
            head = head - scaled * row
        tiles[g] = head
        for t in range(g + 1, 16):
            if t == g + 1:
                scaled = nxt_scaled
            elif t == g + 2:
                scaled = second_scaled
            else:
                column = [lane(t, base + j) for j in range(8)]
                scaled = []
                for j in range(8):
                    scaled.append(column[j] * inverses[j])
                    for i in range(j + 1, 8):
                        column[i] = column[i] - scaled[j] * crosses[j, i]
            tile = tiles[t]
            for j in range(8):
                tile = tile - scaled[j] * rows[j]
            tiles[t] = tile
        if more:
            own = own_later
        if most:
            nxt = nxt_later
    whole = jnp.concatenate(tiles, axis=0)
    rows = lax.broadcasted_iota(jnp.int32, (128, 128), 0)
    cols = lax.broadcasted_iota(jnp.int32, (128, 128), 1)
    diagonal = jnp.where(rows == cols, whole, 0.0)
    along_rows = jnp.sum(diagonal, axis=0, keepdims=True)
    along_cols = jnp.sum(diagonal, axis=1, keepdims=True)
    lower = jnp.where(cols <= rows, whole, 0.0)
    return lower * (1.0 / along_rows) * (1.0 / jnp.sqrt(along_cols))


def factor_kernel(left, right, up_hi, up_lo, inv_hi, inv_lo, gram, invs, crosses, corner, trio_l, trio_r):
    ridge = REG / D
    halves = (left, right)
    for a in range(4):
        for b in range(a, 4):
            for h in range(2):
                for side in range(h if a == b else 0, 2):
                    part = lax.dot_general(
                        halves[h][:, 256 * a : 256 * a + 256],
                        halves[side][:, 256 * b : 256 * b + 256],
                        TN,
                        preferred_element_type=jnp.float32,
                    )
                    if a == b and h == side:
                        rows = lax.broadcasted_iota(jnp.int32, (256, 256), 0)
                        cols = lax.broadcasted_iota(jnp.int32, (256, 256), 1)
                        part = part + jnp.where(rows == cols, ridge, 0.0)
                    gram[512 * a + 256 * h : 512 * a + 256 * h + 256, 512 * b + 256 * side : 512 * b + 256 * side + 256] = part
                    if a == b and h < side:
                        gram[512 * a + 256 : 512 * a + 512, 512 * a : 512 * a + 256] = jnp.zeros((256, 256), jnp.float32)

    def join(top, bottom, cross):
        middle = dot3(cross, top, TN)
        edge = -dot3(bottom, middle, NN)
        zero = jnp.zeros_like(top)
        return jnp.concatenate([jnp.concatenate([top, zero], axis=1), jnp.concatenate([edge, bottom], axis=1)], axis=0)

    def step(s, carry):
        at = pl.multiple_of(s * 256, 256)
        next_at = pl.multiple_of(at + 128, 128)
        rows = pl.ds(at, 256)
        first = s // 2
        upper, lower = pl.ds(at, 128), pl.ds(next_at, 128)
        corner[0] = gram[upper, upper]

        def one(h, carry):
            corner[2 + h] = block_inverse(corner[h])

            if h == 0:
                cross = dot3(corner[2], gram[upper, lower], NN)
                corner[4] = cross
                corner[1] = gram[lower, lower] - dot3(cross, cross, TN)

            return carry

        one(0, 0)
        one(1, 0)
        inverse = join(corner[2], corner[3], corner[4])
        invs[s] = inverse
        ih, il = split2(inverse)
        ileft = jnp.concatenate([ih, ih, il], axis=1)
        half = pl.ds(pl.multiple_of((s % 2) * 256, 256), 256)
        for c in range(4):

            @pl.when(c >= (s + 1) // 2)
            def _():
                cs = slice(512 * c, 512 * c + 512)
                gh, gl = split2(gram[rows, cs])
                panel = lax.dot_general(ileft, jnp.concatenate([gh, gl, gh], axis=0), NN, preferred_element_type=jnp.float32)
                cols = lax.broadcasted_iota(jnp.int32, (256, 512), 1) + 512 * c
                panel = jnp.where(cols >= at + 256, panel, 0.0)
                ph, plo = split2(panel)
                trio_r[0:256, cs] = ph
                trio_r[256:512, cs] = plo
                trio_r[512:768, cs] = ph
                trio_l[0:256, cs] = ph
                trio_l[256:512, cs] = ph
                trio_l[512:768, cs] = plo

                @pl.when(c == first)
                def _():
                    crosses[first] = panel[:, 256:]

                @pl.when(c > first)
                def _():
                    block = first * (7 - first) // 2 + c - first - 1
                    up_hi[block, half, :] = ph
                    up_lo[block, half, :] = plo

        def across(a, carry):
            ra = pl.ds(pl.multiple_of(a * 512, 512), 512)

            def along(b, carry):
                cs = pl.ds(pl.multiple_of(b * 512, 512), 512)
                gram[ra, cs] = gram[ra, cs] - lax.dot_general(trio_l[:, ra], trio_r[:, cs], TN, preferred_element_type=jnp.float32)
                return carry

            return lax.fori_loop(a, 4, along, carry)

        lax.fori_loop((s + 1) // 2, 4, across, 0)
        return carry

    lax.fori_loop(0, 8, step, 0)

    def chunk(a, carry):
        hi, lo = split2(join(invs[2 * a], invs[2 * a + 1], crosses[a]))
        inv_hi[a] = hi
        inv_lo[a] = lo
        return carry

    lax.fori_loop(0, 4, chunk, 0)


def factor(left, right):
    vm = pl.BlockSpec(memory_space=pltpu.VMEM)
    ups = jax.ShapeDtypeStruct((6, 512, 512), jnp.bfloat16)
    inverses = jax.ShapeDtypeStruct((4, 512, 512), jnp.bfloat16)
    return pl.pallas_call(
        factor_kernel,
        out_shape=(ups, ups, inverses, inverses),
        in_specs=[vm, vm],
        out_specs=(vm, vm, vm, vm),
        scratch_shapes=[
            pltpu.VMEM((D, D), jnp.float32),
            pltpu.VMEM((8, 256, 256), jnp.float32),
            pltpu.VMEM((4, 256, 256), jnp.float32),
            pltpu.VMEM((5, 128, 128), jnp.float32),
            pltpu.VMEM((768, D), jnp.bfloat16),
            pltpu.VMEM((768, D), jnp.bfloat16),
        ],
        compiler_params=pltpu.CompilerParams(vmem_limit_bytes=30 * 2**20),
        cost_estimate=pl.CostEstimate(flops=60 * 10**9, bytes_accessed=18 * 2**20, transcendentals=0),
        name="factor",
    )(left, right)


def pieces(row):
    first = row.astype(jnp.bfloat16).astype(jnp.float32)
    rest = row - first
    second = rest.astype(jnp.bfloat16).astype(jnp.float32)
    third = rest - second
    which = lax.broadcasted_iota(jnp.int32, (16, row.shape[1]), 0)
    stacked = jnp.where(which == 0, first, jnp.where(which == 1, second, jnp.where(which == 2, third, 0.0)))
    return stacked.astype(jnp.bfloat16)


def pair(row):
    first = row.astype(jnp.bfloat16).astype(jnp.float32)
    which = lax.broadcasted_iota(jnp.int32, (16, row.shape[1]), 0)
    return jnp.where(which == 0, first, jnp.where(which == 1, row - first, 0.0)).astype(jnp.bfloat16)


def place(a, b):
    return a * (7 - a) // 2 + b - a - 1


def pcg_kernel(total_rows, blocks, start, up_hi, up_lo, inv_hi, inv_lo, weights, radius, out, full, wide, abuf, bbuf, a_s, a_r, b_s, b_r):
    ex = lax.axis_index("ex")
    feat = lax.axis_index("feat")
    plane, within = ex // 8, ex % 8
    ridge = REG / D

    def columns(o):
        return pl.ds(pl.multiple_of(((feat + 4 - o) % 4) * 512, 512), 512)

    def near(o):
        return (plane * 8 + (within + o) % 8, feat)

    def far(o):
        other = (plane * 4 + feat + o) % 16
        return ((other // 4) * 8 + within, other % 4)

    barrier = pltpu.get_barrier_semaphore()
    for o in range(1, 8):
        pl.semaphore_signal(barrier, inc=1, device_id=near(o), device_id_type=MESH)
    for o in range(1, 16):
        pl.semaphore_signal(barrier, inc=1, device_id=far(o), device_id_type=MESH)

    def exchange(value, buf, turn, me, count, peer, send, recv):
        buf[turn, me] = value
        copies = [
            pltpu.make_async_remote_copy(
                src_ref=buf.at[turn, me],
                dst_ref=buf.at[turn, me],
                send_sem=send.at[turn, o],
                recv_sem=recv.at[turn, o],
                device_id=peer(o),
                device_id_type=MESH,
            )
            for o in range(1, count)
        ]
        for copy in copies:
            copy.start()
        for copy in copies:
            copy.wait()
        totals = [buf[turn, q] for q in range(count)]
        while len(totals) > 1:
            totals = [totals[i] + totals[i + 1] for i in range(0, len(totals), 2)]
        return totals[0]

    def everywhere(part, turn):
        return exchange(exchange(part, abuf, turn, within, 8, near, a_s, a_r), bbuf, turn, plane * 4 + feat, 16, far, b_s, b_r)

    def product(stacked, high, low, dims):
        total = lax.dot_general(stacked, high, dims, preferred_element_type=jnp.float32)
        total = total + lax.dot_general(stacked, low, dims, preferred_element_type=jnp.float32)
        return jnp.sum(total, axis=0, keepdims=True)

    def solve(row):
        rest = [row[:, 512 * a : 512 * a + 512] for a in range(4)]
        for a in range(4):
            rest[a] = product(pair(rest[a]), inv_hi[a], inv_lo[a], NT)
            stacked = pair(rest[a])
            for b in range(a + 1, 4):
                at = place(a, b)
                rest[b] = rest[b] - product(stacked, up_hi[at], up_lo[at], NN)
        for a in range(3, -1, -1):
            rest[a] = product(pair(rest[a]), inv_hi[a], inv_lo[a], NN)
            stacked = pair(rest[a])
            for b in range(a):
                at = place(b, a)
                rest[b] = rest[b] - product(stacked, up_hi[at], up_lo[at], NT)
        return jnp.concatenate(rest, axis=1)

    def dot(left, right):
        return jnp.sum(left * right, axis=1, keepdims=True)

    residual = start[...]

    def step(number, carry):
        answer, residual, direction, inner = carry
        solved = solve(residual)
        inner_now = dot(residual, solved)
        direction = solved + jnp.where(number == 0, 0.0, inner_now / inner) * direction
        full[...] = direction
        row_sums = jnp.zeros((16, 512), jnp.float32)
        for o in range(4):
            row_sums = row_sums + lax.dot_general(pieces(full[:, columns(o)]), blocks[o], NT, preferred_element_type=jnp.float32)
        stacked = pieces(jnp.sum(row_sums, axis=0, keepdims=True))
        for o in range(4):
            part = lax.dot_general(stacked, blocks[o], NN, preferred_element_type=jnp.float32)
            wide[:, columns(o)] = jnp.sum(part, axis=0, keepdims=True)

        @pl.when(number == 0)
        def _():
            pl.semaphore_wait(barrier, 22)

        curved = everywhere(wide[...], number) * (1.0 / total_rows) + ridge * direction
        step_size = inner_now / dot(direction, curved)
        return answer + step_size * direction, residual - step_size * curved, direction, inner_now

    zero = jnp.zeros((1, D), jnp.float32)
    answer = lax.fori_loop(0, ITERS, step, (zero, residual, zero, jnp.ones((1, 1), jnp.float32)))[0]
    scale = jnp.minimum(1.0, radius[...] * math.sqrt(D) / jnp.sqrt(dot(answer, answer) + 1e-06))
    full[...] = answer
    out[...] = weights[...] + scale * full[:, columns(0)]


def pcg(total_rows, blocks, start, factors, weights, radius):
    vm = pl.BlockSpec(memory_space=pltpu.VMEM)
    dma = pltpu.SemaphoreType.DMA
    return pl.pallas_call(
        lambda *refs: pcg_kernel(total_rows, *refs),
        out_shape=jax.ShapeDtypeStruct((1, 512), jnp.float32),
        in_specs=[vm] * 8,
        out_specs=vm,
        scratch_shapes=[
            pltpu.VMEM((1, D), jnp.float32),
            pltpu.VMEM((1, D), jnp.float32),
            pltpu.VMEM((4, 8, 1, D), jnp.float32),
            pltpu.VMEM((4, 16, 1, D), jnp.float32),
            dma((4, 8)),
            dma((4, 8)),
            dma((4, 16)),
            dma((4, 16)),
        ],
        compiler_params=pltpu.CompilerParams(vmem_limit_bytes=32 * 2**20, collective_id=0, has_side_effects=True),
        name="pcg",
    )(blocks, start, *factors, weights, radius)


def row_times(row, matrix, dims):
    return jnp.sum(lax.dot_general(pieces(row), matrix, dims, preferred_element_type=jnp.float32), axis=0, keepdims=True)

def sketch_kernel(
    scale, total_rows, all_features, all_weights, all_labels, all_signs, coarse, fine,
    left, right, residual, blocks,
    send, arrive, narrow, xin, yin, stage, xlast, ylast, mine, pattern, weighted, relay, wide, zbuf, abuf, bbuf, features, weights, labels, signs, ssem, rsem, lsem,
):
    fetches = [
        pltpu.make_async_copy(src, dst, lsem.at[3 + at])
        for at, (src, dst) in enumerate(
            ((all_features, features), (all_weights, weights), (all_labels, labels), (all_signs, signs))
        )
    ]
    for fetch in fetches:
        fetch.start()
    ex = lax.axis_index("ex")
    z = lax.axis_index("feat")
    y, x, c = ex // 8, (ex // 2) % 4, ex % 2

    def to_x(o):
        return ((y * 4 + (x + o) % 4) * 2 + c, z)

    def to_y(o):
        return ((((y + o) % 4) * 4 + x) * 2 + c, z)

    def to_z(o):
        return (ex, (z + o) % 4)

    other = (ex + 1 - 2 * c, z)
    within = ex % 8

    def near(o):
        return (y * 8 + (within + o) % 8, z)

    def far(o):
        to = (y * 4 + z + o) % 16
        return ((to // 4) * 8 + within, to % 4)

    barrier = pltpu.get_barrier_semaphore()
    for o in range(1, 8):
        pl.semaphore_signal(barrier, inc=1, device_id=near(o), device_id_type=MESH)
    for o in range(1, 16):
        pl.semaphore_signal(barrier, inc=1, device_id=far(o), device_id_type=MESH)

    started = []

    def ship(src, dst, device):
        at = len(started)
        copy = pltpu.make_async_remote_copy(
            src_ref=src, dst_ref=dst, send_sem=ssem.at[at], recv_sem=rsem.at[at], device_id=device, device_id_type=MESH
        )
        copy.start()
        started.append(copy)
        return copy

    def spread(buf, me, count, peer):
        return [ship(buf.at[me], buf.at[me], peer(o)) for o in range(1, count)]

    def gathered(copies, buf, count):
        for copy in copies:
            copy.wait_recv()
        totals = [buf[q] for q in range(count)]
        while len(totals) > 1:
            totals = [totals[i] + totals[i + 1] for i in range(0, len(totals), 2)]
        return totals[0]

    for fetch in fetches:
        fetch.wait()
    zbuf[z] = row_times(weights[...], features[...], NT)
    pl.semaphore_wait(barrier, 22)
    margin_copies = spread(zbuf, z, 4, to_z)
    sign_row = signs[...].astype(jnp.bfloat16)

    def patterns(q, carry):
        rows = pl.ds(pl.multiple_of(q * 256, 256), 256)
        fine_rows = fine[rows, :]
        for h in range(16):
            signed_rows = fine_rows * jnp.broadcast_to(sign_row[:, 128 * h : 128 * h + 128], (256, 128))
            pattern[rows, 128 * h : 128 * h + 128] = signed_rows * jnp.broadcast_to(coarse[rows, h : h + 1], (256, 128))
        return carry

    lax.fori_loop(0, 8, patterns, 0)
    margins = gathered(margin_copies, zbuf, 4)
    probability = 1.0 / (1.0 + jnp.exp(-margins))
    root = jnp.sqrt(probability * (1.0 - probability))
    for i in range(16):
        rows = slice(128 * i, 128 * i + 128)
        column = jnp.transpose(jnp.broadcast_to(root[:, rows], (128, 128)))
        for h in range(4):
            cols = slice(128 * h, 128 * h + 128)
            weighted[rows, cols] = (features[rows, cols].astype(jnp.float32) * column).astype(jnp.bfloat16)

    def rows_for(o, part, size):
        return weighted.at[pl.ds(pl.multiple_of(((z + o) % 4) * 512 + part * 256, 256), size), :]

    passing = [ship(rows_for(2, 0, 256), relay.at[0], to_z(1)), ship(rows_for(2, 1, 256), relay.at[1], to_z(3))]
    redistributed = [ship(rows_for(1, 0, 512), blocks.at[1], to_z(1)), ship(rows_for(3, 0, 512), blocks.at[3], to_z(3))]
    kept = pltpu.make_async_copy(weighted.at[pl.ds(pl.multiple_of(z * 512, 512), 512), :], blocks.at[0], lsem.at[2])
    kept.start()

    def mixed(half, o):
        parts = []
        for block, cols in (((x + o) % 4, slice(0, 256)), ((y + o) % 4, slice(256, 512))):
            rows = pl.ds(pl.multiple_of(half * 1024 + block * 256, 256), 256)
            parts.append(jnp.dot(pattern[rows, :], weighted[:, cols], preferred_element_type=jnp.float32))
        return parts

    halves = []
    for at, o in enumerate((1, 2, 3, 0)):
        send[at, 0], send[at, 1] = mixed(1 - c, o)
        halves.append(ship(send.at[at], arrive.at[at], other))
    slope = row_times(probability - labels[...].astype(jnp.float32), features[...], NN)
    wide[...] = jnp.zeros((1, D), jnp.float32)
    wide[:, pl.ds(pl.multiple_of(z * 512, 512), 512)] = slope * (1.0 / total_rows) + weights[...] * (REG / D / 32)
    abuf[within] = wide[...]
    near_copies = spread(abuf, within, 8, near)
    first = []
    for at, o in enumerate((1, 2, 3, 0)):
        left_total, right_total = mixed(c, o)
        halves[at].wait_recv()
        left_total = left_total + arrive[at, 0]
        right_total = right_total + arrive[at, 1]
        if o > 0:
            narrow[0, at] = left_total.astype(jnp.bfloat16)
            narrow[1, at] = right_total.astype(jnp.bfloat16)
            first.append(ship(narrow.at[0, at], xin.at[at], to_x(o)))
            first.append(ship(narrow.at[1, at], yin.at[at], to_y(o)))
    for part, o in ((0, 1), (1, 3)):
        passing[part].wait_recv()
        redistributed.append(ship(relay.at[part], blocks.at[2, pl.ds(256 * part, 256)], to_z(o)))
    bbuf[y * 4 + z] = gathered(near_copies, abuf, 8)
    far_copies = spread(bbuf, y * 4 + z, 16, far)
    for copy in first:
        copy.wait_recv()
    for o in range(3):
        left_total = left_total + xin[o].astype(jnp.float32)
        right_total = right_total + yin[o].astype(jnp.float32)
    for q in range(4):
        stage[0, q] = left_total[64 * q : 64 * q + 64, :]
        stage[1, q] = right_total[64 * q : 64 * q + 64, :]
    second = []
    for o in range(1, 4):
        second.append(ship(stage.at[0, (y + o) % 4], ylast.at[o - 1], to_y(o)))
        second.append(ship(stage.at[1, (x + o) % 4], xlast.at[o - 1], to_x(o)))
    for copy in second:
        copy.wait_recv()
    mine[0] = ((stage[0, y] + ylast[0] + ylast[1] + ylast[2]) * scale).astype(jnp.bfloat16)
    mine[1] = ((stage[1, x] + xlast[0] + xlast[1] + xlast[2]) * scale).astype(jnp.bfloat16)

    cols = pl.ds(pl.multiple_of(z * 256, 256), 256)
    big, small = pl.ds(0, 48), pl.ds(48, 16)
    every = pl.ds(0, 4)
    own_left = pltpu.make_async_copy(mine.at[0], left.at[c, x, y, :, cols], lsem.at[0])
    own_right = pltpu.make_async_copy(mine.at[1], right.at[c, y, x, :, cols], lsem.at[1])
    own_left.start()
    own_right.start()

    def pass_on(work):
        copies = []
        for o in range(1, 4):
            for src, dst, peer in work:
                copies.append(ship(src, dst, peer(o)))
        return copies

    def same(ref, peer):
        return (ref, ref, peer)

    copies = pass_on(
        [
            (mine.at[0, big], left.at[c, x, y, big, cols], to_z),
            (mine.at[1, big], right.at[c, y, x, big, cols], to_z),
            (mine.at[0, small], left.at[c, x, y, small, cols], to_y),
            (mine.at[1, small], right.at[c, y, x, small, cols], to_x),
        ]
    )
    own_left.wait()
    own_right.wait()
    for copy in copies:
        copy.wait_recv()
    copies = pass_on(
        [
            same(left.at[c, x, y, big, :], to_y),
            same(right.at[c, y, x, big, :], to_x),
            same(left.at[c, x, every, small, cols], to_x),
            same(right.at[c, y, every, small, cols], to_y),
        ]
    )
    for copy in copies:
        copy.wait_recv()
    across = []

    def cross(ref):
        across.append(ship(ref, ref, other))

    def zcols(o):
        return pl.ds(pl.multiple_of(((z + o) % 4) * 256, 256), 256)

    def x_piece(o, part):
        return left.at[c, (x + o) % 4, pl.ds(2 * part, 2), big, :]

    def y_piece(o, part):
        return right.at[c, (y + o) % 4, pl.ds(2 * part, 2), big, :]

    def z_piece(o, part):
        return (left, right)[part].at[c, every, every, small, zcols(o)]

    streams = ((x_piece, to_x), (y_piece, to_y), (z_piece, to_z))
    up, down, late = [], [], []
    for piece, peer in streams:
        up.append(ship(piece(0, 0), piece(0, 0), peer(1)))
        down.append(ship(piece(0, 1), piece(0, 1), peer(3)))
    for piece, peer in streams:
        late.append((ship(piece(0, 1), piece(0, 1), peer(1)), piece(3, 1)))
        late.append((ship(piece(0, 0), piece(0, 0), peer(3)), piece(1, 0)))
    for piece, peer in streams:
        cross(piece(0, 0))
        cross(piece(0, 1))
    for at, (piece, peer) in enumerate(streams):
        up[at].wait_recv()
        late.append((ship(piece(3, 0), piece(3, 0), peer(1)), piece(2, 0)))
        cross(piece(3, 0))
        down[at].wait_recv()
        late.append((ship(piece(1, 1), piece(1, 1), peer(3)), piece(2, 1)))
        cross(piece(1, 1))
    for copy, ref in late:
        copy.wait_recv()
        cross(ref)
    for copy in across:
        copy.wait_recv()
    residual[...] = -gathered(far_copies, bbuf, 16)
    for copy in redistributed:
        copy.wait_recv()
    kept.wait()
    for copy in started:
        copy.wait_send()


def sketch_rows(scale, total_rows, features, weights, labels, signs, coarse, fine):
    vm = pl.BlockSpec(memory_space=pltpu.VMEM)
    anywhere = pl.BlockSpec(memory_space=pl.ANY)
    f32, bf16 = jnp.float32, jnp.bfloat16
    half = jax.ShapeDtypeStruct((2, 4, 4, 64, D // 2), bf16)
    left, right, residual, blocks = pl.pallas_call(
        lambda *refs: sketch_kernel(scale, total_rows, *refs),
        out_shape=(half, half, jax.ShapeDtypeStruct((1, D), f32), jax.ShapeDtypeStruct((4, 512, 512), bf16)),
        in_specs=[pl.BlockSpec(memory_space=pltpu.HBM)] * 4 + [vm] * 2,
        out_specs=(anywhere, anywhere, vm, anywhere),
        scratch_shapes=[
            pltpu.VMEM((4, 2, 256, 256), f32),
            pltpu.VMEM((4, 2, 256, 256), f32),
            pltpu.VMEM((2, 3, 256, 256), bf16),
            pltpu.VMEM((3, 256, 256), bf16),
            pltpu.VMEM((3, 256, 256), bf16),
            pltpu.VMEM((2, 4, 64, 256), f32),
            pltpu.VMEM((3, 64, 256), f32),
            pltpu.VMEM((3, 64, 256), f32),
            pltpu.VMEM((2, 64, 256), bf16),
            pltpu.VMEM((D, 2048), bf16),
            pltpu.VMEM((2048, 512), bf16),
            pltpu.VMEM((2, 256, 512), bf16),
            pltpu.VMEM((1, D), f32),
            pltpu.VMEM((4, 1, 2048), f32),
            pltpu.VMEM((8, 1, D), f32),
            pltpu.VMEM((16, 1, D), f32),
            pltpu.VMEM((2048, 512), bf16),
            pltpu.VMEM((1, 512), f32),
            pltpu.VMEM((1, 2048), jnp.int32),
            pltpu.VMEM((1, 2048), jnp.int32),
            pltpu.SemaphoreType.DMA((120,)),
            pltpu.SemaphoreType.DMA((120,)),
            pltpu.SemaphoreType.DMA((7,)),
        ],
        compiler_params=pltpu.CompilerParams(vmem_limit_bytes=36 * 2**20, collective_id=1, has_side_effects=True),
        name="sketch",
    )(features, weights, labels, signs, coarse, fine)
    return left.reshape(D, D // 2), right.reshape(D, D // 2), residual, blocks


def parity(common):
    for shift in (8, 4, 2, 1):
        common = common ^ (common >> shift)
    return 1 - 2 * (common & 1)


def local(features, weights, labels, signs, samples, radius):
    row_count, feat_width = features.shape
    ex_count = lax.axis_size("ex")
    ex_index = lax.axis_index("ex")
    total_rows = row_count * ex_count
    sample_count = samples.shape[0]
    low, high = samples & (row_count - 1), samples >> (row_count.bit_length() - 1)
    coarse = parity((low[:, None] >> 7) & lax.iota(jnp.int32, row_count // 128)[None, :])
    coarse = coarse * parity(high & ex_index)[:, None]
    fine = parity((low[:, None] & 127) & lax.iota(jnp.int32, 128)[None, :])
    scale = 1.0 / math.sqrt(total_rows * sample_count)
    left, right, residual, blocks = sketch_rows(
        scale,
        total_rows,
        features,
        weights[None, :],
        labels[None, :],
        signs[None, :],
        coarse.astype(jnp.bfloat16),
        fine.astype(jnp.bfloat16),
    )
    out = pcg(total_rows, blocks, residual, factor(left, right), weights[None, :], radius[None, :])
    return out[0]


def solution(mesh):
    in_specs = (P("ex", "feat"), P("feat"), P("ex"), P("ex"), P(), P())
    return jax.shard_map(local, mesh=mesh, in_specs=in_specs, out_specs=P("feat"), check_vma=False)
```

```python
import math

import jax
import jax.numpy as jnp
from jax import lax
from jax.experimental import pallas as pl
from jax.experimental.pallas import tpu as pltpu
from jax.sharding import PartitionSpec as P

D = 2048
ITERS = 4
REG = 0.02
HI = lax.Precision.HIGHEST
NN = (((1,), (0,)), ((), ()))
NT = (((1,), (1,)), ((), ()))
TN = (((0,), (0,)), ((), ()))
MESH = pl.DeviceIdType.MESH

def split2(value):
    high = value.astype(jnp.bfloat16)
    return high, (value - high.astype(jnp.float32)).astype(jnp.bfloat16)


def dot3(left, right, dims):
    (lc,), (rc,) = dims[0]
    lh, ll = split2(left)
    rh, rl = split2(right)
    left = jnp.concatenate([lh, lh, ll], axis=lc)
    right = jnp.concatenate([rh, rl, rh], axis=rc)
    return lax.dot_general(left, right, dims, preferred_element_type=jnp.float32)


def block_inverse(block):
    lanes = lax.broadcasted_iota(jnp.int32, (1, 128), 1)
    subs = lax.broadcasted_iota(jnp.int32, (8, 128), 0)
    tiles = [block[8 * t : 8 * t + 8, :] for t in range(16)]

    def lane(t, at):
        return jnp.broadcast_to(tiles[t][:, at : at + 1], (8, 128))

    def sub(tile, at):
        return jnp.broadcast_to(tile[at : at + 1, :], (8, 128))

    own = [lane(0, j) for j in range(8)]
    nxt = [lane(1, j) for j in range(8)]
    for g in range(16):
        base = 8 * g
        more, most = g + 1 < 16, g + 2 < 16
        if more:
            own_later = [lane(g + 1, base + 8 + j) for j in range(8)]
        if most:
            nxt_later = [lane(g + 2, base + 8 + j) for j in range(8)]
            second = [lane(g + 2, base + j) for j in range(8)]
        inverses, crosses, rows = [], {}, []
        head = tiles[g]
        nxt_scaled, second_scaled = [], []
        for j in range(8):
            inverse = 1.0 / sub(own[j], j)
            inverses.append(inverse)
            scaled = jnp.where(subs > j, own[j] * inverse, 0.0)
            if more:
                nxt_scaled.append(nxt[j] * inverse)
            if most:
                second_scaled.append(second[j] * inverse)
            for i in range(j + 1, 8):
                cross = sub(own[i], j)
                crosses[j, i] = cross
                own[i] = own[i] - scaled * cross
                if more:
                    nxt[i] = nxt[i] - nxt_scaled[j] * cross
                if most:
                    second[i] = second[i] - second_scaled[j] * cross
            if more:
                for i in range(8):
                    cross = sub(nxt[j], i)
                    own_later[i] = own_later[i] - nxt_scaled[j] * cross
                    if most:
                        nxt_later[i] = nxt_later[i] - second_scaled[j] * cross
            row = head[j : j + 1, :]
            row = jnp.broadcast_to(jnp.where(lanes == base + j, row + row, row), (8, 128))
            rows.append(row)
            head = head - scaled * row
        tiles[g] = head
        for t in range(g + 1, 16):
            if t == g + 1:
                scaled = nxt_scaled
            elif t == g + 2:
                scaled = second_scaled
            else:
                column = [lane(t, base + j) for j in range(8)]
                scaled = []
                for j in range(8):
                    scaled.append(column[j] * inverses[j])
                    for i in range(j + 1, 8):
                        column[i] = column[i] - scaled[j] * crosses[j, i]
            tile = tiles[t]
            for j in range(8):
                tile = tile - scaled[j] * rows[j]
            tiles[t] = tile
        if more:
            own = own_later
        if most:
            nxt = nxt_later
    whole = jnp.concatenate(tiles, axis=0)
    rows = lax.broadcasted_iota(jnp.int32, (128, 128), 0)
    cols = lax.broadcasted_iota(jnp.int32, (128, 128), 1)
    diagonal = jnp.where(rows == cols, whole, 0.0)
    along_rows = jnp.sum(diagonal, axis=0, keepdims=True)
    along_cols = jnp.sum(diagonal, axis=1, keepdims=True)
    lower = jnp.where(cols <= rows, whole, 0.0)
    return lower * (1.0 / along_rows) * (1.0 / jnp.sqrt(along_cols))


def factor_kernel(left, right, up_hi, up_lo, inv_hi, inv_lo, gram, invs, crosses, corner, trio_l, trio_r):
    ridge = REG / D
    halves = (left, right)
    for a in range(4):
        for b in range(a, 4):
            for h in range(2):
                for side in range(h if a == b else 0, 2):
                    part = lax.dot_general(
                        halves[h][:, 256 * a : 256 * a + 256],
                        halves[side][:, 256 * b : 256 * b + 256],
                        TN,
                        preferred_element_type=jnp.float32,
                    )
                    if a == b and h == side:
                        rows = lax.broadcasted_iota(jnp.int32, (256, 256), 0)
                        cols = lax.broadcasted_iota(jnp.int32, (256, 256), 1)
                        part = part + jnp.where(rows == cols, ridge, 0.0)
                    gram[512 * a + 256 * h : 512 * a + 256 * h + 256, 512 * b + 256 * side : 512 * b + 256 * side + 256] = part
                    if a == b and h < side:
                        gram[512 * a + 256 : 512 * a + 512, 512 * a : 512 * a + 256] = jnp.zeros((256, 256), jnp.float32)

    def join(top, bottom, cross):
        middle = dot3(cross, top, TN)
        edge = -dot3(bottom, middle, NN)
        zero = jnp.zeros_like(top)
        return jnp.concatenate([jnp.concatenate([top, zero], axis=1), jnp.concatenate([edge, bottom], axis=1)], axis=0)

    def step(s, carry):
        at = pl.multiple_of(s * 256, 256)
        next_at = pl.multiple_of(at + 128, 128)
        rows = pl.ds(at, 256)
        first = s // 2
        upper, lower = pl.ds(at, 128), pl.ds(next_at, 128)
        corner[0] = gram[upper, upper]

        def one(h, carry):
            corner[2 + h] = block_inverse(corner[h])

            if h == 0:
                cross = dot3(corner[2], gram[upper, lower], NN)
                corner[4] = cross
                corner[1] = gram[lower, lower] - dot3(cross, cross, TN)

            return carry

        one(0, 0)
        one(1, 0)
        inverse = join(corner[2], corner[3], corner[4])
        invs[s] = inverse
        ih, il = split2(inverse)
        ileft = jnp.concatenate([ih, ih, il], axis=1)
        half = pl.ds(pl.multiple_of((s % 2) * 256, 256), 256)
        for c in range(4):

            @pl.when(c >= (s + 1) // 2)
            def _():
                cs = slice(512 * c, 512 * c + 512)
                gh, gl = split2(gram[rows, cs])
                panel = lax.dot_general(ileft, jnp.concatenate([gh, gl, gh], axis=0), NN, preferred_element_type=jnp.float32)
                cols = lax.broadcasted_iota(jnp.int32, (256, 512), 1) + 512 * c
                panel = jnp.where(cols >= at + 256, panel, 0.0)
                ph, plo = split2(panel)
                trio_r[0:256, cs] = ph
                trio_r[256:512, cs] = plo
                trio_r[512:768, cs] = ph
                trio_l[0:256, cs] = ph
                trio_l[256:512, cs] = ph
                trio_l[512:768, cs] = plo

                @pl.when(c == first)
                def _():
                    crosses[first] = panel[:, 256:]

                @pl.when(c > first)
                def _():
                    block = first * (7 - first) // 2 + c - first - 1
                    up_hi[block, half, :] = ph
                    up_lo[block, half, :] = plo

        def across(a, carry):
            ra = pl.ds(pl.multiple_of(a * 512, 512), 512)

            def along(b, carry):
                cs = pl.ds(pl.multiple_of(b * 512, 512), 512)
                gram[ra, cs] = gram[ra, cs] - lax.dot_general(trio_l[:, ra], trio_r[:, cs], TN, preferred_element_type=jnp.float32)
                return carry

            return lax.fori_loop(a, 4, along, carry)

        lax.fori_loop((s + 1) // 2, 4, across, 0)
        return carry

    lax.fori_loop(0, 8, step, 0)

    def chunk(a, carry):
        hi, lo = split2(join(invs[2 * a], invs[2 * a + 1], crosses[a]))
        inv_hi[a] = hi
        inv_lo[a] = lo
        return carry

    lax.fori_loop(0, 4, chunk, 0)


def factor(left, right):
    vm = pl.BlockSpec(memory_space=pltpu.VMEM)
    ups = jax.ShapeDtypeStruct((6, 512, 512), jnp.bfloat16)
    inverses = jax.ShapeDtypeStruct((4, 512, 512), jnp.bfloat16)
    return pl.pallas_call(
        factor_kernel,
        out_shape=(ups, ups, inverses, inverses),
        in_specs=[vm, vm],
        out_specs=(vm, vm, vm, vm),
        scratch_shapes=[
            pltpu.VMEM((D, D), jnp.float32),
            pltpu.VMEM((8, 256, 256), jnp.float32),
            pltpu.VMEM((4, 256, 256), jnp.float32),
            pltpu.VMEM((5, 128, 128), jnp.float32),
            pltpu.VMEM((768, D), jnp.bfloat16),
            pltpu.VMEM((768, D), jnp.bfloat16),
        ],
        compiler_params=pltpu.CompilerParams(vmem_limit_bytes=30 * 2**20),
        cost_estimate=pl.CostEstimate(flops=60 * 10**9, bytes_accessed=18 * 2**20, transcendentals=0),
        name="factor",
    )(left, right)


def pieces(row):
    first = row.astype(jnp.bfloat16).astype(jnp.float32)
    rest = row - first
    second = rest.astype(jnp.bfloat16).astype(jnp.float32)
    third = rest - second
    which = lax.broadcasted_iota(jnp.int32, (16, row.shape[1]), 0)
    stacked = jnp.where(which == 0, first, jnp.where(which == 1, second, jnp.where(which == 2, third, 0.0)))
    return stacked.astype(jnp.bfloat16)


def pair(row):
    first = row.astype(jnp.bfloat16).astype(jnp.float32)
    which = lax.broadcasted_iota(jnp.int32, (16, row.shape[1]), 0)
    return jnp.where(which == 0, first, jnp.where(which == 1, row - first, 0.0)).astype(jnp.bfloat16)


def place(a, b):
    return a * (7 - a) // 2 + b - a - 1


def pcg_kernel(total_rows, blocks, start, up_hi, up_lo, inv_hi, inv_lo, weights, radius, out, full, wide, abuf, bbuf, a_s, a_r, b_s, b_r):
    ex = lax.axis_index("ex")
    feat = lax.axis_index("feat")
    plane, within = ex // 8, ex % 8
    ridge = REG / D

    def columns(o):
        return pl.ds(pl.multiple_of(((feat + 4 - o) % 4) * 512, 512), 512)

    def near(o):
        return (plane * 8 + (within + o) % 8, feat)

    def far(o):
        other = (plane * 4 + feat + o) % 16
        return ((other // 4) * 8 + within, other % 4)

    barrier = pltpu.get_barrier_semaphore()
    for o in range(1, 8):
        pl.semaphore_signal(barrier, inc=1, device_id=near(o), device_id_type=MESH)
    for o in range(1, 16):
        pl.semaphore_signal(barrier, inc=1, device_id=far(o), device_id_type=MESH)

    def exchange(value, buf, turn, me, count, peer, send, recv):
        buf[turn, me] = value
        copies = [
            pltpu.make_async_remote_copy(
                src_ref=buf.at[turn, me],
                dst_ref=buf.at[turn, me],
                send_sem=send.at[turn, o],
                recv_sem=recv.at[turn, o],
                device_id=peer(o),
                device_id_type=MESH,
            )
            for o in range(1, count)
        ]
        for copy in copies:
            copy.start()
        for copy in copies:
            copy.wait()
        totals = [buf[turn, q] for q in range(count)]
        while len(totals) > 1:
            totals = [totals[i] + totals[i + 1] for i in range(0, len(totals), 2)]
        return totals[0]

    def everywhere(part, turn):
        return exchange(exchange(part, abuf, turn, within, 8, near, a_s, a_r), bbuf, turn, plane * 4 + feat, 16, far, b_s, b_r)

    def product(stacked, high, low, dims):
        total = lax.dot_general(stacked, high, dims, preferred_element_type=jnp.float32)
        total = total + lax.dot_general(stacked, low, dims, preferred_element_type=jnp.float32)
        return jnp.sum(total, axis=0, keepdims=True)

    def solve(row):
        rest = [row[:, 512 * a : 512 * a + 512] for a in range(4)]
        for a in range(4):
            rest[a] = product(pair(rest[a]), inv_hi[a], inv_lo[a], NT)
            stacked = pair(rest[a])
            for b in range(a + 1, 4):
                at = place(a, b)
                rest[b] = rest[b] - product(stacked, up_hi[at], up_lo[at], NN)
        for a in range(3, -1, -1):
            rest[a] = product(pair(rest[a]), inv_hi[a], inv_lo[a], NN)
            stacked = pair(rest[a])
            for b in range(a):
                at = place(b, a)
                rest[b] = rest[b] - product(stacked, up_hi[at], up_lo[at], NT)
        return jnp.concatenate(rest, axis=1)

    def dot(left, right):
        return jnp.sum(left * right, axis=1, keepdims=True)

    residual = start[...]

    def step(number, carry):
        answer, residual, direction, inner = carry
        solved = solve(residual)
        inner_now = dot(residual, solved)
        direction = solved + jnp.where(number == 0, 0.0, inner_now / inner) * direction
        full[...] = direction
        row_sums = jnp.zeros((16, 512), jnp.float32)
        for o in range(4):
            row_sums = row_sums + lax.dot_general(pieces(full[:, columns(o)]), blocks[o], NT, preferred_element_type=jnp.float32)
        stacked = pieces(jnp.sum(row_sums, axis=0, keepdims=True))
        for o in range(4):
            part = lax.dot_general(stacked, blocks[o], NN, preferred_element_type=jnp.float32)
            wide[:, columns(o)] = jnp.sum(part, axis=0, keepdims=True)

        @pl.when(number == 0)
        def _():
            pl.semaphore_wait(barrier, 22)

        curved = everywhere(wide[...], number) * (1.0 / total_rows) + ridge * direction
        step_size = inner_now / dot(direction, curved)
        return answer + step_size * direction, residual - step_size * curved, direction, inner_now

    zero = jnp.zeros((1, D), jnp.float32)
    answer = lax.fori_loop(0, ITERS, step, (zero, residual, zero, jnp.ones((1, 1), jnp.float32)))[0]
    scale = jnp.minimum(1.0, radius[...] * math.sqrt(D) / jnp.sqrt(dot(answer, answer) + 1e-06))
    full[...] = answer
    out[...] = weights[...] + scale * full[:, columns(0)]


def pcg(total_rows, blocks, start, factors, weights, radius):
    vm = pl.BlockSpec(memory_space=pltpu.VMEM)
    dma = pltpu.SemaphoreType.DMA
    return pl.pallas_call(
        lambda *refs: pcg_kernel(total_rows, *refs),
        out_shape=jax.ShapeDtypeStruct((1, 512), jnp.float32),
        in_specs=[vm] * 8,
        out_specs=vm,
        scratch_shapes=[
            pltpu.VMEM((1, D), jnp.float32),
            pltpu.VMEM((1, D), jnp.float32),
            pltpu.VMEM((4, 8, 1, D), jnp.float32),
            pltpu.VMEM((4, 16, 1, D), jnp.float32),
            dma((4, 8)),
            dma((4, 8)),
            dma((4, 16)),
            dma((4, 16)),
        ],
        compiler_params=pltpu.CompilerParams(vmem_limit_bytes=32 * 2**20, collective_id=0, has_side_effects=True),
        name="pcg",
    )(blocks, start, *factors, weights, radius)


def row_times(row, matrix, dims):
    return jnp.sum(lax.dot_general(pieces(row), matrix, dims, preferred_element_type=jnp.float32), axis=0, keepdims=True)

def sketch_kernel(
    scale, total_rows, features, weights, labels, signs, coarse, fine,
    left, right, residual, blocks,
    send, arrive, parcel, xin, yin, stage, xlast, ylast, mine, pattern, weighted, relay, wide, zbuf, abuf, bbuf, ssem, rsem, lsem,
):
    ex = lax.axis_index("ex")
    z = lax.axis_index("feat")
    y, x, c = ex // 8, (ex // 2) % 4, ex % 2

    def to_x(o):
        return ((y * 4 + (x + o) % 4) * 2 + c, z)

    def to_y(o):
        return ((((y + o) % 4) * 4 + x) * 2 + c, z)

    def to_z(o):
        return (ex, (z + o) % 4)

    other = (ex + 1 - 2 * c, z)
    within = ex % 8

    def near(o):
        return (y * 8 + (within + o) % 8, z)

    def far(o):
        to = (y * 4 + z + o) % 16
        return ((to // 4) * 8 + within, to % 4)

    barrier = pltpu.get_barrier_semaphore()
    for o in range(1, 8):
        pl.semaphore_signal(barrier, inc=1, device_id=near(o), device_id_type=MESH)
    for o in range(1, 16):
        pl.semaphore_signal(barrier, inc=1, device_id=far(o), device_id_type=MESH)

    started = []

    def ship(src, dst, device):
        at = len(started)
        copy = pltpu.make_async_remote_copy(
            src_ref=src, dst_ref=dst, send_sem=ssem.at[at], recv_sem=rsem.at[at], device_id=device, device_id_type=MESH
        )
        copy.start()
        started.append(copy)
        return copy

    def spread(buf, me, count, peer):
        return [ship(buf.at[me], buf.at[me], peer(o)) for o in range(1, count)]

    def gathered(copies, buf, count):
        for copy in copies:
            copy.wait_recv()
        totals = [buf[q] for q in range(count)]
        while len(totals) > 1:
            totals = [totals[i] + totals[i + 1] for i in range(0, len(totals), 2)]
        return totals[0]

    zbuf[z] = row_times(weights[...], features[...], NT)
    pl.semaphore_wait(barrier, 22)
    margin_copies = spread(zbuf, z, 4, to_z)
    sign_row = signs[...].astype(jnp.bfloat16)

    def patterns(q, carry):
        rows = pl.ds(pl.multiple_of(q * 256, 256), 256)
        fine_rows = fine[rows, :]
        for h in range(16):
            signed_rows = fine_rows * jnp.broadcast_to(sign_row[:, 128 * h : 128 * h + 128], (256, 128))
            pattern[rows, 128 * h : 128 * h + 128] = signed_rows * jnp.broadcast_to(coarse[rows, h : h + 1], (256, 128))
        return carry

    lax.fori_loop(0, 8, patterns, 0)
    margins = gathered(margin_copies, zbuf, 4)
    probability = 1.0 / (1.0 + jnp.exp(-margins))
    root = jnp.sqrt(probability * (1.0 - probability))
    for i in range(16):
        rows = slice(128 * i, 128 * i + 128)
        column = jnp.transpose(jnp.broadcast_to(root[:, rows], (128, 128)))
        for h in range(4):
            cols = slice(128 * h, 128 * h + 128)
            weighted[rows, cols] = (features[rows, cols].astype(jnp.float32) * column).astype(jnp.bfloat16)

    def rows_for(o, part, size):
        return weighted.at[pl.ds(pl.multiple_of(((z + o) % 4) * 512 + part * 256, 256), size), :]

    passing = [ship(rows_for(2, 0, 256), relay.at[0], to_z(1)), ship(rows_for(2, 1, 256), relay.at[1], to_z(3))]
    redistributed = [ship(rows_for(1, 0, 512), blocks.at[1], to_z(1)), ship(rows_for(3, 0, 512), blocks.at[3], to_z(3))]
    kept = pltpu.make_async_copy(weighted.at[pl.ds(pl.multiple_of(z * 512, 512), 512), :], blocks.at[0], lsem.at[2])
    kept.start()

    def mixed(half, o):
        parts = []
        for block, cols in (((x + o) % 4, slice(0, 256)), ((y + o) % 4, slice(256, 512))):
            rows = pl.ds(pl.multiple_of(half * 1024 + block * 256, 256), 256)
            parts.append(jnp.dot(pattern[rows, :], weighted[:, cols], preferred_element_type=jnp.float32))
        return parts

    halves = []
    for at, o in enumerate((1, 2, 3, 0)):
        send[at, 0], send[at, 1] = mixed(1 - c, o)
        halves.append(ship(send.at[at], arrive.at[at], other))
    slope = row_times(probability - labels[...].astype(jnp.float32), features[...], NN)
    wide[...] = jnp.zeros((1, D), jnp.float32)
    wide[:, pl.ds(pl.multiple_of(z * 512, 512), 512)] = slope * (1.0 / total_rows) + weights[...] * (REG / D / 32)
    abuf[within] = wide[...]
    near_copies = spread(abuf, within, 8, near)
    first = []
    for at, o in enumerate((1, 2, 3, 0)):
        left_total, right_total = mixed(c, o)
        halves[at].wait_recv()
        left_total = left_total + arrive[at, 0]
        right_total = right_total + arrive[at, 1]
        if o > 0:
            parcel[0, at] = left_total
            parcel[1, at] = right_total
            first.append(ship(parcel.at[0, at], xin.at[at], to_x(o)))
            first.append(ship(parcel.at[1, at], yin.at[at], to_y(o)))
    for part, o in ((0, 1), (1, 3)):
        passing[part].wait_recv()
        redistributed.append(ship(relay.at[part], blocks.at[2, pl.ds(256 * part, 256)], to_z(o)))
    bbuf[y * 4 + z] = gathered(near_copies, abuf, 8)
    far_copies = spread(bbuf, y * 4 + z, 16, far)
    for copy in first:
        copy.wait_recv()
    for o in range(3):
        left_total = left_total + xin[o]
        right_total = right_total + yin[o]
    for q in range(4):
        stage[0, q] = left_total[64 * q : 64 * q + 64, :]
        stage[1, q] = right_total[64 * q : 64 * q + 64, :]
    second = []
    for o in range(1, 4):
        second.append(ship(stage.at[0, (y + o) % 4], ylast.at[o - 1], to_y(o)))
        second.append(ship(stage.at[1, (x + o) % 4], xlast.at[o - 1], to_x(o)))
    for copy in second:
        copy.wait_recv()
    mine[0] = ((stage[0, y] + ylast[0] + ylast[1] + ylast[2]) * scale).astype(jnp.bfloat16)
    mine[1] = ((stage[1, x] + xlast[0] + xlast[1] + xlast[2]) * scale).astype(jnp.bfloat16)

    cols = pl.ds(pl.multiple_of(z * 256, 256), 256)
    big, small = pl.ds(0, 48), pl.ds(48, 16)
    every = pl.ds(0, 4)
    own_left = pltpu.make_async_copy(mine.at[0], left.at[c, x, y, :, cols], lsem.at[0])
    own_right = pltpu.make_async_copy(mine.at[1], right.at[c, y, x, :, cols], lsem.at[1])
    own_left.start()
    own_right.start()

    def pass_on(work):
        copies = []
        for o in range(1, 4):
            for src, dst, peer in work:
                copies.append(ship(src, dst, peer(o)))
        return copies

    def same(ref, peer):
        return (ref, ref, peer)

    copies = pass_on(
        [
            (mine.at[0, big], left.at[c, x, y, big, cols], to_z),
            (mine.at[1, big], right.at[c, y, x, big, cols], to_z),
            (mine.at[0, small], left.at[c, x, y, small, cols], to_y),
            (mine.at[1, small], right.at[c, y, x, small, cols], to_x),
        ]
    )
    own_left.wait()
    own_right.wait()
    for copy in copies:
        copy.wait_recv()
    copies = pass_on(
        [
            same(left.at[c, x, y, big, :], to_y),
            same(right.at[c, y, x, big, :], to_x),
            same(left.at[c, x, every, small, cols], to_x),
            same(right.at[c, y, every, small, cols], to_y),
        ]
    )
    for copy in copies:
        copy.wait_recv()
    across = []

    def cross(ref):
        across.append(ship(ref, ref, other))

    def zcols(o):
        return pl.ds(pl.multiple_of(((z + o) % 4) * 256, 256), 256)

    def x_piece(o, part):
        return left.at[c, (x + o) % 4, pl.ds(2 * part, 2), big, :]

    def y_piece(o, part):
        return right.at[c, (y + o) % 4, pl.ds(2 * part, 2), big, :]

    def z_piece(o, part):
        return (left, right)[part].at[c, every, every, small, zcols(o)]

    streams = ((x_piece, to_x), (y_piece, to_y), (z_piece, to_z))
    up, down, late = [], [], []
    for piece, peer in streams:
        up.append(ship(piece(0, 0), piece(0, 0), peer(1)))
        down.append(ship(piece(0, 1), piece(0, 1), peer(3)))
    for piece, peer in streams:
        late.append((ship(piece(0, 1), piece(0, 1), peer(1)), piece(3, 1)))
        late.append((ship(piece(0, 0), piece(0, 0), peer(3)), piece(1, 0)))
    for piece, peer in streams:
        cross(piece(0, 0))
        cross(piece(0, 1))
    for at, (piece, peer) in enumerate(streams):
        up[at].wait_recv()
        late.append((ship(piece(3, 0), piece(3, 0), peer(1)), piece(2, 0)))
        cross(piece(3, 0))
        down[at].wait_recv()
        late.append((ship(piece(1, 1), piece(1, 1), peer(3)), piece(2, 1)))
        cross(piece(1, 1))
    for copy, ref in late:
        copy.wait_recv()
        cross(ref)
    for copy in across:
        copy.wait_recv()
    residual[...] = -gathered(far_copies, bbuf, 16)
    for copy in redistributed:
        copy.wait_recv()
    kept.wait()
    for copy in started:
        copy.wait_send()


def sketch_rows(scale, total_rows, features, weights, labels, signs, coarse, fine):
    vm = pl.BlockSpec(memory_space=pltpu.VMEM)
    anywhere = pl.BlockSpec(memory_space=pl.ANY)
    f32, bf16 = jnp.float32, jnp.bfloat16
    half = jax.ShapeDtypeStruct((2, 4, 4, 64, D // 2), bf16)
    left, right, residual, blocks = pl.pallas_call(
        lambda *refs: sketch_kernel(scale, total_rows, *refs),
        out_shape=(half, half, jax.ShapeDtypeStruct((1, D), f32), jax.ShapeDtypeStruct((4, 512, 512), bf16)),
        in_specs=[vm] * 6,
        out_specs=(anywhere, anywhere, vm, anywhere),
        scratch_shapes=[
            pltpu.VMEM((4, 2, 256, 256), f32),
            pltpu.VMEM((4, 2, 256, 256), f32),
            pltpu.VMEM((2, 3, 256, 256), f32),
            pltpu.VMEM((3, 256, 256), f32),
            pltpu.VMEM((3, 256, 256), f32),
            pltpu.VMEM((2, 4, 64, 256), f32),
            pltpu.VMEM((3, 64, 256), f32),
            pltpu.VMEM((3, 64, 256), f32),
            pltpu.VMEM((2, 64, 256), bf16),
            pltpu.VMEM((D, 2048), bf16),
            pltpu.VMEM((2048, 512), bf16),
            pltpu.VMEM((2, 256, 512), bf16),
            pltpu.VMEM((1, D), f32),
            pltpu.VMEM((4, 1, 2048), f32),
            pltpu.VMEM((8, 1, D), f32),
            pltpu.VMEM((16, 1, D), f32),
            pltpu.SemaphoreType.DMA((120,)),
            pltpu.SemaphoreType.DMA((120,)),
            pltpu.SemaphoreType.DMA((3,)),
        ],
        compiler_params=pltpu.CompilerParams(vmem_limit_bytes=36 * 2**20, collective_id=1, has_side_effects=True),
        name="sketch",
    )(features, weights, labels, signs, coarse, fine)
    return left.reshape(D, D // 2), right.reshape(D, D // 2), residual, blocks


def parity(common):
    for shift in (8, 4, 2, 1):
        common = common ^ (common >> shift)
    return 1 - 2 * (common & 1)


def local(features, weights, labels, signs, samples, radius):
    row_count, feat_width = features.shape
    ex_count = lax.axis_size("ex")
    ex_index = lax.axis_index("ex")
    total_rows = row_count * ex_count
    sample_count = samples.shape[0]
    low, high = samples % row_count, samples // row_count
    coarse = parity((low[:, None] // 128) & lax.iota(jnp.int32, row_count // 128)[None, :])
    coarse = coarse * parity(high & ex_index)[:, None]
    fine = parity((low[:, None] % 128) & lax.iota(jnp.int32, 128)[None, :])
    scale = 1.0 / math.sqrt(total_rows * sample_count)
    left, right, residual, blocks = sketch_rows(
        scale,
        total_rows,
        features,
        weights[None, :],
        labels[None, :],
        signs[None, :],
        coarse.astype(jnp.bfloat16),
        fine.astype(jnp.bfloat16),
    )
    out = pcg(total_rows, blocks, residual, factor(left, right), weights[None, :], radius[None, :])
    return out[0]


def solution(mesh):
    in_specs = (P("ex", "feat"), P("feat"), P("ex"), P("ex"), P(), P())
    return jax.shard_map(local, mesh=mesh, in_specs=in_specs, out_specs=P("feat"), check_vma=False)
```

```python
import math

import jax
import jax.numpy as jnp
from jax import lax
from jax.experimental import pallas as pl
from jax.experimental.pallas import tpu as pltpu
from jax.sharding import PartitionSpec as P

D = 2048
ITERS = 4
REG = 0.02
HI = lax.Precision.HIGHEST
NN = (((1,), (0,)), ((), ()))
NT = (((1,), (1,)), ((), ()))
TN = (((0,), (0,)), ((), ()))
MESH = pl.DeviceIdType.MESH

def split2(value):
    high = value.astype(jnp.bfloat16)
    return high, (value - high.astype(jnp.float32)).astype(jnp.bfloat16)


def dot3(left, right, dims):
    (lc,), (rc,) = dims[0]
    lh, ll = split2(left)
    rh, rl = split2(right)
    left = jnp.concatenate([lh, lh, ll], axis=lc)
    right = jnp.concatenate([rh, rl, rh], axis=rc)
    return lax.dot_general(left, right, dims, preferred_element_type=jnp.float32)


def block_inverse(block):
    lanes = lax.broadcasted_iota(jnp.int32, (1, 128), 1)
    subs = lax.broadcasted_iota(jnp.int32, (8, 128), 0)
    tiles = [block[8 * t : 8 * t + 8, :] for t in range(16)]

    def lane(t, at):
        return jnp.broadcast_to(tiles[t][:, at : at + 1], (8, 128))

    def sub(tile, at):
        return jnp.broadcast_to(tile[at : at + 1, :], (8, 128))

    own = [lane(0, j) for j in range(8)]
    nxt = [lane(1, j) for j in range(8)]
    for g in range(16):
        base = 8 * g
        more, most = g + 1 < 16, g + 2 < 16
        if more:
            own_later = [lane(g + 1, base + 8 + j) for j in range(8)]
        if most:
            nxt_later = [lane(g + 2, base + 8 + j) for j in range(8)]
            second = [lane(g + 2, base + j) for j in range(8)]
        inverses, crosses, rows = [], {}, []
        head = tiles[g]
        nxt_scaled, second_scaled = [], []
        for j in range(8):
            inverse = 1.0 / sub(own[j], j)
            inverses.append(inverse)
            scaled = jnp.where(subs > j, own[j] * inverse, 0.0)
            if more:
                nxt_scaled.append(nxt[j] * inverse)
            if most:
                second_scaled.append(second[j] * inverse)
            for i in range(j + 1, 8):
                cross = sub(own[i], j)
                crosses[j, i] = cross
                own[i] = own[i] - scaled * cross
                if more:
                    nxt[i] = nxt[i] - nxt_scaled[j] * cross
                if most:
                    second[i] = second[i] - second_scaled[j] * cross
            if more:
                for i in range(8):
                    cross = sub(nxt[j], i)
                    own_later[i] = own_later[i] - nxt_scaled[j] * cross
                    if most:
                        nxt_later[i] = nxt_later[i] - second_scaled[j] * cross
            row = head[j : j + 1, :]
            row = jnp.broadcast_to(jnp.where(lanes == base + j, row + row, row), (8, 128))
            rows.append(row)
            head = head - scaled * row
        tiles[g] = head
        for t in range(g + 1, 16):
            if t == g + 1:
                scaled = nxt_scaled
            elif t == g + 2:
                scaled = second_scaled
            else:
                column = [lane(t, base + j) for j in range(8)]
                scaled = []
                for j in range(8):
                    scaled.append(column[j] * inverses[j])
                    for i in range(j + 1, 8):
                        column[i] = column[i] - scaled[j] * crosses[j, i]
            tile = tiles[t]
            for j in range(8):
                tile = tile - scaled[j] * rows[j]
            tiles[t] = tile
        if more:
            own = own_later
        if most:
            nxt = nxt_later
    whole = jnp.concatenate(tiles, axis=0)
    rows = lax.broadcasted_iota(jnp.int32, (128, 128), 0)
    cols = lax.broadcasted_iota(jnp.int32, (128, 128), 1)
    diagonal = jnp.where(rows == cols, whole, 0.0)
    along_rows = jnp.sum(diagonal, axis=0, keepdims=True)
    along_cols = jnp.sum(diagonal, axis=1, keepdims=True)
    lower = jnp.where(cols <= rows, whole, 0.0)
    return lower * (1.0 / along_rows) * (1.0 / jnp.sqrt(along_cols))


def factor_kernel(left, right, up_hi, up_lo, inv_hi, inv_lo, gram, invs, crosses, corner, trio_l, trio_r):
    ridge = REG / D
    halves = (left, right)
    for a in range(4):
        for b in range(a, 4):
            for h in range(2):
                for side in range(h if a == b else 0, 2):
                    part = lax.dot_general(
                        halves[h][:, 256 * a : 256 * a + 256],
                        halves[side][:, 256 * b : 256 * b + 256],
                        TN,
                        preferred_element_type=jnp.float32,
                    )
                    if a == b and h == side:
                        rows = lax.broadcasted_iota(jnp.int32, (256, 256), 0)
                        cols = lax.broadcasted_iota(jnp.int32, (256, 256), 1)
                        part = part + jnp.where(rows == cols, ridge, 0.0)
                    gram[512 * a + 256 * h : 512 * a + 256 * h + 256, 512 * b + 256 * side : 512 * b + 256 * side + 256] = part
                    if a == b and h < side:
                        gram[512 * a + 256 : 512 * a + 512, 512 * a : 512 * a + 256] = jnp.zeros((256, 256), jnp.float32)

    def join(top, bottom, cross):
        middle = dot3(cross, top, TN)
        edge = -dot3(bottom, middle, NN)
        zero = jnp.zeros_like(top)
        return jnp.concatenate([jnp.concatenate([top, zero], axis=1), jnp.concatenate([edge, bottom], axis=1)], axis=0)

    def step(s, carry):
        at = pl.multiple_of(s * 256, 256)
        next_at = pl.multiple_of(at + 128, 128)
        rows = pl.ds(at, 256)
        first = s // 2
        upper, lower = pl.ds(at, 128), pl.ds(next_at, 128)
        corner[0] = gram[upper, upper]

        def one(h, carry):
            corner[2 + h] = block_inverse(corner[h])

            if h == 0:
                cross = dot3(corner[2], gram[upper, lower], NN)
                corner[4] = cross
                corner[1] = gram[lower, lower] - dot3(cross, cross, TN)

            return carry

        one(0, 0)
        one(1, 0)
        inverse = join(corner[2], corner[3], corner[4])
        invs[s] = inverse
        ih, il = split2(inverse)
        ileft = jnp.concatenate([ih, ih, il], axis=1)
        half = pl.ds(pl.multiple_of((s % 2) * 256, 256), 256)
        for c in range(4):

            @pl.when(c >= (s + 1) // 2)
            def _():
                cs = slice(512 * c, 512 * c + 512)
                gh, gl = split2(gram[rows, cs])
                panel = lax.dot_general(ileft, jnp.concatenate([gh, gl, gh], axis=0), NN, preferred_element_type=jnp.float32)
                cols = lax.broadcasted_iota(jnp.int32, (256, 512), 1) + 512 * c
                panel = jnp.where(cols >= at + 256, panel, 0.0)
                ph, plo = split2(panel)
                trio_r[0:256, cs] = ph
                trio_r[256:512, cs] = plo
                trio_r[512:768, cs] = ph
                trio_l[0:256, cs] = ph
                trio_l[256:512, cs] = ph
                trio_l[512:768, cs] = plo

                @pl.when(c == first)
                def _():
                    crosses[first] = panel[:, 256:]

                @pl.when(c > first)
                def _():
                    block = first * (7 - first) // 2 + c - first - 1
                    up_hi[block, half, :] = ph
                    up_lo[block, half, :] = plo

        for a in range(4):

            @pl.when(a >= (s + 1) // 2)
            def _():
                ra = slice(512 * a, 512 * a + 512)
                for b in range(a, 4):
                    cs = slice(512 * b, 512 * b + 512)
                    gram[ra, cs] = gram[ra, cs] - lax.dot_general(trio_l[:, ra], trio_r[:, cs], TN, preferred_element_type=jnp.float32)

        return carry

    lax.fori_loop(0, 8, step, 0)

    def chunk(a, carry):
        hi, lo = split2(join(invs[2 * a], invs[2 * a + 1], crosses[a]))
        inv_hi[a] = hi
        inv_lo[a] = lo
        return carry

    lax.fori_loop(0, 4, chunk, 0)


def factor(left, right):
    vm = pl.BlockSpec(memory_space=pltpu.VMEM)
    ups = jax.ShapeDtypeStruct((6, 512, 512), jnp.bfloat16)
    inverses = jax.ShapeDtypeStruct((4, 512, 512), jnp.bfloat16)
    return pl.pallas_call(
        factor_kernel,
        out_shape=(ups, ups, inverses, inverses),
        in_specs=[vm, vm],
        out_specs=(vm, vm, vm, vm),
        scratch_shapes=[
            pltpu.VMEM((D, D), jnp.float32),
            pltpu.VMEM((8, 256, 256), jnp.float32),
            pltpu.VMEM((4, 256, 256), jnp.float32),
            pltpu.VMEM((5, 128, 128), jnp.float32),
            pltpu.VMEM((768, D), jnp.bfloat16),
            pltpu.VMEM((768, D), jnp.bfloat16),
        ],
        compiler_params=pltpu.CompilerParams(vmem_limit_bytes=30 * 2**20),
        cost_estimate=pl.CostEstimate(flops=60 * 10**9, bytes_accessed=18 * 2**20, transcendentals=0),
        name="factor",
    )(left, right)


def pieces(row):
    first = row.astype(jnp.bfloat16).astype(jnp.float32)
    rest = row - first
    second = rest.astype(jnp.bfloat16).astype(jnp.float32)
    third = rest - second
    which = lax.broadcasted_iota(jnp.int32, (16, row.shape[1]), 0)
    stacked = jnp.where(which == 0, first, jnp.where(which == 1, second, jnp.where(which == 2, third, 0.0)))
    return stacked.astype(jnp.bfloat16)


def pair(row):
    first = row.astype(jnp.bfloat16).astype(jnp.float32)
    which = lax.broadcasted_iota(jnp.int32, (16, row.shape[1]), 0)
    return jnp.where(which == 0, first, jnp.where(which == 1, row - first, 0.0)).astype(jnp.bfloat16)


def place(a, b):
    return a * (7 - a) // 2 + b - a - 1


def pcg_kernel(total_rows, blocks, start, up_hi, up_lo, inv_hi, inv_lo, weights, radius, out, full, wide, abuf, bbuf, a_s, a_r, b_s, b_r):
    ex = lax.axis_index("ex")
    feat = lax.axis_index("feat")
    plane, within = ex // 8, ex % 8
    ridge = REG / D

    def columns(o):
        return pl.ds(pl.multiple_of(((feat + 4 - o) % 4) * 512, 512), 512)

    def near(o):
        return (plane * 8 + (within + o) % 8, feat)

    def far(o):
        other = (plane * 4 + feat + o) % 16
        return ((other // 4) * 8 + within, other % 4)

    barrier = pltpu.get_barrier_semaphore()
    for o in range(1, 8):
        pl.semaphore_signal(barrier, inc=1, device_id=near(o), device_id_type=MESH)
    for o in range(1, 16):
        pl.semaphore_signal(barrier, inc=1, device_id=far(o), device_id_type=MESH)

    def exchange(value, buf, turn, me, count, peer, send, recv):
        buf[turn, me] = value
        copies = [
            pltpu.make_async_remote_copy(
                src_ref=buf.at[turn, me],
                dst_ref=buf.at[turn, me],
                send_sem=send.at[turn, o],
                recv_sem=recv.at[turn, o],
                device_id=peer(o),
                device_id_type=MESH,
            )
            for o in range(1, count)
        ]
        for copy in copies:
            copy.start()
        for copy in copies:
            copy.wait()
        totals = [buf[turn, q] for q in range(count)]
        while len(totals) > 1:
            totals = [totals[i] + totals[i + 1] for i in range(0, len(totals), 2)]
        return totals[0]

    def everywhere(part, turn):
        return exchange(exchange(part, abuf, turn, within, 8, near, a_s, a_r), bbuf, turn, plane * 4 + feat, 16, far, b_s, b_r)

    def product(stacked, high, low, dims):
        total = lax.dot_general(stacked, high, dims, preferred_element_type=jnp.float32)
        total = total + lax.dot_general(stacked, low, dims, preferred_element_type=jnp.float32)
        return jnp.sum(total, axis=0, keepdims=True)

    def solve(row):
        rest = [row[:, 512 * a : 512 * a + 512] for a in range(4)]
        for a in range(4):
            rest[a] = product(pair(rest[a]), inv_hi[a], inv_lo[a], NT)
            stacked = pair(rest[a])
            for b in range(a + 1, 4):
                at = place(a, b)
                rest[b] = rest[b] - product(stacked, up_hi[at], up_lo[at], NN)
        for a in range(3, -1, -1):
            rest[a] = product(pair(rest[a]), inv_hi[a], inv_lo[a], NN)
            stacked = pair(rest[a])
            for b in range(a):
                at = place(b, a)
                rest[b] = rest[b] - product(stacked, up_hi[at], up_lo[at], NT)
        return jnp.concatenate(rest, axis=1)

    def dot(left, right):
        return jnp.sum(left * right, axis=1, keepdims=True)

    residual = start[...]

    def step(number, carry):
        answer, residual, direction, inner = carry
        solved = solve(residual)
        inner_now = dot(residual, solved)
        direction = solved + jnp.where(number == 0, 0.0, inner_now / inner) * direction
        full[...] = direction
        row_sums = jnp.zeros((16, 512), jnp.float32)
        for o in range(4):
            row_sums = row_sums + lax.dot_general(pieces(full[:, columns(o)]), blocks[o], NT, preferred_element_type=jnp.float32)
        stacked = pieces(jnp.sum(row_sums, axis=0, keepdims=True))
        for o in range(4):
            part = lax.dot_general(stacked, blocks[o], NN, preferred_element_type=jnp.float32)
            wide[:, columns(o)] = jnp.sum(part, axis=0, keepdims=True)

        @pl.when(number == 0)
        def _():
            pl.semaphore_wait(barrier, 22)

        curved = everywhere(wide[...], number) * (1.0 / total_rows) + ridge * direction
        step_size = inner_now / dot(direction, curved)
        return answer + step_size * direction, residual - step_size * curved, direction, inner_now

    zero = jnp.zeros((1, D), jnp.float32)
    answer = lax.fori_loop(0, ITERS, step, (zero, residual, zero, jnp.ones((1, 1), jnp.float32)))[0]
    scale = jnp.minimum(1.0, radius[...] * math.sqrt(D) / jnp.sqrt(dot(answer, answer) + 1e-06))
    full[...] = answer
    out[...] = weights[...] + scale * full[:, columns(0)]


def pcg(total_rows, blocks, start, factors, weights, radius):
    vm = pl.BlockSpec(memory_space=pltpu.VMEM)
    dma = pltpu.SemaphoreType.DMA
    return pl.pallas_call(
        lambda *refs: pcg_kernel(total_rows, *refs),
        out_shape=jax.ShapeDtypeStruct((1, 512), jnp.float32),
        in_specs=[vm] * 8,
        out_specs=vm,
        scratch_shapes=[
            pltpu.VMEM((1, D), jnp.float32),
            pltpu.VMEM((1, D), jnp.float32),
            pltpu.VMEM((4, 8, 1, D), jnp.float32),
            pltpu.VMEM((4, 16, 1, D), jnp.float32),
            dma((4, 8)),
            dma((4, 8)),
            dma((4, 16)),
            dma((4, 16)),
        ],
        compiler_params=pltpu.CompilerParams(vmem_limit_bytes=32 * 2**20, collective_id=0, has_side_effects=True),
        name="pcg",
    )(blocks, start, *factors, weights, radius)


def row_times(row, matrix, dims):
    return jnp.sum(lax.dot_general(pieces(row), matrix, dims, preferred_element_type=jnp.float32), axis=0, keepdims=True)

def sketch_kernel(
    scale, total_rows, features, weights, labels, signs, coarse, fine,
    left, right, residual, blocks,
    send, arrive, parcel, xin, yin, stage, xlast, ylast, mine, pattern, weighted, relay, wide, zbuf, abuf, bbuf, ssem, rsem, lsem,
):
    ex = lax.axis_index("ex")
    z = lax.axis_index("feat")
    y, x, c = ex // 8, (ex // 2) % 4, ex % 2

    def to_x(o):
        return ((y * 4 + (x + o) % 4) * 2 + c, z)

    def to_y(o):
        return ((((y + o) % 4) * 4 + x) * 2 + c, z)

    def to_z(o):
        return (ex, (z + o) % 4)

    other = (ex + 1 - 2 * c, z)
    within = ex % 8

    def near(o):
        return (y * 8 + (within + o) % 8, z)

    def far(o):
        to = (y * 4 + z + o) % 16
        return ((to // 4) * 8 + within, to % 4)

    barrier = pltpu.get_barrier_semaphore()
    for o in range(1, 8):
        pl.semaphore_signal(barrier, inc=1, device_id=near(o), device_id_type=MESH)
    for o in range(1, 16):
        pl.semaphore_signal(barrier, inc=1, device_id=far(o), device_id_type=MESH)

    started = []

    def ship(src, dst, device):
        at = len(started)
        copy = pltpu.make_async_remote_copy(
            src_ref=src, dst_ref=dst, send_sem=ssem.at[at], recv_sem=rsem.at[at], device_id=device, device_id_type=MESH
        )
        copy.start()
        started.append(copy)
        return copy

    def spread(buf, me, count, peer):
        return [ship(buf.at[me], buf.at[me], peer(o)) for o in range(1, count)]

    def gathered(copies, buf, count):
        for copy in copies:
            copy.wait_recv()
        totals = [buf[q] for q in range(count)]
        while len(totals) > 1:
            totals = [totals[i] + totals[i + 1] for i in range(0, len(totals), 2)]
        return totals[0]

    zbuf[z] = row_times(weights[...], features[...], NT)
    pl.semaphore_wait(barrier, 22)
    margin_copies = spread(zbuf, z, 4, to_z)
    sign_row = signs[...].astype(jnp.bfloat16)

    def patterns(q, carry):
        rows = pl.ds(pl.multiple_of(q * 256, 256), 256)
        fine_rows = fine[rows, :]
        for h in range(16):
            signed_rows = fine_rows * jnp.broadcast_to(sign_row[:, 128 * h : 128 * h + 128], (256, 128))
            pattern[rows, 128 * h : 128 * h + 128] = signed_rows * jnp.broadcast_to(coarse[rows, h : h + 1], (256, 128))
        return carry

    lax.fori_loop(0, 8, patterns, 0)
    margins = gathered(margin_copies, zbuf, 4)
    probability = 1.0 / (1.0 + jnp.exp(-margins))
    root = jnp.sqrt(probability * (1.0 - probability))
    for i in range(16):
        rows = slice(128 * i, 128 * i + 128)
        column = jnp.transpose(jnp.broadcast_to(root[:, rows], (128, 128)))
        for h in range(4):
            cols = slice(128 * h, 128 * h + 128)
            weighted[rows, cols] = (features[rows, cols].astype(jnp.float32) * column).astype(jnp.bfloat16)

    def rows_for(o, part, size):
        return weighted.at[pl.ds(pl.multiple_of(((z + o) % 4) * 512 + part * 256, 256), size), :]

    passing = [ship(rows_for(2, 0, 256), relay.at[0], to_z(1)), ship(rows_for(2, 1, 256), relay.at[1], to_z(3))]
    redistributed = [ship(rows_for(1, 0, 512), blocks.at[1], to_z(1)), ship(rows_for(3, 0, 512), blocks.at[3], to_z(3))]
    kept = pltpu.make_async_copy(weighted.at[pl.ds(pl.multiple_of(z * 512, 512), 512), :], blocks.at[0], lsem.at[2])
    kept.start()

    def mixed(half, o):
        parts = []
        for block, cols in (((x + o) % 4, slice(0, 256)), ((y + o) % 4, slice(256, 512))):
            rows = pl.ds(pl.multiple_of(half * 1024 + block * 256, 256), 256)
            parts.append(jnp.dot(pattern[rows, :], weighted[:, cols], preferred_element_type=jnp.float32))
        return parts

    halves = []
    for at, o in enumerate((1, 2, 3, 0)):
        send[at, 0], send[at, 1] = mixed(1 - c, o)
        halves.append(ship(send.at[at], arrive.at[at], other))
    slope = row_times(probability - labels[...].astype(jnp.float32), features[...], NN)
    wide[...] = jnp.zeros((1, D), jnp.float32)
    wide[:, pl.ds(pl.multiple_of(z * 512, 512), 512)] = slope * (1.0 / total_rows) + weights[...] * (REG / D / 32)
    abuf[within] = wide[...]
    near_copies = spread(abuf, within, 8, near)
    first = []
    for at, o in enumerate((1, 2, 3, 0)):
        left_total, right_total = mixed(c, o)
        halves[at].wait_recv()
        left_total = left_total + arrive[at, 0]
        right_total = right_total + arrive[at, 1]
        if o > 0:
            parcel[0, at] = left_total
            parcel[1, at] = right_total
            first.append(ship(parcel.at[0, at], xin.at[at], to_x(o)))
            first.append(ship(parcel.at[1, at], yin.at[at], to_y(o)))
    for part, o in ((0, 1), (1, 3)):
        passing[part].wait_recv()
        redistributed.append(ship(relay.at[part], blocks.at[2, pl.ds(256 * part, 256)], to_z(o)))
    bbuf[y * 4 + z] = gathered(near_copies, abuf, 8)
    far_copies = spread(bbuf, y * 4 + z, 16, far)
    for copy in first:
        copy.wait_recv()
    for o in range(3):
        left_total = left_total + xin[o]
        right_total = right_total + yin[o]
    for q in range(4):
        stage[0, q] = left_total[64 * q : 64 * q + 64, :]
        stage[1, q] = right_total[64 * q : 64 * q + 64, :]
    second = []
    for o in range(1, 4):
        second.append(ship(stage.at[0, (y + o) % 4], ylast.at[o - 1], to_y(o)))
        second.append(ship(stage.at[1, (x + o) % 4], xlast.at[o - 1], to_x(o)))
    for copy in second:
        copy.wait_recv()
    mine[0] = ((stage[0, y] + ylast[0] + ylast[1] + ylast[2]) * scale).astype(jnp.bfloat16)
    mine[1] = ((stage[1, x] + xlast[0] + xlast[1] + xlast[2]) * scale).astype(jnp.bfloat16)

    cols = pl.ds(pl.multiple_of(z * 256, 256), 256)
    big, small = pl.ds(0, 48), pl.ds(48, 16)
    every = pl.ds(0, 4)
    own_left = pltpu.make_async_copy(mine.at[0], left.at[c, x, y, :, cols], lsem.at[0])
    own_right = pltpu.make_async_copy(mine.at[1], right.at[c, y, x, :, cols], lsem.at[1])
    own_left.start()
    own_right.start()

    def pass_on(work):
        copies = []
        for o in range(1, 4):
            for src, dst, peer in work:
                copies.append(ship(src, dst, peer(o)))
        return copies

    def same(ref, peer):
        return (ref, ref, peer)

    copies = pass_on(
        [
            (mine.at[0, big], left.at[c, x, y, big, cols], to_z),
            (mine.at[1, big], right.at[c, y, x, big, cols], to_z),
            (mine.at[0, small], left.at[c, x, y, small, cols], to_y),
            (mine.at[1, small], right.at[c, y, x, small, cols], to_x),
        ]
    )
    own_left.wait()
    own_right.wait()
    for copy in copies:
        copy.wait_recv()
    copies = pass_on(
        [
            same(left.at[c, x, y, big, :], to_y),
            same(right.at[c, y, x, big, :], to_x),
            same(left.at[c, x, every, small, cols], to_x),
            same(right.at[c, y, every, small, cols], to_y),
        ]
    )
    for copy in copies:
        copy.wait_recv()
    across = []

    def cross(ref):
        across.append(ship(ref, ref, other))

    def zcols(o):
        return pl.ds(pl.multiple_of(((z + o) % 4) * 256, 256), 256)

    def x_piece(o, part):
        return left.at[c, (x + o) % 4, pl.ds(2 * part, 2), big, :]

    def y_piece(o, part):
        return right.at[c, (y + o) % 4, pl.ds(2 * part, 2), big, :]

    def z_piece(o, part):
        return (left, right)[part].at[c, every, every, small, zcols(o)]

    streams = ((x_piece, to_x), (y_piece, to_y), (z_piece, to_z))
    up, down, late = [], [], []
    for piece, peer in streams:
        up.append(ship(piece(0, 0), piece(0, 0), peer(1)))
        down.append(ship(piece(0, 1), piece(0, 1), peer(3)))
    for piece, peer in streams:
        late.append((ship(piece(0, 1), piece(0, 1), peer(1)), piece(3, 1)))
        late.append((ship(piece(0, 0), piece(0, 0), peer(3)), piece(1, 0)))
    for piece, peer in streams:
        cross(piece(0, 0))
        cross(piece(0, 1))
    for at, (piece, peer) in enumerate(streams):
        up[at].wait_recv()
        late.append((ship(piece(3, 0), piece(3, 0), peer(1)), piece(2, 0)))
        cross(piece(3, 0))
        down[at].wait_recv()
        late.append((ship(piece(1, 1), piece(1, 1), peer(3)), piece(2, 1)))
        cross(piece(1, 1))
    for copy, ref in late:
        copy.wait_recv()
        cross(ref)
    for copy in across:
        copy.wait_recv()
    residual[...] = -gathered(far_copies, bbuf, 16)
    for copy in redistributed:
        copy.wait_recv()
    kept.wait()
    for copy in started:
        copy.wait_send()


def sketch_rows(scale, total_rows, features, weights, labels, signs, coarse, fine):
    vm = pl.BlockSpec(memory_space=pltpu.VMEM)
    anywhere = pl.BlockSpec(memory_space=pl.ANY)
    f32, bf16 = jnp.float32, jnp.bfloat16
    half = jax.ShapeDtypeStruct((2, 4, 4, 64, D // 2), bf16)
    left, right, residual, blocks = pl.pallas_call(
        lambda *refs: sketch_kernel(scale, total_rows, *refs),
        out_shape=(half, half, jax.ShapeDtypeStruct((1, D), f32), jax.ShapeDtypeStruct((4, 512, 512), bf16)),
        in_specs=[vm] * 6,
        out_specs=(anywhere, anywhere, vm, anywhere),
        scratch_shapes=[
            pltpu.VMEM((4, 2, 256, 256), f32),
            pltpu.VMEM((4, 2, 256, 256), f32),
            pltpu.VMEM((2, 3, 256, 256), f32),
            pltpu.VMEM((3, 256, 256), f32),
            pltpu.VMEM((3, 256, 256), f32),
            pltpu.VMEM((2, 4, 64, 256), f32),
            pltpu.VMEM((3, 64, 256), f32),
            pltpu.VMEM((3, 64, 256), f32),
            pltpu.VMEM((2, 64, 256), bf16),
            pltpu.VMEM((D, 2048), bf16),
            pltpu.VMEM((2048, 512), bf16),
            pltpu.VMEM((2, 256, 512), bf16),
            pltpu.VMEM((1, D), f32),
            pltpu.VMEM((4, 1, 2048), f32),
            pltpu.VMEM((8, 1, D), f32),
            pltpu.VMEM((16, 1, D), f32),
            pltpu.SemaphoreType.DMA((120,)),
            pltpu.SemaphoreType.DMA((120,)),
            pltpu.SemaphoreType.DMA((3,)),
        ],
        compiler_params=pltpu.CompilerParams(vmem_limit_bytes=36 * 2**20, collective_id=1, has_side_effects=True),
        name="sketch",
    )(features, weights, labels, signs, coarse, fine)
    return left.reshape(D, D // 2), right.reshape(D, D // 2), residual, blocks


def parity(common):
    for shift in (8, 4, 2, 1):
        common = common ^ (common >> shift)
    return 1 - 2 * (common & 1)


def local(features, weights, labels, signs, samples, radius):
    row_count, feat_width = features.shape
    ex_count = lax.axis_size("ex")
    ex_index = lax.axis_index("ex")
    total_rows = row_count * ex_count
    sample_count = samples.shape[0]
    low, high = samples % row_count, samples // row_count
    coarse = parity((low[:, None] // 128) & lax.iota(jnp.int32, row_count // 128)[None, :])
    coarse = coarse * parity(high & ex_index)[:, None]
    fine = parity((low[:, None] % 128) & lax.iota(jnp.int32, 128)[None, :])
    scale = 1.0 / math.sqrt(total_rows * sample_count)
    left, right, residual, blocks = sketch_rows(
        scale,
        total_rows,
        features,
        weights[None, :],
        labels[None, :],
        signs[None, :],
        coarse.astype(jnp.bfloat16),
        fine.astype(jnp.bfloat16),
    )
    out = pcg(total_rows, blocks, residual, factor(left, right), weights[None, :], radius[None, :])
    return out[0]


def solution(mesh):
    in_specs = (P("ex", "feat"), P("feat"), P("ex"), P("ex"), P(), P())
    return jax.shard_map(local, mesh=mesh, in_specs=in_specs, out_specs=P("feat"), check_vma=False)
```
